32 devices in a mesh: groups: 2 (over y), rows: 4 (over z), cams: 2 (over x), cols: 2 (over core).
Axes of the slice: x: 2, y: 2, z: 4, core: 2. Of those that a mesh axis runs over, the one named last changes fastest.
Arguments:
- left_feats: bfloat16 [4, 32, 1024, 128], P(('groups', 'cams'), 'rows', 'cols'), parts along dimension 0, may hold values from -6 to 6
- right_feats: bfloat16 [4, 32, 1024, 128], P(('groups', 'cams'), 'rows', 'cols'), parts along dimension 0, may hold values from -6 to 6
- prev_hidden: bfloat16 [4, 32, 1024, 128], P(('groups', 'cams'), 'rows', 'cols'), parts along dimension 0, may hold values from -1 to 1
- warp_list: int32 [4, 32, 8, 4], P(('groups', 'cams'), 'rows', 'cols'), parts along dimension 0, may hold values from -1 to 7, as said below
- enc_weight: bfloat16 [192, 128], replicated, may hold values from -0.4375 to 0.4375
- hgate_w: bfloat16 [5, 256, 256], replicated, may hold values from -0.15625 to 0.15625
- hcand_w: bfloat16 [5, 256, 128], replicated, may hold values from -0.15625 to 0.15625
- vgate_w: bfloat16 [5, 256, 256], replicated, may hold values from -0.15625 to 0.15625
- vcand_w: bfloat16 [5, 256, 128], replicated, may hold values from -0.15625 to 0.15625
Outputs:
- hidden_next: bfloat16 [4, 32, 1024, 128], P(('groups', 'cams'), 'rows', 'cols'), parts along dimension 0
The draws below stay inside these ranges and needn't reach their ends.
There are 2 independent parts, one for each index of `groups`. The reference program is written for one: setup_inputs(seed, part) draws one part's arguments, and reference() takes and returns one part's arrays. A program takes and returns all parts, laid end to end along the dimension named above; an argument that names none is the same for every part. Nothing has to cross between parts.
Inputs may be any that keep to these rules, and one draw needn't show every extreme that they name: Entry 0 of warp_list is the band offset k, entry 1 the source row within a band of 8 rows, entry 2 the source block among the 4 blocks of the same column half, entry 3 the valid flag. Among the 32 blocks of one band and column half of one view, exactly half take offset 0 and a quarter each take -1 and 1, so at most 8 come from one neighbouring band, and the blocks that take one offset name distinct source blocks. The flag is 0 wherever the source band lies outside the image.
All inputs are finite; a program needn't handle non-finite values.
Results may differ from the reference program's by a relative error of at most 0.0062.
Values may be sent and summed in bfloat16 or wider, within the bound.
No kernel may reach another device: no remote copies, remote signals or barrier semaphores. Data moves between devices by JAX's collectives and lax.ppermute only.
A program may use at most 128 MiB of HBM per device.

```python
import jax
import jax.numpy as jnp
from jax import lax

FEAT = 128
HID = 128
DISP = 192
KERN = 5
BLK_COLS = 128
ITERS = 1
ROWS_DEV = 8
COLS_DEV = 512
VIEWS = 2
H = 32
W = 1024
NBC = 4
NBW = 8
NB = 32


def draw_warp_list(key, part):
    band_total = H // ROWS_DEV
    half_bands = NBW // NBC
    unit_total = VIEWS * band_total * half_bands
    half_count = NB // 2
    quarter = NB // 4

    def one_unit(unit_index):
        unit_key = jax.random.fold_in(key, unit_index)
        rank_of = jax.random.permutation(jax.random.fold_in(unit_key, 1), NB)
        stay_perm = jax.random.permutation(jax.random.fold_in(unit_key, 2), NB)
        lower_perm = jax.random.permutation(jax.random.fold_in(unit_key, 3), NB)
        upper_perm = jax.random.permutation(jax.random.fold_in(unit_key, 4), NB)
        offset = jnp.where(rank_of < half_count, 0, jnp.where(rank_of < half_count + quarter, -1, 1))
        from_stay = jnp.take(stay_perm, jnp.clip(rank_of, 0, NB - 1))
        from_lower = jnp.take(lower_perm, jnp.clip(rank_of - half_count, 0, NB - 1))
        from_upper = jnp.take(upper_perm, jnp.clip(rank_of - half_count - quarter, 0, NB - 1))
        source = jnp.where(rank_of < half_count, from_stay, jnp.where(rank_of < half_count + quarter, from_lower, from_upper))
        band_index = unit_index // half_bands % band_total
        source_band = band_index - offset
        inside = (source_band >= 0) & (source_band < band_total)
        kept = jax.random.randint(jax.random.fold_in(unit_key, 5), (NB,), 0, 8) > 0
        is_valid = (inside & kept).astype(jnp.int32)
        return jnp.stack([offset.astype(jnp.int32), (source // NBC).astype(jnp.int32), (source % NBC).astype(jnp.int32), is_valid], axis=1)
    units = jax.vmap(one_unit)(jnp.arange(unit_total, dtype=jnp.int32))
    units = units.reshape(VIEWS, band_total, half_bands, ROWS_DEV, NBC, 4)
    units = jnp.transpose(units, (0, 1, 3, 2, 4, 5))
    return units.reshape(VIEWS, H, NBW, 4).astype(jnp.int32)


def block_levels(stream_key, shape, cuts, least, largest):
    level = 1.0
    for axis_at, parts in cuts:
        heights = jax.random.uniform(jax.random.fold_in(jax.random.fold_in(stream_key, 6), axis_at), (parts,), jnp.float32, least / len(cuts), largest / len(cuts))
        level = level * jnp.repeat(jnp.exp(heights), shape[axis_at] // parts).reshape((-1,) + (1,) * (len(shape) - 1 - axis_at))
    return level


def noise(rng, shape, scale, bound, shards=(), held_as=jnp.bfloat16):
    entries = jax.random.normal(rng, shape, jnp.float32) * scale
    if len(shards) > 0:
        entries = block_levels(rng, shape, shards, -0.22, 0.18) * entries
    return jnp.clip(entries, min=-bound, max=bound).astype(held_as)


def setup_inputs(seed: int = 0, part: int = 0) -> dict:
    arg_keys = jax.random.split(jax.random.key(seed), 10)
    part_keys = jax.random.split(jax.random.fold_in(arg_keys[9], part), 10)
    return {
        "left_feats": noise(part_keys[0], (VIEWS, H, W, FEAT), 1.0, 6.0, ((0, 2), (1, 4), (2, 2))),
        "right_feats": noise(part_keys[1], (VIEWS, H, W, FEAT), 1.0, 6.0, ((0, 2), (1, 4), (2, 2))),
        "prev_hidden": jnp.clip(jax.random.uniform(part_keys[2], (VIEWS, H, W, HID), jnp.float32, -1.0, 1.0) * block_levels(part_keys[2], (VIEWS, H, W, HID), ((0, 2), (1, 4), (2, 2)), -0.4, 0.0), -1.0, 1.0).astype(jnp.bfloat16),
        "warp_list": draw_warp_list(jax.random.fold_in(jax.random.fold_in(arg_keys[9], part), 71), part),
        "enc_weight": noise(arg_keys[4], (DISP, HID), DISP ** -0.5, 0.4375),
        "hgate_w": noise(arg_keys[5], (KERN, 2 * HID, 2 * HID), (KERN * 2 * HID) ** -0.5, 0.15625),
        "hcand_w": noise(arg_keys[6], (KERN, 2 * HID, HID), (KERN * 2 * HID) ** -0.5, 0.15625),
        "vgate_w": noise(arg_keys[7], (KERN, 2 * HID, 2 * HID), (KERN * 2 * HID) ** -0.5, 0.15625),
        "vcand_w": noise(arg_keys[8], (KERN, 2 * HID, HID), (KERN * 2 * HID) ** -0.5, 0.15625),
    }


def conv_along(extended, weights, along, length):
    summed = None
    for kernel_tap in range(weights.shape[0]):
        sliced = lax.slice_in_dim(extended, kernel_tap, kernel_tap + length, axis=along)
        flat_rows = sliced.reshape(-1, sliced.shape[-1])
        partial_sum = jnp.dot(flat_rows, weights[kernel_tap], preferred_element_type=jnp.float32)
        partial_sum = partial_sum.reshape(sliced.shape[:-1] + (weights.shape[-1],))
        summed = partial_sum if summed is None else summed + partial_sum
    return summed


def gru_pass(hidden, motion, gates_w, cand_w, along):
    half_kernel = KERN // 2
    padding = [(0, 0), (0, 0), (0, 0), (0, 0)]
    padding[along] = (half_kernel, half_kernel)
    length = hidden.shape[along]
    extended = jnp.pad(jnp.concatenate([hidden, motion], axis=3), padding)
    gate_sums = conv_along(extended, gates_w, along, length)
    current = hidden.astype(jnp.float32)
    update_gate = jax.nn.sigmoid(gate_sums[..., :HID])
    reset_state = (jax.nn.sigmoid(gate_sums[..., HID:]) * current).astype(jnp.bfloat16)
    joined = jnp.pad(jnp.concatenate([reset_state, motion], axis=3), padding)
    candidate = jnp.tanh(conv_along(joined, cand_w, along, length))
    return ((1.0 - update_gate) * current + update_gate * candidate).astype(jnp.bfloat16)


def reference(left_feats, right_feats, prev_hidden, warp_list, enc_weight, hgate_w, hcand_w, vgate_w, vcand_w):
    view_count = prev_hidden.shape[0]
    height = prev_hidden.shape[1]
    image_width = prev_hidden.shape[2]
    band_blocks = COLS_DEV // BLK_COLS
    row_blocks = image_width // BLK_COLS
    offset = warp_list[..., 0]
    band_index = (jnp.arange(height, dtype=jnp.int32) // ROWS_DEV)[None, :, None]
    source_row = jnp.clip((band_index - offset) * ROWS_DEV + warp_list[..., 1], 0, height - 1).astype(jnp.int32)
    block_index = jnp.arange(row_blocks, dtype=jnp.int32)[None, None, :]
    source_block = ((block_index // band_blocks) * band_blocks + warp_list[..., 2]).astype(jnp.int32)
    view_index = jnp.arange(view_count, dtype=jnp.int32)[:, None, None]
    blocks = prev_hidden.reshape(view_count, height, row_blocks, BLK_COLS, HID)
    picked = blocks[view_index, source_row, source_block]
    warped = jnp.where(warp_list[..., 3][..., None, None] > 0, picked, jnp.zeros_like(picked))
    warped = warped.reshape(view_count, height, image_width, HID)

    score_scale = FEAT ** -0.5
    group_total = view_count * height // ROWS_DEV
    left_groups = left_feats.reshape(group_total, ROWS_DEV, image_width, FEAT)
    right_groups = right_feats.reshape(group_total, ROWS_DEV, image_width, FEAT)
    window_index = (jnp.arange(image_width, dtype=jnp.int32)[:, None] + DISP - jnp.arange(DISP, dtype=jnp.int32)[None, :]).astype(jnp.int32)

    def encode_group(pair):
        left_group, right_group = pair
        padded = jnp.concatenate([jnp.zeros((ROWS_DEV, DISP, FEAT), right_group.dtype), right_group], axis=1)
        windows = padded[:, window_index]
        correlation = jnp.einsum("rxdf,rxf->rxd", windows.astype(jnp.float32), left_group.astype(jnp.float32)) * score_scale
        correlation = correlation.astype(jnp.bfloat16)
        motion_rows = jnp.dot(correlation.reshape(-1, DISP), enc_weight, preferred_element_type=jnp.float32)
        return motion_rows.astype(jnp.bfloat16).reshape(ROWS_DEV, image_width, HID)

    motion = lax.map(encode_group, (left_groups, right_groups))
    motion = motion.reshape(view_count, height, image_width, HID)

    hidden = warped
    for iteration in range(ITERS):
        hidden = gru_pass(hidden, motion, hgate_w, hcand_w, 2)
        hidden = gru_pass(hidden, motion, vgate_w, vcand_w, 1)
    return hidden
```

```python
import functools

import jax
import jax.numpy as jnp
from jax import lax
from jax.experimental import pallas as pl
from jax.experimental.pallas import tpu as pltpu
from jax.sharding import PartitionSpec as P

bf16 = jnp.bfloat16
f32 = jnp.float32
SEAM = 16
VMEM_LIMIT = 56 << 20


def dotf(a, b):
    return jnp.dot(a, b, preferred_element_type=f32)


def sigmoid(v):
    return 0.5 * jnp.tanh(0.5 * v) + 0.5


def swap_near(value, axis):
    count = lax.axis_size(axis)
    pairs = [(i, i ^ 1) for i in range(count) if i ^ 1 < count]
    return lax.ppermute(value, axis, pairs)


def swap_far(value, axis):
    count = lax.axis_size(axis)
    pairs = []
    for i in range(1, count - 1, 2):
        pairs += [(i, i + 1), (i + 1, i)]
    return lax.ppermute(value, axis, pairs)


def whole(a):
    return pl.BlockSpec(a.shape, lambda *_: (0,) * a.ndim)


def motion_kernel(left_ref, right_ref, edge_ref, weight_ref, out_ref, window):
    disparities = weight_ref.shape[0]
    rows, width, feats = left_ref.shape
    tile = 128
    scale = feats**-0.5
    lane = lax.broadcasted_iota(jnp.int32, (tile, tile), 1)
    row = lax.broadcasted_iota(jnp.int32, (tile, tile), 0)
    keep = lane < row
    flip = (lane + row == tile - 1).astype(f32).astype(bf16)
    weight = weight_ref[...]
    for r in range(rows):
        window[r, pl.ds(0, disparities), :] = edge_ref[r]
        window[r, pl.ds(disparities, width), :] = right_ref[r]
    tiles = [(r, t * tile) for r in range(rows) for t in range(width // tile)]
    span = disparities + tile
    blocks = -(-span // tile)
    flipped = [dotf(flip, left_ref[r, pl.ds(x, tile), :]).astype(bf16) for r, x in tiles]
    scores = [
        lax.dot_general(
            part,
            window[r, pl.ds(x, blocks * tile), :],
            (((1,), (1,)), ((), ())),
            preferred_element_type=f32,
        )
        * scale
        for part, (r, x) in zip(flipped, tiles)
    ]
    skewed = []
    for score in scores:
        rolled = [
            pltpu.roll(score[:, tile * j : tile * (j + 1)], 0, 1, stride=1, stride_axis=0)
            for j in range(blocks)
        ]
        lanes = [
            jnp.where(keep, rolled[j], rolled[j + 1]).astype(bf16) for j in range(blocks - 1)
        ]
        skewed.append(jnp.concatenate(lanes, axis=1)[:, :disparities])
    motions = [dotf(part, weight).astype(bf16) for part in skewed]
    for part, (r, x) in zip(motions, tiles):
        out_ref[r, pl.ds(x, tile), :] = dotf(flip, part).astype(bf16)


def motion_of(left, right, edge, weight_flipped):
    rows, width, feats = left.shape
    disparities, hidden = weight_flipped.shape
    step = 4 if rows % 4 == 0 else 1
    block = lambda *shape: pl.BlockSpec((step,) + shape, lambda i: (i, 0, 0))
    return pl.pallas_call(
        motion_kernel,
        grid=(rows // step,),
        in_specs=[
            block(width, feats),
            block(width, feats),
            block(disparities, feats),
            whole(weight_flipped),
        ],
        out_specs=block(width, hidden),
        out_shape=jax.ShapeDtypeStruct((rows, width, hidden), bf16),
        scratch_shapes=[pltpu.VMEM((step, width + 256, feats), bf16)],
        compiler_params=pltpu.CompilerParams(vmem_limit_bytes=VMEM_LIMIT),
        name="motion",
    )(left, right, edge, weight_flipped)


def gather_kernel(sign_ref, near_ref, far_ref, prev_ref, out_near, out_far, sems):
    band_rows, band_blocks = near_ref.shape[1:3]
    slots = out_near.shape[0]
    width = out_near.shape[1]

    def copy(side, out, slot, row, block):
        return pltpu.make_async_copy(
            prev_ref.at[0, row, pl.ds(pl.multiple_of(block * width, width), width), :],
            out.at[slot],
            sems.at[side, slot],
        )

    sides = ((0, near_ref, out_near, sign_ref[0]), (1, far_ref, out_far, -sign_ref[0]))
    counts = []
    for side, list_ref, out, wanted in sides:

        def visit(i, count, side=side, list_ref=list_ref, out=out, wanted=wanted):
            row, block = i // band_blocks, i % band_blocks
            hit = (list_ref[0, row, block, 0] == wanted) & (count < slots)

            @pl.when(hit)
            def _():
                copy(side, out, count, list_ref[0, row, block, 1], list_ref[0, row, block, 2]).start()

            return count + hit.astype(jnp.int32)

        counts.append(lax.fori_loop(0, band_rows * band_blocks, visit, jnp.int32(0)))
    for side, list_ref, out, wanted in sides:

        @pl.loop(0, counts[side])
        def _(slot, side=side, out=out):
            copy(side, out, slot, 0, 0).wait()


def gather_blocks(sign, near_list, far_list, prev):
    band_rows, width, hidden = prev.shape[1:]
    band_blocks = near_list.shape[2]
    slots = band_rows * band_blocks // 4
    shape = jax.ShapeDtypeStruct((slots, width // band_blocks, hidden), bf16)
    smem = pl.BlockSpec(memory_space=pltpu.SMEM)
    anywhere = pl.BlockSpec(memory_space=pl.ANY)
    return pl.pallas_call(
        gather_kernel,
        in_specs=[smem, smem, smem, anywhere],
        out_specs=[anywhere, anywhere],
        out_shape=[shape, shape],
        scratch_shapes=[pltpu.SemaphoreType.DMA((2, slots))],
        name="gather",
    )(sign, near_list, far_list, prev)


def warp_kernel(sign_ref, list_ref, prev_ref, near_ref, far_ref, out_ref, zeros, sems):
    band_rows, band_blocks = list_ref.shape[1:3]
    slots, width = near_ref.shape[:2]
    zeros[...] = jnp.zeros_like(zeros)

    def visit(i, counts):
        row, block = i // band_blocks, i % band_blocks
        offset = list_ref[0, row, block, 0]
        valid = list_ref[0, row, block, 3] > 0
        target = out_ref.at[row, pl.ds(pl.multiple_of(block * width, width), width), :]
        is_near = offset == -sign_ref[0]
        is_far = offset == sign_ref[0]

        @pl.when(jnp.logical_not(valid))
        def _():
            pltpu.make_async_copy(zeros, target, sems.at[i]).start()

        @pl.when(valid & (offset == 0))
        def _():
            column = pl.multiple_of(list_ref[0, row, block, 2] * width, width)
            source = prev_ref.at[0, list_ref[0, row, block, 1], pl.ds(column, width), :]
            pltpu.make_async_copy(source, target, sems.at[i]).start()

        @pl.when(valid & is_near)
        def _():
            slot = jnp.minimum(counts[0], slots - 1)
            pltpu.make_async_copy(near_ref.at[slot], target, sems.at[i]).start()

        @pl.when(valid & is_far)
        def _():
            slot = jnp.minimum(counts[1], slots - 1)
            pltpu.make_async_copy(far_ref.at[slot], target, sems.at[i]).start()

        return counts[0] + is_near.astype(jnp.int32), counts[1] + is_far.astype(jnp.int32)

    lax.fori_loop(0, band_rows * band_blocks, visit, (jnp.int32(0), jnp.int32(0)))

    @pl.loop(0, band_rows * band_blocks)
    def _(i):
        row, block = i // band_blocks, i % band_blocks
        target = out_ref.at[row, pl.ds(pl.multiple_of(block * width, width), width), :]
        pltpu.make_async_copy(zeros, target, sems.at[i]).wait()


def warp_of(sign, warp_list, prev, near, far):
    band_rows, width, hidden = prev.shape[1:]
    band_blocks = warp_list.shape[2]
    smem = pl.BlockSpec(memory_space=pltpu.SMEM)
    anywhere = pl.BlockSpec(memory_space=pl.ANY)
    return pl.pallas_call(
        warp_kernel,
        in_specs=[smem, smem, anywhere, anywhere, anywhere],
        out_specs=anywhere,
        out_shape=jax.ShapeDtypeStruct((band_rows, width, hidden), bf16),
        scratch_shapes=[
            pltpu.VMEM((width // band_blocks, hidden), bf16),
            pltpu.SemaphoreType.DMA((band_rows * band_blocks,)),
        ],
        name="warp",
    )(sign, warp_list, prev, near, far)


def horizontal_kernel(
    place_ref, hidden_ref, motion_ref, seam_ref, gates_ref, cand_ref, out_ref, near_ref, far_ref,
    joined, reset, partial,
):
    rows, width, ch = hidden_ref.shape
    taps = gates_ref.shape[0]
    half = taps // 2
    right = place_ref[0]
    pad = SEAM
    own = pl.multiple_of(pad + pad * right, pad)
    seam = pl.multiple_of(pad + width * (1 - right), pad)
    span = width + SEAM
    gates = gates_ref[...].reshape(taps * 2 * ch, 2 * ch)
    for r in range(rows):
        for edge in (0, span + pad):
            joined[r, pl.ds(edge, pad), :] = jnp.zeros((pad, 2 * ch), bf16)
            reset[r, pl.ds(edge, pad), :] = jnp.zeros((pad, ch), bf16)
        joined[r, pl.ds(own, width), 0:ch] = hidden_ref[r]
        joined[r, pl.ds(own, width), ch : 2 * ch] = motion_ref[r]
        joined[r, pl.ds(seam, SEAM), :] = seam_ref[r]
    sums = [
        dotf(
            jnp.concatenate(
                [joined[r, pl.ds(pad - half + t, span), :] for t in range(taps)], axis=1
            ),
            gates,
        )
        for r in range(rows)
    ]
    update = []
    for r in range(rows):
        update.append(sigmoid(sums[r][:, :ch]))
        current = joined[r, pl.ds(pad, span), 0:ch].astype(f32)
        reset[r, pl.ds(pad, span), :] = (sigmoid(sums[r][:, ch:]) * current).astype(bf16)
    for r in range(rows):
        both = jnp.concatenate([reset[r], joined[r, :, ch : 2 * ch]], axis=1)
        for t in range(0, taps, 2):
            pair = jnp.concatenate([cand_ref[k] for k in range(t, min(t + 2, taps))], axis=1)
            partial[r, :, pl.ds(t * ch, pair.shape[1])] = dotf(both, pair)
    totals = []
    for r in range(rows):
        total = None
        for t in range(taps):
            part = partial[r, pl.ds(pad - half + t, span), pl.ds(t * ch, ch)]
            total = part if total is None else total + part
        totals.append(total)
    for r in range(rows):
        current = joined[r, pl.ds(pad, span), 0:ch].astype(f32)
        cand = jnp.tanh(totals[r])
        reset[r, pl.ds(pad, span), :] = ((1.0 - update[r]) * current + update[r] * cand).astype(bf16)
    for r in range(rows):
        out_ref[r] = reset[r, pl.ds(own, width), :]
    to_near = pl.program_id(0) == place_ref[1]

    @pl.when(to_near)
    def _():
        near_ref[...] = out_ref[...]

    @pl.when(jnp.logical_not(to_near))
    def _():
        far_ref[...] = out_ref[...]


def horizontal_pass(place, hidden, motion, seam, gates, cand):
    rows, width, ch = hidden.shape
    step = rows // 2
    taps = gates.shape[0]
    length = width + SEAM + 2 * SEAM
    block = lambda *shape: pl.BlockSpec((step,) + shape, lambda i, p: (i, 0, 0))
    kept = pl.BlockSpec((step, width, ch), lambda i, p: (0, 0, 0))
    half_band = jax.ShapeDtypeStruct((step, width, ch), bf16)
    return pl.pallas_call(
        horizontal_kernel,
        grid_spec=pltpu.PrefetchScalarGridSpec(
            num_scalar_prefetch=1,
            grid=(2,),
            in_specs=[
                block(width, ch),
                block(width, ch),
                block(SEAM, 2 * ch),
                whole(gates),
                whole(cand),
            ],
            out_specs=[block(width, ch), kept, kept],
            scratch_shapes=[
                pltpu.VMEM((step, length, 2 * ch), bf16),
                pltpu.VMEM((step, length, ch), bf16),
                pltpu.VMEM((step, length, taps * ch), f32),
            ],
        ),
        out_shape=[jax.ShapeDtypeStruct((rows, width, ch), bf16), half_band, half_band],
        compiler_params=pltpu.CompilerParams(vmem_limit_bytes=VMEM_LIMIT),
        name="horizontal",
    )(place, hidden, motion, seam, gates, cand)


def row_pair(taps):
    count = len(taps)
    none = jnp.zeros_like(taps[0])
    return jnp.concatenate(
        [
            jnp.concatenate(
                [taps[j] if j < count else none, taps[j - 1] if j > 0 else none], axis=1
            )
            for j in range(count + 1)
        ],
        axis=0,
    )


def vertical_kernel(
    place_ref, hidden_ref, motion_ref, hidden_near, hidden_far, motion_near, motion_far,
    gates_ref, cand_ref, out_ref, hidden_rim, motion_rim, reset_pair, cand_pair,
):
    rows, _, ch = hidden_ref.shape
    taps = gates_ref.shape[0]
    half = taps // 2
    rim = 2 * half
    near_below = place_ref[2]
    near, far = rim * near_below, rim - rim * near_below
    hidden_rim[pl.ds(near, rim)] = hidden_near[...]
    hidden_rim[pl.ds(far, rim)] = hidden_far[...]
    motion_rim[pl.ds(near, rim)] = motion_near[...]
    motion_rim[pl.ds(far, rim)] = motion_far[...]

    @pl.when(pl.program_id(0) == 0)
    def _():
        reset_pair[...] = row_pair([gates_ref[t][:, ch:] for t in range(taps)])
        cand_pair[...] = row_pair([cand_ref[t] for t in range(taps)])

    gates = gates_ref[...].reshape(taps * 2 * ch, 2 * ch)

    def row_of(own, rim_ref, y):
        if y < 0:
            return rim_ref[y + rim]
        return own[y] if y < rows else rim_ref[rim + y - rows]

    state = lambda y: row_of(hidden_ref, hidden_rim, y)
    flow = lambda y: row_of(motion_ref, motion_rim, y)

    def stack(first, last, source):
        return jnp.concatenate(
            [part for y in range(first, last + 1) for part in (source(y), flow(y))], axis=1
        )

    reset_sums, update = {}, []
    for y in (-half, rows):
        both = dotf(stack(y - half, y + half + 1, state), reset_pair[...])
        reset_sums[y], reset_sums[y + 1] = both[:, :ch], both[:, ch:]
    sums = [dotf(stack(y - half, y + half, state), gates) for y in range(rows)]
    for y in range(rows):
        update.append(sigmoid(sums[y][:, :ch]))
        reset_sums[y] = sums[y][:, ch:]
    reset = {
        y: (sigmoid(reset_sums[y]) * state(y).astype(f32)).astype(bf16)
        for y in range(-half, rows + half)
    }
    totals = []
    for y in range(0, rows, 2):
        both = dotf(stack(y - half, y + half + 1, lambda k: reset[k]), cand_pair[...])
        totals += [both[:, :ch], both[:, ch:]]
    for y in range(rows):
        cand = jnp.tanh(totals[y])
        blended = (1.0 - update[y]) * state(y).astype(f32) + update[y] * cand
        out_ref[0, y] = blended.astype(bf16)


def vertical_pass(place, hidden, motion, rims, gates, cand):
    rows, width, ch = hidden.shape
    taps = gates.shape[0]
    rim = rims[0].shape[0]
    tile = 256
    block = lambda count: pl.BlockSpec((count, tile, ch), lambda i, p: (0, i, 0))
    return pl.pallas_call(
        vertical_kernel,
        grid_spec=pltpu.PrefetchScalarGridSpec(
            num_scalar_prefetch=1,
            grid=(width // tile,),
            in_specs=[block(rows), block(rows)] + [block(rim)] * 4 + [whole(gates), whole(cand)],
            out_specs=pl.BlockSpec((1, rows, tile, ch), lambda i, p: (0, 0, i, 0)),
            scratch_shapes=[pltpu.VMEM((2 * rim, tile, ch), bf16)] * 2
            + [pltpu.VMEM(((taps + 1) * 2 * ch, 2 * ch), bf16)] * 2,
        ),
        out_shape=jax.ShapeDtypeStruct((1, rows, width, ch), bf16),
        compiler_params=pltpu.CompilerParams(vmem_limit_bytes=VMEM_LIMIT),
        name="vertical",
    )(place, hidden, motion, *rims, gates, cand)


def shards(
    left_feats, right_feats, prev_hidden, warp_list, enc_weight, hgate_w, hcand_w, vgate_w, vcand_w
):
    rows, width = prev_hidden.shape[1:3]
    disparities = enc_weight.shape[0]
    half = rows // 2
    odd = lax.axis_index("rows") % 2
    right = lax.axis_index("cols")
    place = jnp.stack([right, 1 - odd, 1 - odd]).astype(jnp.int32)
    sign = jnp.stack([1 - 2 * odd]).astype(jnp.int32)

    edge = lax.ppermute(right_feats[0, :, width - disparities :, :], "cols", [(0, 1)])
    near_list = swap_near(warp_list, "rows")
    far_list = swap_far(warp_list, "rows")
    motion = motion_of(left_feats[0], right_feats[0], edge, enc_weight[::-1])
    to_near, to_far = gather_blocks(sign, near_list, far_list, prev_hidden)
    near = swap_near(to_near, "rows")
    far = swap_far(to_far, "rows")
    low, high = motion[:half], motion[half:]
    motion_near = swap_near(jnp.where(odd == 0, high, low), "rows")
    motion_far = swap_far(jnp.where(odd == 0, low, high), "rows")
    warped = warp_of(sign, warp_list, prev_hidden, near, far)
    stacked = lambda at: jnp.concatenate(
        [warped[:, at : at + SEAM], motion[:, at : at + SEAM]], axis=2
    )
    seam = lax.ppermute(
        jnp.where(right == 0, stacked(width - SEAM), stacked(0)), "cols", [(0, 1), (1, 0)]
    )
    hidden, state_to_near, state_to_far = horizontal_pass(
        place, warped, motion, seam, hgate_w, hcand_w
    )
    state_near = swap_near(state_to_near, "rows")
    state_far = swap_far(state_to_far, "rows")
    return vertical_pass(
        place,
        hidden,
        motion,
        (state_near, state_far, motion_near, motion_far),
        vgate_w,
        vcand_w,
    )


def solution(mesh):
    spread = P(("groups", "cams"), "rows", "cols", None)
    return jax.shard_map(
        shards,
        mesh=mesh,
        in_specs=(spread,) * 4 + (P(),) * 5,
        out_specs=spread,
        check_vma=False,
    )
```

```python
import functools

import jax
import jax.numpy as jnp
from jax import lax
from jax.experimental import pallas as pl
from jax.experimental.pallas import tpu as pltpu
from jax.sharding import PartitionSpec as P

bf16 = jnp.bfloat16
f32 = jnp.float32
SEAM = 16


def dotf(a, b):
    return jnp.dot(a, b, preferred_element_type=f32)


def sigmoid(v):
    return 0.5 * jnp.tanh(0.5 * v) + 0.5


def swap_near(value, axis):
    count = lax.axis_size(axis)
    pairs = [(i, i ^ 1) for i in range(count) if i ^ 1 < count]
    return lax.ppermute(value, axis, pairs)


def swap_far(value, axis):
    count = lax.axis_size(axis)
    pairs = []
    for i in range(1, count - 1, 2):
        pairs += [(i, i + 1), (i + 1, i)]
    return lax.ppermute(value, axis, pairs)


IN_VMEM = pl.BlockSpec(memory_space=pltpu.VMEM)
IN_SMEM = pl.BlockSpec(memory_space=pltpu.SMEM)


def params(megabytes):
    return pltpu.CompilerParams(vmem_limit_bytes=megabytes << 20)


def motion_kernel(
    place_ref, left_ref, right_ref, edge_ref, weight_ref, out_ref, near_ref, far_ref, window
):
    disparities = weight_ref.shape[0]
    _, rows, width, feats = left_ref.shape
    tile = 128
    scale = feats**-0.5
    lane = lax.broadcasted_iota(jnp.int32, (tile, tile), 1)
    row = lax.broadcasted_iota(jnp.int32, (tile, tile), 0)
    keep = lane < row
    flip = (lane + row == tile - 1).astype(f32).astype(bf16)
    turned = jnp.concatenate(
        [dotf(flip, weight_ref[pl.ds(disparities - tile, tile), :]).astype(bf16),
         dotf(flip, weight_ref[pl.ds(0, tile), :]).astype(bf16)[2 * tile - disparities :, :]],
        axis=0,
    )
    span = disparities + tile
    blocks = -(-span // tile)
    far_edge = edge_ref.shape[2] - disparities
    group = rows // 2
    for first in range(0, rows, group):
        own = range(first, first + group)
        for r in own:
            window[r, pl.ds(0, disparities), :] = edge_ref[0, r, pl.ds(far_edge, disparities), :]
            window[r, pl.ds(disparities, width), :] = right_ref[0, r]
        tiles = [(r, t * tile) for r in own for t in range(width // tile)]
        flipped = [dotf(flip, left_ref[0, r, pl.ds(x, tile), :]).astype(bf16) for r, x in tiles]
        scores = [
            lax.dot_general(
                part,
                window[r, pl.ds(x, blocks * tile), :],
                (((1,), (1,)), ((), ())),
                preferred_element_type=f32,
            )
            * scale
            for part, (r, x) in zip(flipped, tiles)
        ]
        skewed = []
        for score in scores:
            rolled = [
                pltpu.roll(score[:, tile * j : tile * (j + 1)], 0, 1, stride=1, stride_axis=0)
                for j in range(blocks)
            ]
            lanes = [
                jnp.where(keep, rolled[j], rolled[j + 1]).astype(bf16) for j in range(blocks - 1)
            ]
            skewed.append(jnp.concatenate(lanes, axis=1)[:, :disparities])
        motions = [dotf(part, turned).astype(bf16) for part in skewed]
        for part, (r, x) in zip(motions, tiles):
            out_ref[r, pl.ds(x, tile), :] = dotf(flip, part).astype(bf16)
    half = rows // 2
    near_ref[...] = out_ref[pl.ds(half * place_ref[1], half)]
    far_ref[...] = out_ref[pl.ds(half - half * place_ref[1], half)]


def motion_of(place, left, right, edge, weight):
    _, rows, width, feats = left.shape
    hidden = weight.shape[1]
    half_band = jax.ShapeDtypeStruct((rows // 2, width, hidden), bf16)
    return pl.pallas_call(
        motion_kernel,
        in_specs=[IN_SMEM] + [IN_VMEM] * 4,
        out_specs=[IN_VMEM] * 3,
        out_shape=[jax.ShapeDtypeStruct((rows, width, hidden), bf16), half_band, half_band],
        scratch_shapes=[pltpu.VMEM((rows, width + 256, feats), bf16)],
        compiler_params=params(24),
        name="motion",
    )(place, left, right, edge, weight)


def gather_kernel(place_ref, near_list, far_list, prev_ref, near_out, far_out, near_ref, far_ref, sems):
    copies = [
        pltpu.make_async_copy(near_list, near_ref, sems.at[0]),
        pltpu.make_async_copy(far_list, far_ref, sems.at[1]),
    ]
    for copy in copies:
        copy.start()
    for copy in copies:
        copy.wait()
    _, band_blocks, _, band_rows = near_ref.shape
    slots, width, _ = near_out.shape
    sign = 2 * place_ref[1] - 1
    for list_ref, out, wanted in ((near_ref, near_out, sign), (far_ref, far_out, -sign)):

        def visit(i, count, list_ref=list_ref, out=out, wanted=wanted):
            row, block = i // band_blocks, i % band_blocks
            hit = (list_ref[0, block, 0, row] == wanted) & (count < slots)

            @pl.when(hit)
            def _():
                column = pl.multiple_of(list_ref[0, block, 2, row] * width, width)
                out[count] = prev_ref[0, list_ref[0, block, 1, row], pl.ds(column, width), :]

            return count + hit.astype(jnp.int32)

        lax.fori_loop(0, band_rows * band_blocks, visit, jnp.int32(0))


def gather_blocks(place, near_list, far_list, prev):
    _, band_blocks, _, band_rows = near_list.shape
    _, _, width, hidden = prev.shape
    slots = band_rows * band_blocks // 4
    shape = jax.ShapeDtypeStruct((slots, width // band_blocks, hidden), bf16)
    return pl.pallas_call(
        gather_kernel,
        in_specs=[IN_SMEM, IN_VMEM, IN_VMEM, IN_VMEM],
        out_specs=[IN_VMEM, IN_VMEM],
        out_shape=[shape, shape],
        scratch_shapes=[pltpu.SMEM(near_list.shape, jnp.int32)] * 2
        + [pltpu.SemaphoreType.DMA((2,))],
        compiler_params=params(4),
        name="gather",
    )(place, near_list, far_list, prev)


def warp_kernel(place_ref, list_ref, prev_ref, near_ref, far_ref, motion_ref, out_ref, seam_ref):
    _, band_blocks, _, band_rows = list_ref.shape
    slots, width, ch = near_ref.shape
    sign = 2 * place_ref[1] - 1
    nears, fars = jnp.int32(0), jnp.int32(0)
    for row in range(band_rows):
        for block in range(band_blocks):
            offset = list_ref[0, block, 0, row]
            is_near, is_far = offset == -sign, offset == sign
            column = pl.multiple_of(list_ref[0, block, 2, row] * width, width)
            local = prev_ref[0, list_ref[0, block, 1, row], pl.ds(column, width), :]
            near = near_ref[jnp.minimum(nears, slots - 1)]
            far = far_ref[jnp.minimum(fars, slots - 1)]
            picked = jnp.where(is_near, near, jnp.where(is_far, far, local))
            picked = jnp.where(list_ref[0, block, 3, row] > 0, picked, jnp.zeros_like(picked))
            out_ref[row, pl.ds(block * width, width), :] = picked
            nears += is_near.astype(jnp.int32)
            fars += is_far.astype(jnp.int32)
    total = out_ref.shape[1]
    edge = pl.multiple_of((total - SEAM) * (1 - place_ref[0]), SEAM)
    for row in range(band_rows):
        seam_ref[row, :, 0:ch] = out_ref[row, pl.ds(edge, SEAM), :]
        seam_ref[row, :, ch : 2 * ch] = motion_ref[row, pl.ds(edge, SEAM), :]


def warp_of(place, warp_list, prev, near, far, motion):
    _, rows, width, ch = prev.shape
    return pl.pallas_call(
        warp_kernel,
        in_specs=[IN_SMEM, IN_SMEM] + [IN_VMEM] * 4,
        out_specs=[IN_VMEM, IN_VMEM],
        out_shape=[
            jax.ShapeDtypeStruct((rows, width, ch), bf16),
            jax.ShapeDtypeStruct((rows, SEAM, 2 * ch), bf16),
        ],
        compiler_params=params(4),
        name="warp",
    )(place, warp_list, prev, near, far, motion)


def horizontal_kernel(
    place_ref, hidden_ref, motion_ref, seam_ref, gates_ref, cand_ref, out_ref, near_ref, far_ref,
    joined, reset, partial,
):
    band_rows, width, ch = hidden_ref.shape
    taps = gates_ref.shape[0]
    half = taps // 2
    right = place_ref[0]
    pad = SEAM
    own = pl.multiple_of(pad + pad * right, pad)
    seam = pl.multiple_of(pad + width * (1 - right), pad)
    span = width + SEAM
    gates = gates_ref[...].reshape(taps * 2 * ch, 2 * ch)
    group = joined.shape[0]
    rows = range(group)
    for first in range(0, band_rows, group):
        for r in rows:
            for edge in (0, span + pad):
                joined[r, pl.ds(edge, pad), :] = jnp.zeros((pad, 2 * ch), bf16)
                reset[r, pl.ds(edge, pad), :] = jnp.zeros((pad, ch), bf16)
            joined[r, pl.ds(own, width), 0:ch] = hidden_ref[first + r]
            joined[r, pl.ds(own, width), ch : 2 * ch] = motion_ref[first + r]
            joined[r, pl.ds(seam, SEAM), :] = seam_ref[first + r]
        sums = [
            dotf(
                jnp.concatenate(
                    [joined[r, pl.ds(pad - half + t, span), :] for t in range(taps)], axis=1
                ),
                gates,
            )
            for r in rows
        ]
        update = []
        for r in rows:
            update.append(sigmoid(sums[r][:, :ch]))
            current = joined[r, pl.ds(pad, span), 0:ch].astype(f32)
            reset[r, pl.ds(pad, span), :] = (sigmoid(sums[r][:, ch:]) * current).astype(bf16)
        for r in rows:
            both = jnp.concatenate([reset[r], joined[r, :, ch : 2 * ch]], axis=1)
            for t in range(0, taps, 2):
                pair = jnp.concatenate([cand_ref[k] for k in range(t, min(t + 2, taps))], axis=1)
                partial[r, :, pl.ds(t * ch, pair.shape[1])] = dotf(both, pair)
        totals = []
        for r in rows:
            total = None
            for t in range(taps):
                part = partial[r, pl.ds(pad - half + t, span), pl.ds(t * ch, ch)]
                total = part if total is None else total + part
            totals.append(total)
        for r in rows:
            current = joined[r, pl.ds(pad, span), 0:ch].astype(f32)
            cand = jnp.tanh(totals[r])
            blended = (1.0 - update[r]) * current + update[r] * cand
            reset[r, pl.ds(pad, span), :] = blended.astype(bf16)
        for r in rows:
            out_ref[first + r] = reset[r, pl.ds(own, width), :]
    count = band_rows // 2
    near_ref[...] = out_ref[pl.ds(count * place_ref[1], count)]
    far_ref[...] = out_ref[pl.ds(count - count * place_ref[1], count)]


def horizontal_pass(place, hidden, motion, seam, gates, cand):
    rows, width, ch = hidden.shape
    group = rows // 2
    taps = gates.shape[0]
    length = width + SEAM + 2 * SEAM
    half_band = jax.ShapeDtypeStruct((rows // 2, width, ch), bf16)
    return pl.pallas_call(
        horizontal_kernel,
        in_specs=[IN_SMEM] + [IN_VMEM] * 5,
        out_specs=[IN_VMEM] * 3,
        out_shape=[jax.ShapeDtypeStruct((rows, width, ch), bf16), half_band, half_band],
        scratch_shapes=[
            pltpu.VMEM((group, length, 2 * ch), bf16),
            pltpu.VMEM((group, length, ch), bf16),
            pltpu.VMEM((group, length, taps * ch), f32),
        ],
        compiler_params=params(24),
        name="horizontal",
    )(place, hidden, motion, seam, gates, cand)


def row_pair(taps):
    count = len(taps)
    none = jnp.zeros_like(taps[0])
    return jnp.concatenate(
        [
            jnp.concatenate(
                [taps[j] if j < count else none, taps[j - 1] if j > 0 else none], axis=1
            )
            for j in range(count + 1)
        ],
        axis=0,
    )


def vertical_kernel(
    place_ref, hidden_ref, motion_ref, hidden_near, hidden_far, motion_near, motion_far,
    gates_ref, cand_ref, out_ref, hidden_rim, motion_rim, reset_pair, cand_pair,
):
    rows, _, ch = hidden_ref.shape
    taps = gates_ref.shape[0]
    tile = out_ref.shape[2]
    half = taps // 2
    rim = 2 * half
    near_below = place_ref[1]
    near, far = rim * near_below, rim - rim * near_below
    here = pl.ds(pl.multiple_of(pl.program_id(0) * tile, tile), tile)
    hidden_rim[pl.ds(near, rim)] = hidden_near[:, here, :]
    hidden_rim[pl.ds(far, rim)] = hidden_far[:, here, :]
    motion_rim[pl.ds(near, rim)] = motion_near[:, here, :]
    motion_rim[pl.ds(far, rim)] = motion_far[:, here, :]

    @pl.when(pl.program_id(0) == 0)
    def _():
        reset_pair[...] = row_pair([gates_ref[t][:, ch:] for t in range(taps)])
        cand_pair[...] = row_pair([cand_ref[t] for t in range(taps)])

    gates = gates_ref[...].reshape(taps * 2 * ch, 2 * ch)

    def row_of(own, rim_ref, y):
        if y < 0:
            return rim_ref[y + rim]
        return own[y, here, :] if y < rows else rim_ref[rim + y - rows]

    state = lambda y: row_of(hidden_ref, hidden_rim, y)
    flow = lambda y: row_of(motion_ref, motion_rim, y)

    def stack(first, last, source):
        return jnp.concatenate(
            [part for y in range(first, last + 1) for part in (source(y), flow(y))], axis=1
        )

    reset_sums, update = {}, []
    for y in (-half, rows):
        both = dotf(stack(y - half, y + half + 1, state), reset_pair[...])
        reset_sums[y], reset_sums[y + 1] = both[:, :ch], both[:, ch:]
    sums = [dotf(stack(y - half, y + half, state), gates) for y in range(rows)]
    for y in range(rows):
        update.append(sigmoid(sums[y][:, :ch]))
        reset_sums[y] = sums[y][:, ch:]
    reset = {
        y: (sigmoid(reset_sums[y]) * state(y).astype(f32)).astype(bf16)
        for y in range(-half, rows + half)
    }
    totals = []
    for y in range(0, rows, 2):
        both = dotf(stack(y - half, y + half + 1, lambda k: reset[k]), cand_pair[...])
        totals += [both[:, :ch], both[:, ch:]]
    for y in range(rows):
        cand = jnp.tanh(totals[y])
        blended = (1.0 - update[y]) * state(y).astype(f32) + update[y] * cand
        out_ref[0, y] = blended.astype(bf16)


def vertical_pass(place, hidden, motion, rims, gates, cand):
    rows, width, ch = hidden.shape
    taps = gates.shape[0]
    rim = rims[0].shape[0]
    tile = 256
    return pl.pallas_call(
        vertical_kernel,
        grid=(width // tile,),
        in_specs=[IN_SMEM] + [IN_VMEM] * 8,
        out_specs=pl.BlockSpec((1, rows, tile, ch), lambda i: (0, 0, i, 0)),
        scratch_shapes=[pltpu.VMEM((2 * rim, tile, ch), bf16)] * 2
        + [pltpu.VMEM(((taps + 1) * 2 * ch, 2 * ch), bf16)] * 2,
        out_shape=jax.ShapeDtypeStruct((1, rows, width, ch), bf16),
        compiler_params=params(24),
        name="vertical",
    )(place, hidden, motion, *rims, gates, cand)


def shards(
    left_feats, right_feats, prev_hidden, warp_list, enc_weight, hgate_w, hcand_w, vgate_w, vcand_w
):
    right = lax.axis_index("cols")
    below = 1 - lax.axis_index("rows") % 2
    place = jnp.stack([right, below]).astype(jnp.int32)
    swap_cols = lambda value: lax.ppermute(value, "cols", [(0, 1), (1, 0)])
    pinned = lax.optimization_barrier

    warp_list = jnp.transpose(warp_list, (0, 2, 3, 1))
    edge = lax.ppermute(right_feats, "cols", [(0, 1)])
    near_list = swap_near(warp_list, "rows")
    far_list = swap_far(warp_list, "rows")
    motion, motion_to_near, motion_to_far = motion_of(
        place, left_feats, right_feats, edge, enc_weight
    )
    near_list, far_list, motion = pinned((near_list, far_list, motion))
    to_near, to_far = gather_blocks(place, near_list, far_list, prev_hidden)
    near = swap_near(to_near, "rows")
    far = swap_far(to_far, "rows")
    motion_near = swap_near(motion_to_near, "rows")
    motion_far = swap_far(motion_to_far, "rows")
    warped, seam = warp_of(place, warp_list, prev_hidden, near, far, motion)
    seam = swap_cols(seam)
    hidden, to_near, to_far = horizontal_pass(place, warped, motion, seam, hgate_w, hcand_w)
    state_near = swap_near(to_near, "rows")
    state_far = swap_far(to_far, "rows")
    rims = (state_near, state_far, motion_near, motion_far)
    return vertical_pass(place, hidden, motion, rims, vgate_w, vcand_w)


def solution(mesh):
    spread = P(("groups", "cams"), "rows", "cols", None)
    return jax.shard_map(
        shards,
        mesh=mesh,
        in_specs=(spread,) * 4 + (P(),) * 5,
        out_specs=spread,
        check_vma=False,
    )
```

```python
import functools

import jax
import jax.numpy as jnp
from jax import lax
from jax.experimental import pallas as pl
from jax.experimental.pallas import tpu as pltpu
from jax.sharding import PartitionSpec as P

bf16 = jnp.bfloat16
f32 = jnp.float32
SEAM = 16


def dotf(a, b):
    return jnp.dot(a, b, preferred_element_type=f32)


def sigmoid(v):
    return 0.5 * jnp.tanh(0.5 * v) + 0.5


def state_rows(*pieces):
    return [(piece, r) for piece in pieces for r in range(piece.shape[0])]


def swap_near(value, axis):
    count = lax.axis_size(axis)
    pairs = [(i, i ^ 1) for i in range(count) if i ^ 1 < count]
    return lax.ppermute(value, axis, pairs)


def swap_far(value, axis):
    count = lax.axis_size(axis)
    pairs = []
    for i in range(1, count - 1, 2):
        pairs += [(i, i + 1), (i + 1, i)]
    return lax.ppermute(value, axis, pairs)


IN_VMEM = pl.BlockSpec(memory_space=pltpu.VMEM)
IN_SMEM = pl.BlockSpec(memory_space=pltpu.SMEM)
IN_HBM = pl.BlockSpec(memory_space=pltpu.HBM)


def in_hbm(value):
    return pltpu.with_memory_space_constraint(value, pltpu.HBM)


def params(megabytes):
    return pltpu.CompilerParams(vmem_limit_bytes=megabytes << 20)


def motion_kernel(
    first, left_feats, right_feats, edge_ref, weight_ref, out_ref, left_ref, window, sems
):
    disparities = weight_ref.shape[0]
    rows, width, feats = left_ref.shape
    tile = 128
    own = pl.ds(first, rows)
    loads = [
        pltpu.make_async_copy(left_feats.at[0, own], left_ref, sems.at[0]),
        pltpu.make_async_copy(
            right_feats.at[0, own], window.at[:, pl.ds(disparities, width), :], sems.at[1]
        ),
    ]
    for load in loads:
        load.start()
    far_edge = edge_ref.shape[2] - disparities
    for r in range(rows):
        window[r, pl.ds(0, disparities), :] = edge_ref[
            0, first + r, pl.ds(far_edge, disparities), :
        ]
    scale = feats**-0.5
    lane = lax.broadcasted_iota(jnp.int32, (tile, tile), 1)
    row = lax.broadcasted_iota(jnp.int32, (tile, tile), 0)
    keep = lane < row
    flip = (lane + row == tile - 1).astype(f32).astype(bf16)
    turned = jnp.concatenate(
        [
            dotf(flip, weight_ref[pl.ds(disparities - tile, tile), :]).astype(bf16),
            dotf(flip, weight_ref[pl.ds(0, tile), :]).astype(bf16)[2 * tile - disparities :, :],
        ],
        axis=0,
    )
    span = disparities + tile
    blocks = -(-span // tile)
    tiles = [(r, t * tile) for r in range(rows) for t in range(width // tile)]
    for load in loads:
        load.wait()
    flipped = [dotf(flip, left_ref[r, pl.ds(x, tile), :]).astype(bf16) for r, x in tiles]
    scores = [
        lax.dot_general(
            part,
            window[r, pl.ds(x, blocks * tile), :],
            (((1,), (1,)), ((), ())),
            preferred_element_type=f32,
        )
        * scale
        for part, (r, x) in zip(flipped, tiles)
    ]
    skewed = []
    for score in scores:
        rolled = [
            pltpu.roll(score[:, tile * j : tile * (j + 1)], 0, 1, stride=1, stride_axis=0)
            for j in range(blocks)
        ]
        lanes = [jnp.where(keep, rolled[j], rolled[j + 1]).astype(bf16) for j in range(blocks - 1)]
        skewed.append(jnp.concatenate(lanes, axis=1)[:, :disparities])
    motions = [dotf(part, turned).astype(bf16) for part in skewed]
    for part, (r, x) in zip(motions, tiles):
        out_ref[r, pl.ds(x, tile), :] = dotf(flip, part).astype(bf16)


def motion_of(first, rows, left, right, edge, weight):
    width, feats = left.shape[2:]
    return pl.pallas_call(
        functools.partial(motion_kernel, first),
        in_specs=[IN_HBM, IN_HBM, IN_VMEM, IN_VMEM],
        out_specs=IN_VMEM,
        out_shape=jax.ShapeDtypeStruct((rows, width, weight.shape[1]), bf16),
        scratch_shapes=[
            pltpu.VMEM((rows, width, feats), bf16),
            pltpu.VMEM((rows, width + 256, feats), bf16),
            pltpu.SemaphoreType.DMA((2,)),
        ],
        compiler_params=params(16),
        name="motion",
    )(in_hbm(left), in_hbm(right), edge, weight)


def edges_kernel(place_ref, low_ref, high_ref, near_ref, far_ref):
    count = near_ref.shape[0]
    low, high = low_ref[pl.ds(0, count)], high_ref[pl.ds(high_ref.shape[0] - count, count)]
    below = place_ref[1] == 1
    near_ref[...] = jnp.where(below, high, low)
    far_ref[...] = jnp.where(below, low, high)


def edges_of(place, low, high, count):
    shape = jax.ShapeDtypeStruct((count,) + low.shape[1:], bf16)
    return pl.pallas_call(
        edges_kernel,
        in_specs=[IN_SMEM, IN_VMEM, IN_VMEM],
        out_specs=[IN_VMEM, IN_VMEM],
        out_shape=[shape, shape],
        compiler_params=params(4),
        name="edges",
    )(place, low, high)


def gather_kernel(
    place_ref, near_list, far_list, prev_ref, near_out, far_out, near_ref, far_ref, picks, sems
):
    lists = [
        pltpu.make_async_copy(near_list, near_ref, sems.at[0, 0]),
        pltpu.make_async_copy(far_list, far_ref, sems.at[1, 0]),
    ]
    for load in lists:
        load.start()
    _, band_blocks, _, band_rows = near_ref.shape
    slots, width, _ = near_out.shape
    sign = 2 * place_ref[1] - 1
    copies = []
    sides = ((near_ref, near_out, sign), (far_ref, far_out, -sign))
    for side, (list_ref, out, wanted) in enumerate(sides):
        lists[side].wait()
        count, source = jnp.int32(0), jnp.int32(0)
        for r in range(band_rows):
            for block in range(band_blocks):
                hit = list_ref[0, block, 0, r] == wanted
                count = count + hit.astype(jnp.int32)
                here = list_ref[0, block, 1, r] * band_blocks + list_ref[0, block, 2, r]
                source = jnp.where(hit & (count <= slots), here, source)
                picks[side, jnp.clip(count - 1, 0, slots - 1)] = source
        for slot in range(slots):
            row = picks[side, slot] // band_blocks
            column = pl.multiple_of(picks[side, slot] % band_blocks * width, width)
            block = prev_ref.at[0, row, pl.ds(column, width), :]
            copies.append(pltpu.make_async_copy(block, out.at[slot], sems.at[side, slot]))
            copies[-1].start()
    for copy in copies:
        copy.wait()


def gather_blocks(place, near_list, far_list, prev):
    _, band_blocks, _, band_rows = near_list.shape
    _, _, width, hidden = prev.shape
    slots = band_rows * band_blocks // 4
    shape = jax.ShapeDtypeStruct((slots, width // band_blocks, hidden), bf16)
    return pl.pallas_call(
        gather_kernel,
        in_specs=[IN_SMEM, IN_VMEM, IN_VMEM, IN_HBM],
        out_specs=[IN_VMEM, IN_VMEM],
        out_shape=[shape, shape],
        scratch_shapes=[pltpu.SMEM(near_list.shape, jnp.int32)] * 2
        + [pltpu.SMEM((2, slots), jnp.int32), pltpu.SemaphoreType.DMA((2, slots))],
        compiler_params=params(4),
        name="gather",
    )(place, near_list, far_list, in_hbm(prev))


def pick_blocks(place_ref, list_ref, visit):
    _, band_blocks, _, band_rows = list_ref.shape
    last = band_rows * band_blocks // 4 - 1
    sign = 2 * place_ref[1] - 1
    nears, fars = jnp.int32(0), jnp.int32(0)
    for row in range(band_rows):
        for block in range(band_blocks):
            offset = list_ref[0, block, 0, row]
            is_near, is_far = offset == -sign, offset == sign
            visit(row, block, is_near, is_far, jnp.minimum(nears, last), jnp.minimum(fars, last))
            nears += is_near.astype(jnp.int32)
            fars += is_far.astype(jnp.int32)


def seam_kernel(place_ref, list_ref, prev_ref, near_ref, far_ref, low_ref, high_ref, seam_ref):
    band_blocks = list_ref.shape[1]
    width, ch = near_ref.shape[1:]
    is_left = place_ref[0] == 0
    start = pl.multiple_of((width - SEAM) * (1 - place_ref[0]), SEAM)
    inside = pl.ds(start, SEAM)

    def visit(row, block, is_near, is_far, near_slot, far_slot):
        if block in (0, band_blocks - 1):
            source = pl.multiple_of(list_ref[0, block, 2, row] * width + start, SEAM)
            local = prev_ref[0, list_ref[0, block, 1, row], pl.ds(source, SEAM), :]
            near, far = near_ref[near_slot, inside, :], far_ref[far_slot, inside, :]
            picked = jnp.where(is_near, near, jnp.where(is_far, far, local))
            picked = jnp.where(list_ref[0, block, 3, row] > 0, picked, jnp.zeros_like(picked))
            if block > 0:
                picked = jnp.where(is_left, picked, seam_ref[row, :, 0:ch])
            seam_ref[row, :, 0:ch] = picked

    pick_blocks(place_ref, list_ref, visit)
    edge = pl.multiple_of((band_blocks * width - SEAM) * (1 - place_ref[0]), SEAM)
    half = low_ref.shape[0]
    seam_ref[pl.ds(0, half), :, ch : 2 * ch] = low_ref[:, pl.ds(edge, SEAM), :]
    seam_ref[pl.ds(half, half), :, ch : 2 * ch] = high_ref[:, pl.ds(edge, SEAM), :]


def seam_of(place, warp_list, prev, near, far, low, high):
    _, rows, _, ch = prev.shape
    return pl.pallas_call(
        seam_kernel,
        in_specs=[IN_SMEM, IN_SMEM] + [IN_VMEM] * 5,
        out_specs=IN_VMEM,
        out_shape=jax.ShapeDtypeStruct((rows, SEAM, 2 * ch), bf16),
        compiler_params=params(4),
        name="seam",
    )(place, warp_list, prev, near, far, low, high)


def warp_kernel(place_ref, list_ref, prev_ref, near_ref, far_ref, out_ref):
    width = near_ref.shape[1]

    def visit(row, block, is_near, is_far, near_slot, far_slot):
        column = pl.multiple_of(list_ref[0, block, 2, row] * width, width)
        local = prev_ref[0, list_ref[0, block, 1, row], pl.ds(column, width), :]
        picked = jnp.where(
            is_near, near_ref[near_slot], jnp.where(is_far, far_ref[far_slot], local)
        )
        picked = jnp.where(list_ref[0, block, 3, row] > 0, picked, jnp.zeros_like(picked))
        out_ref[row, pl.ds(block * width, width), :] = picked

    pick_blocks(place_ref, list_ref, visit)


def warp_of(place, warp_list, prev, near, far):
    return pl.pallas_call(
        warp_kernel,
        in_specs=[IN_SMEM, IN_SMEM] + [IN_VMEM] * 3,
        out_specs=IN_VMEM,
        out_shape=jax.ShapeDtypeStruct(prev.shape[1:], bf16),
        compiler_params=params(4),
        name="warp",
    )(place, warp_list, prev, near, far)


def horizontal_kernel(
    rows, place_ref, hidden_ref, low_ref, high_ref, seam_ref, gates_ref, cand_ref, out_ref, *rest
):
    *edges, joined, reset, partial = rest
    _, width, ch = hidden_ref.shape
    taps = gates_ref.shape[0]
    half = taps // 2
    right = place_ref[0]
    pad = SEAM
    own = pl.multiple_of(pad + pad * right, pad)
    seam = pl.multiple_of(pad + width * (1 - right), pad)
    span = width + SEAM
    flow = state_rows(low_ref, high_ref)
    gates = gates_ref[...].reshape(taps * 2 * ch, 2 * ch)
    count = range(len(rows))
    for r in count:
        piece, at = flow[rows[r]]
        for edge in (0, span + pad):
            joined[r, pl.ds(edge, pad), :] = jnp.zeros((pad, 2 * ch), bf16)
            reset[r, pl.ds(edge, pad), :] = jnp.zeros((pad, ch), bf16)
        joined[r, pl.ds(own, width), 0:ch] = hidden_ref[rows[r]]
        joined[r, pl.ds(own, width), ch : 2 * ch] = piece[at]
        joined[r, pl.ds(seam, SEAM), :] = seam_ref[rows[r]]
    sums = [
        dotf(
            jnp.concatenate(
                [joined[r, pl.ds(pad - half + t, span), :] for t in range(taps)], axis=1
            ),
            gates,
        )
        for r in count
    ]
    update = []
    for r in count:
        update.append(sigmoid(sums[r][:, :ch]))
        current = joined[r, pl.ds(pad, span), 0:ch].astype(f32)
        reset[r, pl.ds(pad, span), :] = (sigmoid(sums[r][:, ch:]) * current).astype(bf16)
    for r in count:
        both = jnp.concatenate([reset[r], joined[r, :, ch : 2 * ch]], axis=1)
        for t in range(0, taps, 2):
            pair = jnp.concatenate([cand_ref[k] for k in range(t, min(t + 2, taps))], axis=1)
            partial[r, :, pl.ds(t * ch, pair.shape[1])] = dotf(both, pair)
    totals = []
    for r in count:
        total = None
        for t in range(taps):
            part = partial[r, pl.ds(pad - half + t, span), pl.ds(t * ch, ch)]
            total = part if total is None else total + part
        totals.append(total)
    for r in count:
        current = joined[r, pl.ds(pad, span), 0:ch].astype(f32)
        cand = jnp.tanh(totals[r])
        blended = (1.0 - update[r]) * current + update[r] * cand
        reset[r, pl.ds(pad, span), :] = blended.astype(bf16)
    for r in count:
        out_ref[r] = reset[r, pl.ds(own, width), :]
    if edges:
        near_ref, far_ref = edges
        near_ref[...] = out_ref[pl.ds(half * place_ref[1], half)]
        far_ref[...] = out_ref[pl.ds(half - half * place_ref[1], half)]


def horizontal_pass(rows, send, place, hidden, low, high, seam, gates, cand):
    _, width, ch = hidden.shape
    taps = gates.shape[0]
    length = width + SEAM + 2 * SEAM
    shape = lambda count: jax.ShapeDtypeStruct((count, width, ch), bf16)
    shapes = [shape(len(rows))] + [shape(taps // 2)] * (2 if send else 0)
    return pl.pallas_call(
        functools.partial(horizontal_kernel, rows),
        in_specs=[IN_SMEM] + [IN_VMEM] * 6,
        out_specs=[IN_VMEM] * len(shapes),
        out_shape=shapes,
        scratch_shapes=[
            pltpu.VMEM((len(rows), length, 2 * ch), bf16),
            pltpu.VMEM((len(rows), length, ch), bf16),
            pltpu.VMEM((len(rows), length, taps * ch), f32),
        ],
        compiler_params=params(24),
        name="horizontal",
    )(place, hidden, low, high, seam, gates, cand)


def pairs_kernel(cand_ref, out_ref):
    taps, depth, ch = cand_ref.shape
    for j in range(taps + 1):
        none = jnp.zeros((depth, ch), bf16)
        out_ref[j, :, 0:ch] = cand_ref[j] if j < taps else none
        out_ref[j, :, ch : 2 * ch] = cand_ref[j - 1] if j > 0 else none


def pairs_of(cand):
    taps, depth, ch = cand.shape
    return pl.pallas_call(
        pairs_kernel,
        in_specs=[IN_VMEM],
        out_specs=IN_VMEM,
        out_shape=jax.ShapeDtypeStruct((taps + 1, depth, 2 * ch), bf16),
        compiler_params=params(4),
        name="pairs",
    )(cand)


def banded(outer_ref, inner_ref, half):
    outer = state_rows(outer_ref)
    return outer[:half] + state_rows(inner_ref) + outer[half:]


def stack(sources, rows):
    return jnp.concatenate(
        [piece[at] for y in rows for piece, at in (source[y] for source in sources)], axis=1
    )


def gates_kernel(
    outer_ref, inner_ref, low_ref, high_ref, gates_ref, update_ref, reset_ref, partial_ref
):
    taps, depth, wide = gates_ref.shape
    ch = wide // 2
    half = taps // 2
    state = banded(outer_ref, inner_ref, half)
    sources = (state, state_rows(low_ref, high_ref))
    rows = len(state)
    inner = range(half, rows - half)
    weights = lambda first, last: gates_ref[pl.ds(first, last - first)].reshape(-1, wide)
    sums = [dotf(stack(sources, range(y - half, y + half + 1)), weights(0, taps)) for y in inner]
    for i, y in enumerate([*range(half), *range(rows - half, rows)]):
        first, last = max(y - half, 0), min(y + half + 1, rows)
        partial_ref[i] = dotf(
            stack(sources, range(first, last)), weights(first - y + half, last - y + half)
        )
    for i, y in enumerate(inner):
        piece, at = state[y]
        update_ref[i] = sigmoid(sums[i][:, :ch])
        reset_ref[i] = (sigmoid(sums[i][:, ch:]) * piece[at].astype(f32)).astype(bf16)


def inner_gates(outer, inner, low, high, gates):
    count, width, ch = inner.shape
    half = gates.shape[0] // 2
    return pl.pallas_call(
        gates_kernel,
        in_specs=[IN_VMEM] * 5,
        out_specs=[IN_VMEM] * 3,
        out_shape=[
            jax.ShapeDtypeStruct((count, width, ch), f32),
            jax.ShapeDtypeStruct((count, width, ch), bf16),
            jax.ShapeDtypeStruct((2 * half, width, 2 * ch), f32),
        ],
        compiler_params=params(24),
        name="inner_gates",
    )(outer, inner, low, high, gates)


def outer_kernel(
    place_ref, outer_ref, partial_ref, hidden_near, hidden_far, motion_near, motion_far, gates_ref,
    update_ref, reset_ref, near_ref, far_ref, hidden_rim, motion_rim,
):
    taps, _, wide = gates_ref.shape
    ch = wide // 2
    half = taps // 2
    near = half * place_ref[1]
    far = half - near
    hidden_rim[pl.ds(near, half)] = hidden_near[...]
    hidden_rim[pl.ds(far, half)] = hidden_far[...]
    motion_rim[pl.ds(near, half)] = motion_near[...]
    motion_rim[pl.ds(far, half)] = motion_far[...]
    sources = (state_rows(hidden_rim), state_rows(motion_rim))
    weights = lambda first, last: gates_ref[pl.ds(first, last - first)].reshape(-1, wide)
    sums = []
    for i in range(half):
        sums.append(dotf(stack(sources, range(i, half)), weights(0, half - i)))
    for i in range(half):
        sums.append(dotf(stack(sources, range(half, half + i + 1)), weights(taps - 1 - i, taps)))
    for i in range(2 * half):
        total = sums[i] + partial_ref[i]
        update_ref[i] = sigmoid(total[:, :ch])
        reset_ref[i] = (sigmoid(total[:, ch:]) * outer_ref[i].astype(f32)).astype(bf16)
    near_ref[...] = reset_ref[pl.ds(near, half)]
    far_ref[...] = reset_ref[pl.ds(far, half)]


def outer_gates(place, outer, partial, rims, gates):
    count, width, ch = outer.shape
    half = gates.shape[0] // 2
    shape = lambda n, kind: jax.ShapeDtypeStruct((n, width, ch), kind)
    return pl.pallas_call(
        outer_kernel,
        in_specs=[IN_SMEM] + [IN_VMEM] * 7,
        out_specs=[IN_VMEM] * 4,
        out_shape=[shape(count, f32), shape(count, bf16), shape(half, bf16), shape(half, bf16)],
        scratch_shapes=[pltpu.VMEM((2 * half, width, ch), bf16)] * 2,
        compiler_params=params(16),
        name="outer_gates",
    )(place, outer, partial, *rims, gates)


def blend(state, update, total):
    return ((1.0 - update) * state.astype(f32) + update * jnp.tanh(total)).astype(bf16)


def cand_kernel(
    place_ref, reset_outer, reset_inner, low_ref, high_ref, motion_near, motion_far, inner_ref,
    update_ref, pairs_ref, out_ref, partial_ref, motion_rim,
):
    blocks, depth, wide = pairs_ref.shape
    ch = wide // 2
    half = (blocks - 1) // 2
    near = half * place_ref[1]
    motion_rim[pl.ds(near, half)] = motion_near[...]
    motion_rim[pl.ds(half - near, half)] = motion_far[...]
    reset = banded(reset_outer, reset_inner, half)
    sources = (reset, state_rows(low_ref, high_ref))
    rows = len(reset)
    weights = lambda first, last: pairs_ref[pl.ds(first, last - first)].reshape(-1, wide)
    sums = {}
    for y in range(half, rows - half, 2):
        rows_read = range(y - half, y + half + 2)
        sums[y] = dotf(stack(sources, rows_read), weights(0, blocks))
    rim = state_rows(motion_rim)
    flow_weights = lambda first, last: pairs_ref[pl.ds(first, last - first), ch:, :].reshape(
        -1, wide
    )
    for i, y in enumerate((0, rows - half)):
        first, last = max(y - half, 0), min(y + half + 2, rows)
        total = dotf(stack(sources, range(first, last)), weights(first - y + half, last - y + half))
        at = (0, half) if i == 0 else (blocks - half, blocks)
        total += dotf(stack((rim,), range(half * i, half * i + half)), flow_weights(*at))
        partial_ref[2 * i], partial_ref[2 * i + 1] = total[:, :ch], total[:, ch:]
    for y in range(half, rows - half, 2):
        for k in range(2):
            i = y - half + k
            total = sums[y][:, k * ch : (k + 1) * ch]
            out_ref[i] = blend(inner_ref[i], update_ref[i], total)


def inner_states(place, resets, low, high, motion_rims, inner, update, pairs):
    count, width, ch = inner.shape
    half = (pairs.shape[0] - 1) // 2
    return pl.pallas_call(
        cand_kernel,
        in_specs=[IN_SMEM] + [IN_VMEM] * 9,
        out_specs=[IN_VMEM] * 2,
        out_shape=[
            jax.ShapeDtypeStruct((count, width, ch), bf16),
            jax.ShapeDtypeStruct((2 * half, width, ch), f32),
        ],
        scratch_shapes=[pltpu.VMEM((2 * half, width, ch), bf16)],
        compiler_params=params(16),
        name="inner_states",
    )(place, *resets, low, high, *motion_rims, inner, update, pairs)


def final_kernel(
    place_ref, inner_ref, reset_near, reset_far, outer_ref, update_ref, partial_ref, pairs_ref,
    out_ref, reset_rim, done, sems,
):
    blocks, _, wide = pairs_ref.shape
    ch = wide // 2
    half = (blocks - 1) // 2
    rows = out_ref.shape[1]
    count = inner_ref.shape[0]
    stores = [pltpu.make_async_copy(inner_ref, out_ref.at[0, pl.ds(half, count)], sems.at[0])]
    stores[0].start()
    near = half * place_ref[1]
    reset_rim[pl.ds(near, half)] = reset_near[...]
    reset_rim[pl.ds(half - near, half)] = reset_far[...]
    rim = state_rows(reset_rim)
    sums = []
    for i in range(2):
        first = 0 if i == 0 else blocks - half
        weights = pairs_ref[pl.ds(first, half), :ch, :].reshape(-1, wide)
        sums.append(dotf(stack((rim,), range(half * i, half * i + half)), weights))
    for i in range(2):
        for k in range(2):
            at = 2 * i + k
            total = partial_ref[at] + sums[i][:, k * ch : (k + 1) * ch]
            done[at] = blend(outer_ref[at], update_ref[at], total)
        target = out_ref.at[0, pl.ds(0 if i == 0 else rows - half, half)]
        stores.append(pltpu.make_async_copy(done.at[pl.ds(half * i, half)], target, sems.at[i + 1]))
        stores[-1].start()
    for store in stores:
        store.wait()


def final_states(place, inner, reset_rims, outer, update, partial, pairs):
    count, width, ch = outer.shape
    rows = count + inner.shape[0]
    return pl.pallas_call(
        final_kernel,
        in_specs=[IN_SMEM] + [IN_VMEM] * 7,
        out_specs=IN_HBM,
        out_shape=jax.ShapeDtypeStruct((1, rows, width, ch), bf16),
        scratch_shapes=[pltpu.VMEM((count, width, ch), bf16)] * 2 + [pltpu.SemaphoreType.DMA((3,))],
        compiler_params=params(16),
        name="final_states",
    )(place, inner, *reset_rims, outer, update, partial, pairs)


def shards(
    left_feats, right_feats, prev_hidden, warp_list, enc_weight, hgate_w, hcand_w, vgate_w, vcand_w
):
    rows = prev_hidden.shape[1]
    half = vgate_w.shape[0] // 2
    outer_rows = (*range(half), *range(rows - half, rows))
    inner_rows = tuple(range(half, rows - half))
    right = lax.axis_index("cols")
    below = 1 - lax.axis_index("rows") % 2
    place = jnp.stack([right, below]).astype(jnp.int32)
    swap_cols = lambda value: lax.ppermute(value, "cols", [(0, 1), (1, 0)])
    swap_rows = lambda near, far: (swap_near(near, "rows"), swap_far(far, "rows"))
    pinned = lax.optimization_barrier

    warp_list = jnp.transpose(warp_list, (0, 2, 3, 1))
    edge = lax.ppermute(right_feats, "cols", [(0, 1)])
    lists = swap_rows(warp_list, warp_list)
    low = motion_of(0, rows // 2, left_feats, right_feats, edge, enc_weight)
    pairs = pairs_of(vcand_w)
    lists, low, pairs = pinned((lists, low, pairs))
    blocks = gather_blocks(place, *lists, prev_hidden)
    edge, blocks = pinned((edge, blocks))
    near, far = swap_rows(*blocks)
    high = motion_of(rows // 2, rows // 2, left_feats, right_feats, edge, enc_weight)
    high, edges = pinned((high, edges_of(place, low, high, half)))
    motion_rims = swap_rows(*edges)
    seam = seam_of(place, warp_list, prev_hidden, near, far, low, high)
    near, seam = pinned((near, seam))
    warped = warp_of(place, warp_list, prev_hidden, near, far)
    seam = swap_cols(seam)
    outer, *edges = horizontal_pass(
        outer_rows, True, place, warped, low, high, seam, hgate_w, hcand_w
    )
    warped, edges = pinned((warped, edges))
    hidden_rims = swap_rows(*edges)
    (inner,) = horizontal_pass(
        inner_rows, False, place, warped, low, high, seam, hgate_w, hcand_w
    )
    update_inner, reset_inner, partial = inner_gates(outer, inner, low, high, vgate_w)
    update_outer, reset_outer, *edges = outer_gates(
        place, outer, partial, hidden_rims + motion_rims, vgate_w
    )
    reset_inner, edges = pinned((reset_inner, edges))
    reset_rims = swap_rows(*edges)
    inner, partial = inner_states(
        place, (reset_outer, reset_inner), low, high, motion_rims, inner, update_inner, pairs
    )
    return final_states(place, inner, reset_rims, outer, update_outer, partial, pairs)


def solution(mesh):
    spread = P(("groups", "cams"), "rows", "cols", None)
    return jax.shard_map(
        shards,
        mesh=mesh,
        in_specs=(spread,) * 4 + (P(),) * 5,
        out_specs=spread,
        check_vma=False,
    )
```

```python
import functools

import jax
import jax.numpy as jnp
from jax import lax
from jax.experimental import pallas as pl
from jax.experimental.pallas import tpu as pltpu
from jax.sharding import PartitionSpec as P

bf16 = jnp.bfloat16
f32 = jnp.float32
SEAM = 16


def dotf(a, b):
    return jnp.dot(a, b, preferred_element_type=f32)


def sigmoid(v):
    return 0.5 * jnp.tanh(0.5 * v) + 0.5


def state_rows(*pieces):
    return [(piece, r) for piece in pieces for r in range(piece.shape[0])]


def swap_near(value, axis):
    count = lax.axis_size(axis)
    pairs = [(i, i ^ 1) for i in range(count) if i ^ 1 < count]
    return lax.ppermute(value, axis, pairs)


def swap_far(value, axis):
    count = lax.axis_size(axis)
    pairs = []
    for i in range(1, count - 1, 2):
        pairs += [(i, i + 1), (i + 1, i)]
    return lax.ppermute(value, axis, pairs)


IN_VMEM = pl.BlockSpec(memory_space=pltpu.VMEM)
IN_SMEM = pl.BlockSpec(memory_space=pltpu.SMEM)
IN_HBM = pl.BlockSpec(memory_space=pltpu.HBM)


def right_half():
    return lax.axis_index("cols")


def near_below():
    return 1 - lax.axis_index("rows") % 2


def in_hbm(value):
    return pltpu.with_memory_space_constraint(value, pltpu.HBM)


def params(megabytes):
    return pltpu.CompilerParams(vmem_limit_bytes=megabytes << 20)


def motion_kernel(
    first, left_feats, right_feats, edge_ref, weight, out_ref, left_ref, window,
    weight_ref, sems,
):
    disparities = weight_ref.shape[0]
    rows, width, feats = left_ref.shape
    tile = 128
    own = pl.ds(first, rows)
    loads = [
        pltpu.make_async_copy(left_feats.at[0, own], left_ref, sems.at[0]),
        pltpu.make_async_copy(
            right_feats.at[0, own], window.at[:, pl.ds(disparities, width), :], sems.at[1]
        ),
        pltpu.make_async_copy(weight, weight_ref, sems.at[2]),
    ]
    for load in loads:
        load.start()
    far_edge = edge_ref.shape[2] - disparities
    for r in range(rows):
        other = edge_ref[0, first + r, pl.ds(far_edge, disparities), :]
        window[r, pl.ds(0, disparities), :] = jnp.where(
            right_half() == 1, other, jnp.zeros_like(other)
        )
    scale = feats**-0.5
    lane = lax.broadcasted_iota(jnp.int32, (tile, tile), 1)
    row = lax.broadcasted_iota(jnp.int32, (tile, tile), 0)
    keep = lane < row
    flip = (lane + row == tile - 1).astype(f32).astype(bf16)
    for load in loads:
        load.wait()
    turned = jnp.concatenate(
        [
            dotf(flip, weight_ref[pl.ds(disparities - tile, tile), :]).astype(bf16),
            dotf(flip, weight_ref[pl.ds(0, tile), :]).astype(bf16)[2 * tile - disparities :, :],
        ],
        axis=0,
    )
    span = disparities + tile
    blocks = -(-span // tile)
    tiles = [(r, t * tile) for r in range(rows) for t in range(width // tile)]
    flipped = [dotf(flip, left_ref[r, pl.ds(x, tile), :]).astype(bf16) for r, x in tiles]
    scores = [
        lax.dot_general(
            part,
            window[r, pl.ds(x, blocks * tile), :],
            (((1,), (1,)), ((), ())),
            preferred_element_type=f32,
        )
        * scale
        for part, (r, x) in zip(flipped, tiles)
    ]
    skewed = []
    for score in scores:
        rolled = [
            pltpu.roll(score[:, tile * j : tile * (j + 1)], 0, 1, stride=1, stride_axis=0)
            for j in range(blocks)
        ]
        lanes = [jnp.where(keep, rolled[j], rolled[j + 1]).astype(bf16) for j in range(blocks - 1)]
        skewed.append(jnp.concatenate(lanes, axis=1)[:, :disparities])
    motions = [dotf(part, turned).astype(bf16) for part in skewed]
    for part, (r, x) in zip(motions, tiles):
        out_ref[r, pl.ds(x, tile), :] = dotf(flip, part).astype(bf16)


def motion_of(first, rows, left, right, edge, weight):
    width, feats = left.shape[2:]
    return pl.pallas_call(
        functools.partial(motion_kernel, first),
        in_specs=[IN_HBM, IN_HBM, IN_VMEM, IN_HBM],
        out_specs=IN_VMEM,
        out_shape=jax.ShapeDtypeStruct((rows, width, weight.shape[1]), bf16),
        scratch_shapes=[
            pltpu.VMEM((rows, width, feats), bf16),
            pltpu.VMEM((rows, width + 256, feats), bf16),
            pltpu.VMEM(weight.shape, bf16),
            pltpu.SemaphoreType.DMA((3,)),
        ],
        compiler_params=params(16),
        name="motion",
    )(in_hbm(left), in_hbm(right), edge, in_hbm(weight))


def edges_kernel(low_ref, high_ref, near_ref, far_ref):
    count = near_ref.shape[0]
    low, high = low_ref[pl.ds(0, count)], high_ref[pl.ds(high_ref.shape[0] - count, count)]
    below = near_below() == 1
    near_ref[...] = jnp.where(below, high, low)
    far_ref[...] = jnp.where(below, low, high)


def edges_of(low, high, count):
    shape = jax.ShapeDtypeStruct((count,) + low.shape[1:], bf16)
    return pl.pallas_call(
        edges_kernel,
        in_specs=[IN_VMEM, IN_VMEM],
        out_specs=[IN_VMEM, IN_VMEM],
        out_shape=[shape, shape],
        compiler_params=params(4),
        name="edges",
    )(low, high)


def gather_kernel(near_list, far_list, prev_ref, near_out, far_out, sems):
    _, band_blocks, _, band_rows = near_list.shape
    slots, width, _ = near_out.shape
    sign = 2 * near_below() - 1
    lane = lax.broadcasted_iota(jnp.int32, (1, band_rows), 1)
    copies = []
    sides = ((near_list, near_out, sign), (far_list, far_out, -sign))
    for side, (list_ref, out, wanted) in enumerate(sides):
        before = jnp.zeros((1, 1), jnp.int32)
        ranks, asked = [], []
        for block in range(band_blocks):
            field = lambda k: list_ref[0, block, pl.ds(k, 1), :]
            hit = (field(0) == wanted).astype(jnp.int32)
            rank = jnp.broadcast_to(before, (1, band_rows))
            for r in range(band_rows - 1):
                rank = rank + jnp.where(lane > r, hit[:, r : r + 1], 0)
            ranks.append(jnp.where(hit > 0, rank, -1))
            asked.append(field(1) * band_blocks + field(2))
            before = before + jnp.sum(hit, axis=1, keepdims=True)
        for slot in range(slots):
            found = sum(
                jnp.where(rank == slot, source, 0) for rank, source in zip(ranks, asked)
            )
            source = jnp.sum(found)
            row = source // band_blocks
            column = pl.multiple_of(source % band_blocks * width, width)
            block = prev_ref.at[0, row, pl.ds(column, width), :]
            copies.append(pltpu.make_async_copy(block, out.at[slot], sems.at[side, slot]))
            copies[-1].start()
    for copy in copies:
        copy.wait()


def gather_blocks(near_list, far_list, prev):
    _, band_blocks, _, band_rows = near_list.shape
    _, _, width, hidden = prev.shape
    slots = band_rows * band_blocks // 4
    shape = jax.ShapeDtypeStruct((slots, width // band_blocks, hidden), bf16)
    return pl.pallas_call(
        gather_kernel,
        in_specs=[IN_VMEM, IN_VMEM, IN_HBM],
        out_specs=[IN_VMEM, IN_VMEM],
        out_shape=[shape, shape],
        scratch_shapes=[pltpu.SemaphoreType.DMA((2, slots))],
        compiler_params=params(4),
        name="gather",
    )(near_list, far_list, in_hbm(prev))


def pick_blocks(list_ref, rows, blocks, visit):
    last = rows * blocks // 4 - 1
    sign = 2 * near_below() - 1
    nears, fars = jnp.int32(0), jnp.int32(0)
    for block in range(blocks):
        for row in range(rows):
            field = lambda k: list_ref[(block * 4 + k) * rows + row]
            offset = field(0)
            is_near, is_far = offset == -sign, offset == sign
            visit(
                row, block, field, is_near, is_far, jnp.minimum(nears, last),
                jnp.minimum(fars, last),
            )
            nears += is_near.astype(jnp.int32)
            fars += is_far.astype(jnp.int32)


def seam_kernel(list_ref, prev_ref, near_ref, far_ref, low_ref, high_ref, seam_ref):
    width, ch = near_ref.shape[1:]
    rows, total = prev_ref.shape[1:3]
    band_blocks = total // width
    is_left = right_half() == 0
    start = pl.multiple_of((width - SEAM) * (1 - right_half()), SEAM)
    inside = pl.ds(start, SEAM)

    def visit(row, block, field, is_near, is_far, near_slot, far_slot):
        if block in (0, band_blocks - 1):
            source = pl.multiple_of(field(2) * width + start, SEAM)
            local = prev_ref[0, field(1), pl.ds(source, SEAM), :]
            near, far = near_ref[near_slot, inside, :], far_ref[far_slot, inside, :]
            picked = jnp.where(is_near, near, jnp.where(is_far, far, local))
            picked = jnp.where(field(3) > 0, picked, jnp.zeros_like(picked))
            if block > 0:
                picked = jnp.where(is_left, picked, seam_ref[row, :, 0:ch])
            seam_ref[row, :, 0:ch] = picked

    pick_blocks(list_ref, rows, band_blocks, visit)
    edge = pl.multiple_of((band_blocks * width - SEAM) * (1 - right_half()), SEAM)
    half = low_ref.shape[0]
    seam_ref[pl.ds(0, half), :, ch : 2 * ch] = low_ref[:, pl.ds(edge, SEAM), :]
    seam_ref[pl.ds(half, half), :, ch : 2 * ch] = high_ref[:, pl.ds(edge, SEAM), :]


def seam_of(warp_list, prev, near, far, low, high):
    _, rows, _, ch = prev.shape
    return pl.pallas_call(
        seam_kernel,
        in_specs=[IN_SMEM] + [IN_VMEM] * 5,
        out_specs=IN_VMEM,
        out_shape=jax.ShapeDtypeStruct((rows, SEAM, 2 * ch), bf16),
        compiler_params=params(4),
        name="seam",
    )(warp_list, prev, near, far, low, high)


def warp_kernel(list_ref, prev_ref, near_ref, far_ref, out_ref):
    width = near_ref.shape[1]

    def visit(row, block, field, is_near, is_far, near_slot, far_slot):
        column = pl.multiple_of(field(2) * width, width)
        local = prev_ref[0, field(1), pl.ds(column, width), :]
        picked = jnp.where(
            is_near, near_ref[near_slot], jnp.where(is_far, far_ref[far_slot], local)
        )
        picked = jnp.where(field(3) > 0, picked, jnp.zeros_like(picked))
        out_ref[row, pl.ds(block * width, width), :] = picked

    rows, total = prev_ref.shape[1:3]
    pick_blocks(list_ref, rows, total // width, visit)


def warp_of(warp_list, prev, near, far):
    return pl.pallas_call(
        warp_kernel,
        in_specs=[IN_SMEM] + [IN_VMEM] * 3,
        out_specs=IN_VMEM,
        out_shape=jax.ShapeDtypeStruct(prev.shape[1:], bf16),
        compiler_params=params(4),
        name="warp",
    )(warp_list, prev, near, far)


def horizontal_kernel(
    rows, hidden_ref, low_ref, high_ref, seam_ref, gates_ref, cand_ref, out_ref, *rest
):
    *edges, joined, reset, partial = rest
    _, width, ch = hidden_ref.shape
    taps = gates_ref.shape[0]
    half = taps // 2
    right = right_half()
    pad = SEAM
    own = pl.multiple_of(pad + pad * right, pad)
    seam = pl.multiple_of(pad + width * (1 - right), pad)
    span = width + SEAM
    flow = state_rows(low_ref, high_ref)
    gates = gates_ref[...].reshape(taps * 2 * ch, 2 * ch)
    count = range(len(rows))
    for r in count:
        piece, at = flow[rows[r]]
        for edge in (0, span + pad):
            joined[r, pl.ds(edge, pad), :] = jnp.zeros((pad, 2 * ch), bf16)
            reset[r, pl.ds(edge, pad), :] = jnp.zeros((pad, ch), bf16)
        joined[r, pl.ds(own, width), 0:ch] = hidden_ref[rows[r]]
        joined[r, pl.ds(own, width), ch : 2 * ch] = piece[at]
        joined[r, pl.ds(seam, SEAM), :] = seam_ref[rows[r]]
    sums = [
        dotf(
            jnp.concatenate(
                [joined[r, pl.ds(pad - half + t, span), :] for t in range(taps)], axis=1
            ),
            gates,
        )
        for r in count
    ]
    update = []
    for r in count:
        update.append(sigmoid(sums[r][:, :ch]))
        current = joined[r, pl.ds(pad, span), 0:ch].astype(f32)
        reset[r, pl.ds(pad, span), :] = (sigmoid(sums[r][:, ch:]) * current).astype(bf16)
    for r in count:
        both = jnp.concatenate([reset[r], joined[r, :, ch : 2 * ch]], axis=1)
        for t in range(0, taps, 2):
            pair = jnp.concatenate([cand_ref[k] for k in range(t, min(t + 2, taps))], axis=1)
            partial[r, :, pl.ds(t * ch, pair.shape[1])] = dotf(both, pair)
    totals = []
    for r in count:
        total = None
        for t in range(taps):
            part = partial[r, pl.ds(pad - half + t, span), pl.ds(t * ch, ch)]
            total = part if total is None else total + part
        totals.append(total)
    for r in count:
        current = joined[r, pl.ds(pad, span), 0:ch].astype(f32)
        cand = jnp.tanh(totals[r])
        blended = (1.0 - update[r]) * current + update[r] * cand
        reset[r, pl.ds(pad, span), :] = blended.astype(bf16)
    for r in count:
        out_ref[r] = reset[r, pl.ds(own, width), :]
    if edges:
        near_ref, far_ref = edges
        near_ref[...] = out_ref[pl.ds(half * near_below(), half)]
        far_ref[...] = out_ref[pl.ds(half - half * near_below(), half)]


def horizontal_pass(rows, send, hidden, low, high, seam, gates, cand):
    _, width, ch = hidden.shape
    taps = gates.shape[0]
    length = width + SEAM + 2 * SEAM
    shape = lambda count: jax.ShapeDtypeStruct((count, width, ch), bf16)
    shapes = [shape(len(rows))] + [shape(taps // 2)] * (2 if send else 0)
    return pl.pallas_call(
        functools.partial(horizontal_kernel, rows),
        in_specs=[IN_VMEM] * 6,
        out_specs=[IN_VMEM] * len(shapes),
        out_shape=shapes,
        scratch_shapes=[
            pltpu.VMEM((len(rows), length, 2 * ch), bf16),
            pltpu.VMEM((len(rows), length, ch), bf16),
            pltpu.VMEM((len(rows), length, taps * ch), f32),
        ],
        compiler_params=params(24),
        name="horizontal",
    )(hidden, low, high, seam, gates, cand)


def pairs_kernel(cand_ref, out_ref):
    taps, depth, ch = cand_ref.shape
    for j in range(taps + 1):
        none = jnp.zeros((depth, ch), bf16)
        out_ref[j, :, 0:ch] = cand_ref[j] if j < taps else none
        out_ref[j, :, ch : 2 * ch] = cand_ref[j - 1] if j > 0 else none


def pairs_of(cand):
    taps, depth, ch = cand.shape
    return pl.pallas_call(
        pairs_kernel,
        in_specs=[IN_VMEM],
        out_specs=IN_VMEM,
        out_shape=jax.ShapeDtypeStruct((taps + 1, depth, 2 * ch), bf16),
        compiler_params=params(4),
        name="pairs",
    )(cand)


def banded(outer_ref, inner_ref, half):
    outer = state_rows(outer_ref)
    return outer[:half] + state_rows(inner_ref) + outer[half:]


def stack(sources, rows):
    return jnp.concatenate(
        [piece[at] for y in rows for piece, at in (source[y] for source in sources)], axis=1
    )


def gates_kernel(
    outer_ref, inner_ref, low_ref, high_ref, gates_ref, update_ref, reset_ref, partial_ref
):
    taps, depth, wide = gates_ref.shape
    ch = wide // 2
    half = taps // 2
    state = banded(outer_ref, inner_ref, half)
    sources = (state, state_rows(low_ref, high_ref))
    rows = len(state)
    inner = range(half, rows - half)
    weights = lambda first, last: gates_ref[pl.ds(first, last - first)].reshape(-1, wide)
    sums = [dotf(stack(sources, range(y - half, y + half + 1)), weights(0, taps)) for y in inner]
    for i, y in enumerate([*range(half), *range(rows - half, rows)]):
        first, last = max(y - half, 0), min(y + half + 1, rows)
        partial_ref[i] = dotf(
            stack(sources, range(first, last)), weights(first - y + half, last - y + half)
        )
    for i, y in enumerate(inner):
        piece, at = state[y]
        update_ref[i] = sigmoid(sums[i][:, :ch])
        reset_ref[i] = (sigmoid(sums[i][:, ch:]) * piece[at].astype(f32)).astype(bf16)


def inner_gates(outer, inner, low, high, gates):
    count, width, ch = inner.shape
    half = gates.shape[0] // 2
    return pl.pallas_call(
        gates_kernel,
        in_specs=[IN_VMEM] * 5,
        out_specs=[IN_VMEM] * 3,
        out_shape=[
            jax.ShapeDtypeStruct((count, width, ch), f32),
            jax.ShapeDtypeStruct((count, width, ch), bf16),
            jax.ShapeDtypeStruct((2 * half, width, 2 * ch), f32),
        ],
        compiler_params=params(24),
        name="inner_gates",
    )(outer, inner, low, high, gates)


def outer_kernel(
    outer_ref, partial_ref, hidden_near, hidden_far, motion_near, motion_far, gates_ref,
    update_ref, reset_ref, near_ref, far_ref, hidden_rim, motion_rim,
):
    taps, _, wide = gates_ref.shape
    ch = wide // 2
    half = taps // 2
    near = half * near_below()
    far = half - near
    hidden_rim[pl.ds(near, half)] = hidden_near[...]
    hidden_rim[pl.ds(far, half)] = hidden_far[...]
    motion_rim[pl.ds(near, half)] = motion_near[...]
    motion_rim[pl.ds(far, half)] = motion_far[...]
    sources = (state_rows(hidden_rim), state_rows(motion_rim))
    weights = lambda first, last: gates_ref[pl.ds(first, last - first)].reshape(-1, wide)
    sums = []
    for i in range(half):
        sums.append(dotf(stack(sources, range(i, half)), weights(0, half - i)))
    for i in range(half):
        sums.append(dotf(stack(sources, range(half, half + i + 1)), weights(taps - 1 - i, taps)))
    for i in range(2 * half):
        total = sums[i] + partial_ref[i]
        update_ref[i] = sigmoid(total[:, :ch])
        reset_ref[i] = (sigmoid(total[:, ch:]) * outer_ref[i].astype(f32)).astype(bf16)
    near_ref[...] = reset_ref[pl.ds(near, half)]
    far_ref[...] = reset_ref[pl.ds(far, half)]


def outer_gates(outer, partial, rims, gates):
    count, width, ch = outer.shape
    half = gates.shape[0] // 2
    shape = lambda n, kind: jax.ShapeDtypeStruct((n, width, ch), kind)
    return pl.pallas_call(
        outer_kernel,
        in_specs=[IN_VMEM] * 7,
        out_specs=[IN_VMEM] * 4,
        out_shape=[shape(count, f32), shape(count, bf16), shape(half, bf16), shape(half, bf16)],
        scratch_shapes=[pltpu.VMEM((2 * half, width, ch), bf16)] * 2,
        compiler_params=params(16),
        name="outer_gates",
    )(outer, partial, *rims, gates)


def blend(state, update, total):
    return ((1.0 - update) * state.astype(f32) + update * jnp.tanh(total)).astype(bf16)


def cand_kernel(
    reset_outer, reset_inner, low_ref, high_ref, motion_near, motion_far, inner_ref,
    update_ref, pairs_ref, out_ref, partial_ref, motion_rim,
):
    blocks, depth, wide = pairs_ref.shape
    ch = wide // 2
    half = (blocks - 1) // 2
    near = half * near_below()
    motion_rim[pl.ds(near, half)] = motion_near[...]
    motion_rim[pl.ds(half - near, half)] = motion_far[...]
    reset = banded(reset_outer, reset_inner, half)
    sources = (reset, state_rows(low_ref, high_ref))
    rows = len(reset)
    weights = lambda first, last: pairs_ref[pl.ds(first, last - first)].reshape(-1, wide)
    sums = {}
    for y in range(half, rows - half, 2):
        rows_read = range(y - half, y + half + 2)
        sums[y] = dotf(stack(sources, rows_read), weights(0, blocks))
    rim = state_rows(motion_rim)
    flow_weights = lambda first, last: pairs_ref[pl.ds(first, last - first), ch:, :].reshape(
        -1, wide
    )
    for i, y in enumerate((0, rows - half)):
        first, last = max(y - half, 0), min(y + half + 2, rows)
        total = dotf(stack(sources, range(first, last)), weights(first - y + half, last - y + half))
        at = (0, half) if i == 0 else (blocks - half, blocks)
        total += dotf(stack((rim,), range(half * i, half * i + half)), flow_weights(*at))
        partial_ref[2 * i], partial_ref[2 * i + 1] = total[:, :ch], total[:, ch:]
    for y in range(half, rows - half, 2):
        for k in range(2):
            i = y - half + k
            total = sums[y][:, k * ch : (k + 1) * ch]
            out_ref[i] = blend(inner_ref[i], update_ref[i], total)


def inner_states(resets, low, high, motion_rims, inner, update, pairs):
    count, width, ch = inner.shape
    half = (pairs.shape[0] - 1) // 2
    return pl.pallas_call(
        cand_kernel,
        in_specs=[IN_VMEM] * 9,
        out_specs=[IN_VMEM] * 2,
        out_shape=[
            jax.ShapeDtypeStruct((count, width, ch), bf16),
            jax.ShapeDtypeStruct((2 * half, width, ch), f32),
        ],
        scratch_shapes=[pltpu.VMEM((2 * half, width, ch), bf16)],
        compiler_params=params(16),
        name="inner_states",
    )(*resets, low, high, *motion_rims, inner, update, pairs)


def final_kernel(
    inner_ref, reset_near, reset_far, outer_ref, update_ref, partial_ref, pairs_ref,
    out_ref, reset_rim, done, sems,
):
    blocks, _, wide = pairs_ref.shape
    ch = wide // 2
    half = (blocks - 1) // 2
    rows = out_ref.shape[1]
    count = inner_ref.shape[0]
    stores = [pltpu.make_async_copy(inner_ref, out_ref.at[0, pl.ds(half, count)], sems.at[0])]
    stores[0].start()
    near = half * near_below()
    reset_rim[pl.ds(near, half)] = reset_near[...]
    reset_rim[pl.ds(half - near, half)] = reset_far[...]
    rim = state_rows(reset_rim)
    sums = []
    for i in range(2):
        first = 0 if i == 0 else blocks - half
        weights = pairs_ref[pl.ds(first, half), :ch, :].reshape(-1, wide)
        sums.append(dotf(stack((rim,), range(half * i, half * i + half)), weights))
    for i in range(2):
        for k in range(2):
            at = 2 * i + k
            total = partial_ref[at] + sums[i][:, k * ch : (k + 1) * ch]
            done[at] = blend(outer_ref[at], update_ref[at], total)
        target = out_ref.at[0, pl.ds(0 if i == 0 else rows - half, half)]
        stores.append(pltpu.make_async_copy(done.at[pl.ds(half * i, half)], target, sems.at[i + 1]))
        stores[-1].start()
    for store in stores:
        store.wait()


def final_states(inner, reset_rims, outer, update, partial, pairs):
    count, width, ch = outer.shape
    rows = count + inner.shape[0]
    return pl.pallas_call(
        final_kernel,
        in_specs=[IN_VMEM] * 7,
        out_specs=IN_HBM,
        out_shape=jax.ShapeDtypeStruct((1, rows, width, ch), bf16),
        scratch_shapes=[pltpu.VMEM((count, width, ch), bf16)] * 2 + [pltpu.SemaphoreType.DMA((3,))],
        compiler_params=params(16),
        name="final_states",
    )(inner, *reset_rims, outer, update, partial, pairs)


def shards(
    left_feats, right_feats, prev_hidden, warp_list, enc_weight, hgate_w, hcand_w, vgate_w, vcand_w
):
    rows = prev_hidden.shape[1]
    half = vgate_w.shape[0] // 2
    outer_rows = (*range(half), *range(rows - half, rows))
    inner_rows = tuple(range(half, rows - half))
    swap_cols = lambda value: lax.ppermute(value, "cols", [(0, 1), (1, 0)])
    swap_rows = lambda near, far: (swap_near(near, "rows"), swap_far(far, "rows"))
    pinned = lax.optimization_barrier

    warp_list = jnp.transpose(warp_list, (0, 2, 3, 1))
    flat_list = warp_list.reshape(-1)
    lists = swap_rows(warp_list, warp_list)
    edge = swap_cols(right_feats)
    low = motion_of(0, rows // 2, left_feats, right_feats, edge, enc_weight)
    lists, low = pinned((lists, low))
    blocks = gather_blocks(*lists, prev_hidden)
    edge, blocks = pinned((edge, blocks))
    near, far = swap_rows(*blocks)
    high = motion_of(rows // 2, rows // 2, left_feats, right_feats, edge, enc_weight)
    pairs = pairs_of(vcand_w)
    high, edges, pairs = pinned((high, edges_of(low, high, half), pairs))
    motion_rims = swap_rows(*edges)
    seam = seam_of(flat_list, prev_hidden, near, far, low, high)
    near, seam = pinned((near, seam))
    warped = warp_of(flat_list, prev_hidden, near, far)
    seam = swap_cols(seam)
    outer, *edges = horizontal_pass(
        outer_rows, True, warped, low, high, seam, hgate_w, hcand_w
    )
    warped, edges = pinned((warped, edges))
    hidden_rims = swap_rows(*edges)
    (inner,) = horizontal_pass(
        inner_rows, False, warped, low, high, seam, hgate_w, hcand_w
    )
    update_inner, reset_inner, partial = inner_gates(outer, inner, low, high, vgate_w)
    update_outer, reset_outer, *edges = outer_gates(
        outer, partial, hidden_rims + motion_rims, vgate_w
    )
    reset_inner, edges = pinned((reset_inner, edges))
    reset_rims = swap_rows(*edges)
    inner, partial = inner_states(
        (reset_outer, reset_inner), low, high, motion_rims, inner, update_inner, pairs
    )
    return final_states(inner, reset_rims, outer, update_outer, partial, pairs)


def solution(mesh):
    spread = P(("groups", "cams"), "rows", "cols", None)
    return jax.shard_map(
        shards,
        mesh=mesh,
        in_specs=(spread,) * 4 + (P(),) * 5,
        out_specs=spread,
        check_vma=False,
    )
```

```python
import functools

import jax
import jax.numpy as jnp
from jax import lax
from jax.experimental import pallas as pl
from jax.experimental.pallas import tpu as pltpu
from jax.sharding import PartitionSpec as P

bf16 = jnp.bfloat16
f32 = jnp.float32
SEAM = 16


def dotf(a, b):
    return jnp.dot(a, b, preferred_element_type=f32)


def sigmoid(v):
    return 0.5 * jnp.tanh(0.5 * v) + 0.5


def state_rows(*pieces):
    return [(piece, r) for piece in pieces for r in range(piece.shape[0])]


def fill_rim(rim_ref, near_ref, far_ref):
    count = near_ref.shape[0]
    near = count * near_below()
    rim_ref[pl.ds(near, count)] = near_ref[...]
    rim_ref[pl.ds(count - near, count)] = far_ref[...]


def swap_near(value, axis):
    count = lax.axis_size(axis)
    pairs = [(i, i ^ 1) for i in range(count) if i ^ 1 < count]
    return lax.ppermute(value, axis, pairs)


def swap_far(value, axis):
    count = lax.axis_size(axis)
    pairs = []
    for i in range(1, count - 1, 2):
        pairs += [(i, i + 1), (i + 1, i)]
    return lax.ppermute(value, axis, pairs)


IN_VMEM = pl.BlockSpec(memory_space=pltpu.VMEM)
IN_SMEM = pl.BlockSpec(memory_space=pltpu.SMEM)
IN_HBM = pl.BlockSpec(memory_space=pltpu.HBM)


def ordered(kernel, inputs, earlier):
    return lambda *refs: kernel(*refs[:inputs], *refs[inputs + len(earlier) :])


def right_half():
    return lax.axis_index("cols")


def near_below():
    return 1 - lax.axis_index("rows") % 2


def in_hbm(value):
    return pltpu.with_memory_space_constraint(value, pltpu.HBM)


def params(megabytes):
    return pltpu.CompilerParams(vmem_limit_bytes=megabytes << 20)


def motion_kernel(
    first, left_feats, right_feats, edge_ref, weight, out_ref, left_ref, window,
    weight_ref, sems,
):
    disparities = weight_ref.shape[0]
    rows, width, feats = left_ref.shape
    tile = 128
    own = pl.ds(first, rows)
    loads = [
        pltpu.make_async_copy(left_feats.at[0, own], left_ref, sems.at[0]),
        pltpu.make_async_copy(
            right_feats.at[0, own], window.at[:, pl.ds(disparities, width), :], sems.at[1]
        ),
        pltpu.make_async_copy(weight, weight_ref, sems.at[2]),
    ]
    for load in loads:
        load.start()
    far_edge = edge_ref.shape[2] - disparities
    for r in range(rows):
        other = edge_ref[0, first + r, pl.ds(far_edge, disparities), :]
        window[r, pl.ds(0, disparities), :] = jnp.where(
            right_half() == 1, other, jnp.zeros_like(other)
        )
    scale = feats**-0.5
    lane = lax.broadcasted_iota(jnp.int32, (tile, tile), 1)
    row = lax.broadcasted_iota(jnp.int32, (tile, tile), 0)
    keep = lane < row
    flip = (lane + row == tile - 1).astype(f32).astype(bf16)
    for load in loads:
        load.wait()
    turned = jnp.concatenate(
        [
            dotf(flip, weight_ref[pl.ds(disparities - tile, tile), :]).astype(bf16),
            dotf(flip, weight_ref[pl.ds(0, tile), :]).astype(bf16)[2 * tile - disparities :, :],
        ],
        axis=0,
    )
    span = disparities + tile
    blocks = -(-span // tile)
    tiles = [(r, t * tile) for r in range(rows) for t in range(width // tile)]
    flipped = [dotf(flip, left_ref[r, pl.ds(x, tile), :]).astype(bf16) for r, x in tiles]
    scores = [
        lax.dot_general(
            part,
            window[r, pl.ds(x, blocks * tile), :],
            (((1,), (1,)), ((), ())),
            preferred_element_type=f32,
        )
        * scale
        for part, (r, x) in zip(flipped, tiles)
    ]
    skewed = []
    for score in scores:
        rolled = [
            pltpu.roll(score[:, tile * j : tile * (j + 1)], 0, 1, stride=1, stride_axis=0)
            for j in range(blocks)
        ]
        lanes = [jnp.where(keep, rolled[j], rolled[j + 1]).astype(bf16) for j in range(blocks - 1)]
        skewed.append(jnp.concatenate(lanes, axis=1)[:, :disparities])
    motions = [dotf(part, turned).astype(bf16) for part in skewed]
    for part, (r, x) in zip(motions, tiles):
        out_ref[r, pl.ds(x, tile), :] = dotf(flip, part).astype(bf16)


def motion_of(first, rows, left, right, edge, weight, *earlier):
    width, feats = left.shape[2:]
    return pl.pallas_call(
        ordered(functools.partial(motion_kernel, first), 4, earlier),
        in_specs=[IN_HBM, IN_HBM, IN_VMEM, IN_HBM] + [IN_VMEM] * len(earlier),
        out_specs=IN_VMEM,
        out_shape=jax.ShapeDtypeStruct((rows, width, weight.shape[1]), bf16),
        scratch_shapes=[
            pltpu.VMEM((rows, width, feats), bf16),
            pltpu.VMEM((rows, width + 256, feats), bf16),
            pltpu.VMEM(weight.shape, bf16),
            pltpu.SemaphoreType.DMA((3,)),
        ],
        compiler_params=params(4),
        name="motion",
    )(in_hbm(left), in_hbm(right), edge, in_hbm(weight), *earlier)


def edges_kernel(low_ref, high_ref, near_ref, far_ref):
    count = near_ref.shape[0]
    low, high = low_ref[pl.ds(0, count)], high_ref[pl.ds(high_ref.shape[0] - count, count)]
    below = near_below() == 1
    near_ref[...] = jnp.where(below, high, low)
    far_ref[...] = jnp.where(below, low, high)


def edges_of(low, high, count):
    shape = jax.ShapeDtypeStruct((count,) + low.shape[1:], bf16)
    return pl.pallas_call(
        edges_kernel,
        in_specs=[IN_VMEM] * 2,
        out_specs=[IN_VMEM, IN_VMEM],
        out_shape=[shape, shape],
        compiler_params=params(4),
        name="edges",
    )(low, high)


def held_until(values, *earlier):
    anywhere = pl.BlockSpec(memory_space=pl.ANY)
    count = len(values)
    return pl.pallas_call(
        lambda *refs: None,
        in_specs=[anywhere] * count + [IN_VMEM] * len(earlier),
        out_specs=[anywhere] * count,
        out_shape=[jax.ShapeDtypeStruct(value.shape, value.dtype) for value in values],
        input_output_aliases={i: i for i in range(count)},
        compiler_params=params(4),
        name="held",
    )(*values, *earlier)


def gather_kernel(near_list, far_list, prev_ref, near_out, far_out, sems):
    _, band_blocks, _, band_rows = near_list.shape
    slots, width, _ = near_out.shape
    sign = 2 * near_below() - 1
    lane = lax.broadcasted_iota(jnp.int32, (1, band_rows), 1)
    copies = []
    sides = ((near_list, near_out, sign), (far_list, far_out, -sign))
    for side, (list_ref, out, wanted) in enumerate(sides):
        before = jnp.zeros((1, 1), jnp.int32)
        ranks, asked = [], []
        for block in range(band_blocks):
            field = lambda k: list_ref[0, block, pl.ds(k, 1), :]
            hit = (field(0) == wanted).astype(jnp.int32)
            rank = jnp.broadcast_to(before, (1, band_rows))
            for r in range(band_rows - 1):
                rank = rank + jnp.where(lane > r, hit[:, r : r + 1], 0)
            ranks.append(jnp.where(hit > 0, rank, -1))
            asked.append(field(1) * band_blocks + field(2))
            before = before + jnp.sum(hit, axis=1, keepdims=True)
        for slot in range(slots):
            found = sum(
                jnp.where(rank == slot, source, 0) for rank, source in zip(ranks, asked)
            )
            source = jnp.sum(found)
            row = source // band_blocks
            column = pl.multiple_of(source % band_blocks * width, width)
            block = prev_ref.at[0, row, pl.ds(column, width), :]
            copies.append(pltpu.make_async_copy(block, out.at[slot], sems.at[side, slot]))
            copies[-1].start()
    for copy in copies:
        copy.wait()


def gather_blocks(near_list, far_list, prev, *earlier):
    _, band_blocks, _, band_rows = near_list.shape
    _, _, width, hidden = prev.shape
    slots = band_rows * band_blocks // 4
    shape = jax.ShapeDtypeStruct((slots, width // band_blocks, hidden), bf16)
    return pl.pallas_call(
        ordered(gather_kernel, 3, earlier),
        in_specs=[IN_VMEM, IN_VMEM, IN_HBM] + [IN_VMEM] * len(earlier),
        out_specs=[IN_VMEM, IN_VMEM],
        out_shape=[shape, shape],
        scratch_shapes=[pltpu.SemaphoreType.DMA((2, slots))],
        compiler_params=params(4),
        name="gather",
    )(near_list, far_list, in_hbm(prev), *earlier)


def pick_blocks(list_ref, rows, blocks, visit):
    last = rows * blocks // 4 - 1
    sign = 2 * near_below() - 1
    nears, fars = jnp.int32(0), jnp.int32(0)
    for block in range(blocks):
        for row in range(rows):
            field = lambda k: list_ref[0, block, k, row]
            offset = field(0)
            is_near, is_far = offset == -sign, offset == sign
            visit(
                row, block, field, is_near, is_far, jnp.minimum(nears, last),
                jnp.minimum(fars, last),
            )
            nears += is_near.astype(jnp.int32)
            fars += is_far.astype(jnp.int32)


def seam_kernel(list_ref, prev_ref, near_ref, far_ref, low_ref, high_ref, seam_ref):
    width, ch = near_ref.shape[1:]
    rows, total = prev_ref.shape[1:3]
    band_blocks = total // width
    is_left = right_half() == 0
    start = pl.multiple_of((width - SEAM) * (1 - right_half()), SEAM)
    inside = pl.ds(start, SEAM)

    def visit(row, block, field, is_near, is_far, near_slot, far_slot):
        if block in (0, band_blocks - 1):
            source = pl.multiple_of(field(2) * width + start, SEAM)
            local = prev_ref[0, field(1), pl.ds(source, SEAM), :]
            near, far = near_ref[near_slot, inside, :], far_ref[far_slot, inside, :]
            picked = jnp.where(is_near, near, jnp.where(is_far, far, local))
            picked = jnp.where(field(3) > 0, picked, jnp.zeros_like(picked))
            if block > 0:
                picked = jnp.where(is_left, picked, seam_ref[row, :, 0:ch])
            seam_ref[row, :, 0:ch] = picked

    pick_blocks(list_ref, rows, band_blocks, visit)
    edge = pl.multiple_of((band_blocks * width - SEAM) * (1 - right_half()), SEAM)
    half = low_ref.shape[0]
    seam_ref[pl.ds(0, half), :, ch : 2 * ch] = low_ref[:, pl.ds(edge, SEAM), :]
    seam_ref[pl.ds(half, half), :, ch : 2 * ch] = high_ref[:, pl.ds(edge, SEAM), :]


def seam_of(warp_list, prev, near, far, low, high):
    _, rows, _, ch = prev.shape
    return pl.pallas_call(
        seam_kernel,
        in_specs=[IN_SMEM] + [IN_VMEM] * 5,
        out_specs=IN_VMEM,
        out_shape=jax.ShapeDtypeStruct((rows, SEAM, 2 * ch), bf16),
        compiler_params=params(4),
        name="seam",
    )(warp_list, prev, near, far, low, high)


def warp_kernel(list_ref, prev_ref, near_ref, far_ref, out_ref):
    width = near_ref.shape[1]

    def visit(row, block, field, is_near, is_far, near_slot, far_slot):
        column = pl.multiple_of(field(2) * width, width)
        local = prev_ref[0, field(1), pl.ds(column, width), :]
        picked = jnp.where(
            is_near, near_ref[near_slot], jnp.where(is_far, far_ref[far_slot], local)
        )
        picked = jnp.where(field(3) > 0, picked, jnp.zeros_like(picked))
        out_ref[row, pl.ds(block * width, width), :] = picked

    rows, total = prev_ref.shape[1:3]
    pick_blocks(list_ref, rows, total // width, visit)


def warp_of(warp_list, prev, near, far, *earlier):
    return pl.pallas_call(
        ordered(warp_kernel, 4, earlier),
        in_specs=[IN_SMEM] + [IN_VMEM] * (3 + len(earlier)),
        out_specs=IN_VMEM,
        out_shape=jax.ShapeDtypeStruct(prev.shape[1:], bf16),
        compiler_params=params(4),
        name="warp",
    )(warp_list, prev, near, far, *earlier)


def horizontal_kernel(
    rows, hidden_ref, low_ref, high_ref, seam_ref, gates_ref, cand_ref, out_ref, near_ref, far_ref,
    joined, reset, partial,
):
    _, width, ch = hidden_ref.shape
    taps = gates_ref.shape[0]
    half = taps // 2
    right = right_half()
    pad = SEAM
    own = pl.multiple_of(pad + pad * right, pad)
    seam = pl.multiple_of(pad + width * (1 - right), pad)
    span = width + SEAM
    flow = state_rows(low_ref, high_ref)
    gates = gates_ref[...].reshape(taps * 2 * ch, 2 * ch)
    count = range(len(rows))
    for r in count:
        piece, at = flow[rows[r]]
        for edge in (0, span + pad):
            joined[r, pl.ds(edge, pad), :] = jnp.zeros((pad, 2 * ch), bf16)
            reset[r, pl.ds(edge, pad), :] = jnp.zeros((pad, ch), bf16)
        joined[r, pl.ds(own, width), 0:ch] = hidden_ref[rows[r]]
        joined[r, pl.ds(own, width), ch : 2 * ch] = piece[at]
        joined[r, pl.ds(seam, SEAM), :] = seam_ref[rows[r]]
    sums = [
        dotf(
            jnp.concatenate(
                [joined[r, pl.ds(pad - half + t, span), :] for t in range(taps)], axis=1
            ),
            gates,
        )
        for r in count
    ]
    update = []
    for r in count:
        update.append(sigmoid(sums[r][:, :ch]))
        current = joined[r, pl.ds(pad, span), 0:ch].astype(f32)
        reset[r, pl.ds(pad, span), :] = (sigmoid(sums[r][:, ch:]) * current).astype(bf16)
    for r in count:
        both = jnp.concatenate([reset[r], joined[r, :, ch : 2 * ch]], axis=1)
        for t in range(0, taps, 2):
            pair = jnp.concatenate([cand_ref[k] for k in range(t, min(t + 2, taps))], axis=1)
            partial[r, :, pl.ds(t * ch, pair.shape[1])] = dotf(both, pair)
    totals = []
    for r in count:
        total = None
        for t in range(taps):
            part = partial[r, pl.ds(pad - half + t, span), pl.ds(t * ch, ch)]
            total = part if total is None else total + part
        totals.append(total)
    for r in count:
        current = joined[r, pl.ds(pad, span), 0:ch].astype(f32)
        cand = jnp.tanh(totals[r])
        blended = (1.0 - update[r]) * current + update[r] * cand
        reset[r, pl.ds(pad, span), :] = blended.astype(bf16)
    for r in count:
        out_ref[r] = reset[r, pl.ds(own, width), :]
    near_ref[...] = out_ref[pl.ds(half * near_below(), half)]
    far_ref[...] = out_ref[pl.ds(half - half * near_below(), half)]


def horizontal_pass(rows, hidden, low, high, seam, gates, cand, *earlier):
    _, width, ch = hidden.shape
    taps = gates.shape[0]
    length = width + SEAM + 2 * SEAM
    shape = lambda count: jax.ShapeDtypeStruct((count, width, ch), bf16)
    shapes = [shape(len(rows))] + [shape(taps // 2)] * 2
    return pl.pallas_call(
        ordered(functools.partial(horizontal_kernel, rows), 6, earlier),
        in_specs=[IN_VMEM] * (6 + len(earlier)),
        out_specs=[IN_VMEM] * len(shapes),
        out_shape=shapes,
        scratch_shapes=[
            pltpu.VMEM((len(rows), length, 2 * ch), bf16),
            pltpu.VMEM((len(rows), length, ch), bf16),
            pltpu.VMEM((len(rows), length, taps * ch), f32),
        ],
        compiler_params=params(11),
        name="horizontal",
    )(hidden, low, high, seam, gates, cand, *earlier)


def pairs_kernel(gates_ref, cand_ref, reset_out, cand_out):
    taps, depth, ch = cand_ref.shape
    none = jnp.zeros((depth, ch), bf16)
    reset = lambda j: gates_ref[j, :, pl.ds(ch, ch)]
    cand = lambda j: cand_ref[j]
    for out_ref, tap in ((reset_out, reset), (cand_out, cand)):
        for j in range(taps + 1):
            out_ref[j, :, 0:ch] = tap(j) if j < taps else none
            out_ref[j, :, ch : 2 * ch] = tap(j - 1) if j > 0 else none


def pairs_of(gates, cand):
    taps, depth, ch = cand.shape
    shape = jax.ShapeDtypeStruct((taps + 1, depth, 2 * ch), bf16)
    return pl.pallas_call(
        pairs_kernel,
        in_specs=[IN_VMEM] * 2,
        out_specs=[IN_VMEM] * 2,
        out_shape=[shape, shape],
        compiler_params=params(4),
        name="pairs",
    )(gates, cand)


def banded(outer_ref, inner_ref, half):
    outer = state_rows(outer_ref)
    return outer[:half] + state_rows(inner_ref) + outer[half:]


def stack(sources, rows):
    return jnp.concatenate(
        [piece[at] for y in rows for piece, at in (source[y] for source in sources)], axis=1
    )


def gates_kernel(
    outer_ref, inner_ref, low_ref, high_ref, gates_ref, update_ref, reset_ref, partial_ref
):
    taps, depth, wide = gates_ref.shape
    ch = wide // 2
    half = taps // 2
    state = banded(outer_ref, inner_ref, half)
    sources = (state, state_rows(low_ref, high_ref))
    rows = len(state)
    inner = range(half, rows - half)
    weights = lambda first, last: gates_ref[pl.ds(first, last - first)].reshape(-1, wide)
    sums = [dotf(stack(sources, range(y - half, y + half + 1)), weights(0, taps)) for y in inner]
    for i, y in enumerate([*range(half), *range(rows - half, rows)]):
        first, last = max(y - half, 0), min(y + half + 1, rows)
        partial_ref[i] = dotf(
            stack(sources, range(first, last)), weights(first - y + half, last - y + half)
        )
    for i, y in enumerate(inner):
        piece, at = state[y]
        update_ref[i] = sigmoid(sums[i][:, :ch])
        reset_ref[i] = (sigmoid(sums[i][:, ch:]) * piece[at].astype(f32)).astype(bf16)


def inner_gates(outer, inner, low, high, gates):
    count, width, ch = inner.shape
    half = gates.shape[0] // 2
    return pl.pallas_call(
        gates_kernel,
        in_specs=[IN_VMEM] * 5,
        out_specs=[IN_VMEM] * 3,
        out_shape=[
            jax.ShapeDtypeStruct((count, width, ch), f32),
            jax.ShapeDtypeStruct((count, width, ch), bf16),
            jax.ShapeDtypeStruct((2 * half, width, 2 * ch), f32),
        ],
        compiler_params=params(4),
        name="inner_gates",
    )(outer, inner, low, high, gates)


def outer_kernel(
    outer_ref, partial_ref, low_ref, high_ref, hidden_near, hidden_far, motion_near, motion_far,
    gates_ref, pairs_ref, update_ref, reset_ref, rim_ref, motion_rim, hidden_rim,
):
    taps, _, wide = gates_ref.shape
    ch = wide // 2
    half = taps // 2
    fill_rim(motion_rim, motion_near, motion_far)
    fill_rim(hidden_rim, hidden_near, hidden_far)
    above, below = state_rows(hidden_rim)[:half], state_rows(hidden_rim)[half:]
    own, flow = state_rows(outer_ref), state_rows(low_ref, high_ref)
    rim = state_rows(motion_rim)
    top = (above + own[:half], rim[half : 2 * half] + flow[:half])
    bottom = (own[half:] + below, flow[-half:] + rim[2 * half : 3 * half])
    weights = lambda first, last: gates_ref[pl.ds(first, last - first)].reshape(-1, wide)
    pairs = lambda first, last: pairs_ref[pl.ds(first, last - first)].reshape(-1, wide)
    flow_pairs = lambda first: pairs_ref[pl.ds(first, half), ch:, :].reshape(-1, wide)
    sums = []
    for i in range(half):
        sums.append(dotf(stack(top, range(i, half)), weights(0, half - i)))
    for i in range(half):
        rows = range(half, half + i + 1)
        sums.append(dotf(stack(bottom, rows), weights(taps - 1 - i, taps)))
    beyond = [
        dotf(stack(top, range(2 * half)), pairs(half, taps + 1))
        + dotf(stack((rim,), range(half)), flow_pairs(0)),
        dotf(stack(bottom, range(2 * half)), pairs(0, 2 * half))
        + dotf(stack((rim,), range(3 * half, 4 * half)), flow_pairs(2 * half)),
    ]
    for i in range(2 * half):
        total = sums[i] + partial_ref[i]
        update_ref[i] = sigmoid(total[:, :ch])
        reset_ref[i] = (sigmoid(total[:, ch:]) * outer_ref[i].astype(f32)).astype(bf16)
    for i in range(2):
        rim_ref[2 * i], rim_ref[2 * i + 1] = beyond[i][:, :ch], beyond[i][:, ch:]


def outer_gates(outer, partial, low, high, hidden_rims, motion_rims, gates, pairs):
    count, width, ch = outer.shape
    half = gates.shape[0] // 2
    shape = lambda kind: jax.ShapeDtypeStruct((count, width, ch), kind)
    return pl.pallas_call(
        outer_kernel,
        in_specs=[IN_VMEM] * 10,
        out_specs=[IN_VMEM] * 4,
        out_shape=[
            shape(f32),
            shape(bf16),
            shape(f32),
            jax.ShapeDtypeStruct((4 * half, width, ch), bf16),
        ],
        scratch_shapes=[pltpu.VMEM((2 * half, width, ch), bf16)],
        compiler_params=params(4),
        name="outer_gates",
    )(outer, partial, low, high, *hidden_rims, *motion_rims, gates, pairs)


def blend(state, update, total):
    return ((1.0 - update) * state.astype(f32) + update * jnp.tanh(total)).astype(bf16)


def cand_kernel(
    reset_outer, reset_inner, low_ref, high_ref, motion_rim, inner_ref, update_ref, pairs_ref,
    out_ref, partial_ref,
):
    blocks, depth, wide = pairs_ref.shape
    ch = wide // 2
    half = (blocks - 1) // 2
    reset = banded(reset_outer, reset_inner, half)
    sources = (reset, state_rows(low_ref, high_ref))
    rows = len(reset)
    weights = lambda first, last: pairs_ref[pl.ds(first, last - first)].reshape(-1, wide)
    sums = {}
    for y in range(half, rows - half, 2):
        rows_read = range(y - half, y + half + 2)
        sums[y] = dotf(stack(sources, rows_read), weights(0, blocks))
    rim = state_rows(motion_rim)
    flow_weights = lambda first, last: pairs_ref[pl.ds(first, last - first), ch:, :].reshape(
        -1, wide
    )
    for i, y in enumerate((0, rows - half)):
        first, last = max(y - half, 0), min(y + half + 2, rows)
        total = dotf(stack(sources, range(first, last)), weights(first - y + half, last - y + half))
        at = (0, half) if i == 0 else (blocks - half, blocks)
        total += dotf(stack((rim,), range(half * (i + 1), half * (i + 2))), flow_weights(*at))
        partial_ref[2 * i], partial_ref[2 * i + 1] = total[:, :ch], total[:, ch:]
    for y in range(half, rows - half, 2):
        for k in range(2):
            i = y - half + k
            total = sums[y][:, k * ch : (k + 1) * ch]
            out_ref[i] = blend(inner_ref[i], update_ref[i], total)


def inner_states(resets, low, high, motion_rim, inner, update, pairs):
    count, width, ch = inner.shape
    half = (pairs.shape[0] - 1) // 2
    return pl.pallas_call(
        cand_kernel,
        in_specs=[IN_VMEM] * 8,
        out_specs=[IN_VMEM] * 2,
        out_shape=[
            jax.ShapeDtypeStruct((count, width, ch), bf16),
            jax.ShapeDtypeStruct((2 * half, width, ch), f32),
        ],
        compiler_params=params(4),
        name="inner_states",
    )(*resets, low, high, motion_rim, inner, update, pairs)


def final_kernel(
    inner_ref, edge_near, edge_far, last_near, last_far, outer_ref, update_ref, partial_ref,
    beyond_ref, reset_pairs, cand_pairs, out_ref, edge_rim, last_rim, reset_rim, done, sems,
):
    blocks, _, wide = cand_pairs.shape
    ch = wide // 2
    half = (blocks - 1) // 2
    rows = out_ref.shape[1]
    count = inner_ref.shape[0]
    stores = [pltpu.make_async_copy(inner_ref, out_ref.at[0, pl.ds(half, count)], sems.at[0])]
    stores[0].start()
    fill_rim(edge_rim, edge_near, edge_far)
    fill_rim(last_rim, last_near, last_far)
    last, rim = state_rows(last_rim), state_rows(reset_rim)
    side = lambda i: range(half * i, half * i + half)
    weights = lambda ref, i: ref[pl.ds((blocks - half) * i, half), :ch, :].reshape(-1, wide)
    beyond = [dotf(stack((last,), side(i)), weights(reset_pairs, i)) for i in range(2)]
    for i in range(2):
        for k in range(2):
            at = 2 * i + k
            total = beyond_ref[at] + beyond[i][:, k * ch : (k + 1) * ch]
            reset_rim[at] = (sigmoid(total) * edge_rim[at].astype(f32)).astype(bf16)
    sums = [dotf(stack((rim,), side(i)), weights(cand_pairs, i)) for i in range(2)]
    for i in range(2):
        for k in range(2):
            at = 2 * i + k
            total = partial_ref[at] + sums[i][:, k * ch : (k + 1) * ch]
            done[at] = blend(outer_ref[at], update_ref[at], total)
        target = out_ref.at[0, pl.ds(0 if i == 0 else rows - half, half)]
        stores.append(pltpu.make_async_copy(done.at[pl.ds(half * i, half)], target, sems.at[i + 1]))
        stores[-1].start()
    for store in stores:
        store.wait()


def final_states(inner, edge_rims, last_rims, outer, update, partial, beyond, reset_pairs, cand_pairs):
    count, width, ch = outer.shape
    rows = count + inner.shape[0]
    return pl.pallas_call(
        final_kernel,
        in_specs=[IN_VMEM] * 11,
        out_specs=IN_HBM,
        out_shape=jax.ShapeDtypeStruct((1, rows, width, ch), bf16),
        scratch_shapes=[pltpu.VMEM((count, width, ch), bf16)] * 4 + [pltpu.SemaphoreType.DMA((3,))],
        compiler_params=params(4),
        name="final_states",
    )(inner, *edge_rims, *last_rims, outer, update, partial, beyond, reset_pairs, cand_pairs)


def shards(
    left_feats, right_feats, prev_hidden, warp_list, enc_weight, hgate_w, hcand_w, vgate_w, vcand_w
):
    rows = prev_hidden.shape[1]
    half = vgate_w.shape[0] // 2
    outer_rows = (*range(half), *range(rows - half, rows))
    inner_rows = tuple(range(half, rows - half))
    swap_cols = lambda value: lax.ppermute(value, "cols", [(0, 1), (1, 0)])
    swap_rows = lambda near, far: (swap_near(near, "rows"), swap_far(far, "rows"))
    pinned = lax.optimization_barrier

    warp_list = jnp.transpose(warp_list, (0, 2, 3, 1))
    lists = swap_rows(warp_list, warp_list)
    edge = swap_cols(right_feats)
    low = motion_of(0, rows // 2, left_feats, right_feats, edge, enc_weight)
    blocks = gather_blocks(*lists, prev_hidden, low)
    near, far = swap_rows(*blocks)
    high = motion_of(rows // 2, rows // 2, left_feats, right_feats, edge, enc_weight, *blocks)
    reset_pairs, cand_pairs = pairs_of(vgate_w, vcand_w)
    edges = held_until(edges_of(low, high, rows // 2), near, far, reset_pairs)
    motion_rims = swap_rows(*edges)
    seam = seam_of(warp_list, prev_hidden, near, far, low, high)
    warped = warp_of(warp_list, prev_hidden, near, far, seam)
    seam = swap_cols(seam)
    outer, *edges = horizontal_pass(outer_rows, warped, low, high, seam, hgate_w, hcand_w)
    edge_rims = swap_rows(*edges)
    inner, *edges = horizontal_pass(
        inner_rows, warped, low, high, seam, hgate_w, hcand_w, *edges
    )
    inner, edges, motion_near = pinned((inner, edges, motion_rims[0]))
    motion_rims = (motion_near, motion_rims[1])
    last_rims = swap_rows(*edges)
    update_inner, reset_inner, partial = inner_gates(outer, inner, low, high, vgate_w)
    update_outer, reset_outer, beyond, motion_rim = outer_gates(
        outer, partial, low, high, edge_rims, motion_rims, vgate_w, reset_pairs
    )
    resets = (reset_outer, reset_inner)
    inner, partial = inner_states(
        resets, low, high, motion_rim, inner, update_inner, cand_pairs
    )
    return final_states(
        inner, edge_rims, last_rims, outer, update_outer, partial, beyond, reset_pairs, cand_pairs
    )


def solution(mesh):
    spread = P(("groups", "cams"), "rows", "cols", None)
    return jax.shard_map(
        shards,
        mesh=mesh,
        in_specs=(spread,) * 4 + (P(),) * 5,
        out_specs=spread,
        check_vma=False,
    )
```

```python
import functools

import jax
import jax.numpy as jnp
from jax import lax
from jax.experimental import pallas as pl
from jax.experimental.pallas import tpu as pltpu
from jax.sharding import PartitionSpec as P

bf16 = jnp.bfloat16
f32 = jnp.float32
SEAM = 16


def dotf(a, b):
    return jnp.dot(a, b, preferred_element_type=f32)


def sigmoid(v):
    return 0.5 * jnp.tanh(0.5 * v) + 0.5


def state_rows(*pieces):
    return [(piece, r) for piece in pieces for r in range(piece.shape[0])]


def fill_rim(rim_ref, near_ref, far_ref):
    count = near_ref.shape[0]
    near = count * near_below()
    rim_ref[pl.ds(near, count)] = near_ref[...]
    rim_ref[pl.ds(count - near, count)] = far_ref[...]


def swap_near(value, axis):
    count = lax.axis_size(axis)
    pairs = [(i, i ^ 1) for i in range(count) if i ^ 1 < count]
    return lax.ppermute(value, axis, pairs)


def swap_far(value, axis):
    count = lax.axis_size(axis)
    pairs = []
    for i in range(1, count - 1, 2):
        pairs += [(i, i + 1), (i + 1, i)]
    return lax.ppermute(value, axis, pairs)


IN_VMEM = pl.BlockSpec(memory_space=pltpu.VMEM)
IN_SMEM = pl.BlockSpec(memory_space=pltpu.SMEM)
IN_HBM = pl.BlockSpec(memory_space=pltpu.HBM)


def ordered(kernel, inputs, earlier):
    return lambda *refs: kernel(*refs[:inputs], *refs[inputs + len(earlier) :])


def right_half():
    return lax.axis_index("cols")


def near_below():
    return 1 - lax.axis_index("rows") % 2


def in_hbm(value):
    return pltpu.with_memory_space_constraint(value, pltpu.HBM)


def params(megabytes):
    return pltpu.CompilerParams(vmem_limit_bytes=megabytes << 20)


def motion_kernel(
    first, left_feats, right_feats, edge_ref, weight, out_ref, left_ref, window,
    weight_ref, sems,
):
    disparities = weight_ref.shape[0]
    rows, width, feats = left_ref.shape
    tile = 128
    own = pl.ds(first, rows)
    loads = [
        pltpu.make_async_copy(left_feats.at[0, own], left_ref, sems.at[0]),
        pltpu.make_async_copy(
            right_feats.at[0, own], window.at[:, pl.ds(disparities, width), :], sems.at[1]
        ),
        pltpu.make_async_copy(weight, weight_ref, sems.at[2]),
    ]
    for load in loads:
        load.start()
    far_edge = edge_ref.shape[2] - disparities
    for r in range(rows):
        other = edge_ref[0, first + r, pl.ds(far_edge, disparities), :]
        window[r, pl.ds(0, disparities), :] = jnp.where(
            right_half() == 1, other, jnp.zeros_like(other)
        )
    scale = feats**-0.5
    lane = lax.broadcasted_iota(jnp.int32, (tile, tile), 1)
    row = lax.broadcasted_iota(jnp.int32, (tile, tile), 0)
    keep = lane < row
    flip = (lane + row == tile - 1).astype(f32).astype(bf16)
    for load in loads:
        load.wait()
    turned = jnp.concatenate(
        [
            dotf(flip, weight_ref[pl.ds(disparities - tile, tile), :]).astype(bf16),
            dotf(flip, weight_ref[pl.ds(0, tile), :]).astype(bf16)[2 * tile - disparities :, :],
        ],
        axis=0,
    )
    span = disparities + tile
    blocks = -(-span // tile)
    tiles = [(r, t * tile) for r in range(rows) for t in range(width // tile)]
    flipped = [dotf(flip, left_ref[r, pl.ds(x, tile), :]).astype(bf16) for r, x in tiles]
    scores = [
        lax.dot_general(
            part,
            window[r, pl.ds(x, blocks * tile), :],
            (((1,), (1,)), ((), ())),
            preferred_element_type=f32,
        )
        * scale
        for part, (r, x) in zip(flipped, tiles)
    ]
    skewed = []
    for score in scores:
        rolled = [
            pltpu.roll(score[:, tile * j : tile * (j + 1)], 0, 1, stride=1, stride_axis=0)
            for j in range(blocks)
        ]
        lanes = [jnp.where(keep, rolled[j], rolled[j + 1]).astype(bf16) for j in range(blocks - 1)]
        skewed.append(jnp.concatenate(lanes, axis=1)[:, :disparities])
    motions = [dotf(part, turned).astype(bf16) for part in skewed]
    for part, (r, x) in zip(motions, tiles):
        out_ref[r, pl.ds(x, tile), :] = dotf(flip, part).astype(bf16)


def motion_of(first, rows, left, right, edge, weight, *earlier):
    width, feats = left.shape[2:]
    return pl.pallas_call(
        ordered(functools.partial(motion_kernel, first), 4, earlier),
        in_specs=[IN_HBM, IN_HBM, IN_VMEM, IN_HBM] + [IN_VMEM] * len(earlier),
        out_specs=IN_VMEM,
        out_shape=jax.ShapeDtypeStruct((rows, width, weight.shape[1]), bf16),
        scratch_shapes=[
            pltpu.VMEM((rows, width, feats), bf16),
            pltpu.VMEM((rows, width + 256, feats), bf16),
            pltpu.VMEM(weight.shape, bf16),
            pltpu.SemaphoreType.DMA((3,)),
        ],
        compiler_params=params(4),
        name="motion",
    )(in_hbm(left), in_hbm(right), edge, in_hbm(weight), *earlier)


def edges_kernel(low_ref, high_ref, near_ref, far_ref):
    count = near_ref.shape[0]
    low, high = low_ref[pl.ds(0, count)], high_ref[pl.ds(high_ref.shape[0] - count, count)]
    below = near_below() == 1
    near_ref[...] = jnp.where(below, high, low)
    far_ref[...] = jnp.where(below, low, high)


def edges_of(low, high, count):
    shape = jax.ShapeDtypeStruct((count,) + low.shape[1:], bf16)
    return pl.pallas_call(
        edges_kernel,
        in_specs=[IN_VMEM] * 2,
        out_specs=[IN_VMEM, IN_VMEM],
        out_shape=[shape, shape],
        compiler_params=params(4),
        name="edges",
    )(low, high)


def gather_kernel(near_list, far_list, prev_ref, near_out, far_out, sems):
    _, band_blocks, _, band_rows = near_list.shape
    slots, width, _ = near_out.shape
    sign = 2 * near_below() - 1
    lane = lax.broadcasted_iota(jnp.int32, (1, band_rows), 1)
    copies = []
    sides = ((near_list, near_out, sign), (far_list, far_out, -sign))
    for side, (list_ref, out, wanted) in enumerate(sides):
        before = jnp.zeros((1, 1), jnp.int32)
        ranks, asked = [], []
        for block in range(band_blocks):
            field = lambda k: list_ref[0, block, pl.ds(k, 1), :]
            hit = (field(0) == wanted).astype(jnp.int32)
            rank = jnp.broadcast_to(before, (1, band_rows))
            for r in range(band_rows - 1):
                rank = rank + jnp.where(lane > r, hit[:, r : r + 1], 0)
            ranks.append(jnp.where(hit > 0, rank, -1))
            asked.append(field(1) * band_blocks + field(2))
            before = before + jnp.sum(hit, axis=1, keepdims=True)
        for slot in range(slots):
            found = sum(
                jnp.where(rank == slot, source, 0) for rank, source in zip(ranks, asked)
            )
            source = jnp.sum(found)
            row = source // band_blocks
            column = pl.multiple_of(source % band_blocks * width, width)
            block = prev_ref.at[0, row, pl.ds(column, width), :]
            copies.append(pltpu.make_async_copy(block, out.at[slot], sems.at[side, slot]))
            copies[-1].start()
    for copy in copies:
        copy.wait()


def gather_blocks(near_list, far_list, prev, *earlier):
    _, band_blocks, _, band_rows = near_list.shape
    _, _, width, hidden = prev.shape
    slots = band_rows * band_blocks // 4
    shape = jax.ShapeDtypeStruct((slots, width // band_blocks, hidden), bf16)
    return pl.pallas_call(
        ordered(gather_kernel, 3, earlier),
        in_specs=[IN_VMEM, IN_VMEM, IN_HBM] + [IN_VMEM] * len(earlier),
        out_specs=[IN_VMEM, IN_VMEM],
        out_shape=[shape, shape],
        scratch_shapes=[pltpu.SemaphoreType.DMA((2, slots))],
        compiler_params=params(4),
        name="gather",
    )(near_list, far_list, in_hbm(prev), *earlier)


def pick_blocks(list_ref, rows, blocks, visit):
    last = rows * blocks // 4 - 1
    sign = 2 * near_below() - 1
    nears, fars = jnp.int32(0), jnp.int32(0)
    for block in range(blocks):
        for row in range(rows):
            field = lambda k: list_ref[0, block, k, row]
            offset = field(0)
            is_near, is_far = offset == -sign, offset == sign
            visit(
                row, block, field, is_near, is_far, jnp.minimum(nears, last),
                jnp.minimum(fars, last),
            )
            nears += is_near.astype(jnp.int32)
            fars += is_far.astype(jnp.int32)


def seam_kernel(list_ref, prev_ref, near_ref, far_ref, low_ref, high_ref, seam_ref):
    width, ch = near_ref.shape[1:]
    rows, total = prev_ref.shape[1:3]
    band_blocks = total // width
    is_left = right_half() == 0
    start = pl.multiple_of((width - SEAM) * (1 - right_half()), SEAM)
    inside = pl.ds(start, SEAM)

    def visit(row, block, field, is_near, is_far, near_slot, far_slot):
        if block in (0, band_blocks - 1):
            source = pl.multiple_of(field(2) * width + start, SEAM)
            local = prev_ref[0, field(1), pl.ds(source, SEAM), :]
            near, far = near_ref[near_slot, inside, :], far_ref[far_slot, inside, :]
            picked = jnp.where(is_near, near, jnp.where(is_far, far, local))
            picked = jnp.where(field(3) > 0, picked, jnp.zeros_like(picked))
            if block > 0:
                picked = jnp.where(is_left, picked, seam_ref[row, :, 0:ch])
            seam_ref[row, :, 0:ch] = picked

    pick_blocks(list_ref, rows, band_blocks, visit)
    edge = pl.multiple_of((band_blocks * width - SEAM) * (1 - right_half()), SEAM)
    half = low_ref.shape[0]
    seam_ref[pl.ds(0, half), :, ch : 2 * ch] = low_ref[:, pl.ds(edge, SEAM), :]
    seam_ref[pl.ds(half, half), :, ch : 2 * ch] = high_ref[:, pl.ds(edge, SEAM), :]


def seam_of(warp_list, prev, near, far, low, high):
    _, rows, _, ch = prev.shape
    return pl.pallas_call(
        seam_kernel,
        in_specs=[IN_SMEM] + [IN_VMEM] * 5,
        out_specs=IN_VMEM,
        out_shape=jax.ShapeDtypeStruct((rows, SEAM, 2 * ch), bf16),
        compiler_params=params(4),
        name="seam",
    )(warp_list, prev, near, far, low, high)


def warp_kernel(list_ref, prev_ref, near_ref, far_ref, out_ref):
    width = near_ref.shape[1]

    def visit(row, block, field, is_near, is_far, near_slot, far_slot):
        column = pl.multiple_of(field(2) * width, width)
        local = prev_ref[0, field(1), pl.ds(column, width), :]
        picked = jnp.where(
            is_near, near_ref[near_slot], jnp.where(is_far, far_ref[far_slot], local)
        )
        picked = jnp.where(field(3) > 0, picked, jnp.zeros_like(picked))
        out_ref[row, pl.ds(block * width, width), :] = picked

    rows, total = prev_ref.shape[1:3]
    pick_blocks(list_ref, rows, total // width, visit)


def warp_of(warp_list, prev, near, far, *earlier):
    return pl.pallas_call(
        ordered(warp_kernel, 4, earlier),
        in_specs=[IN_SMEM] + [IN_VMEM] * (3 + len(earlier)),
        out_specs=IN_VMEM,
        out_shape=jax.ShapeDtypeStruct(prev.shape[1:], bf16),
        compiler_params=params(4),
        name="warp",
    )(warp_list, prev, near, far, *earlier)


def horizontal_kernel(
    rows, hidden_ref, low_ref, high_ref, seam_ref, gates_ref, cand_ref, out_ref, *rest
):
    *sent, joined, reset, partial = rest
    _, width, ch = hidden_ref.shape
    taps = gates_ref.shape[0]
    half = taps // 2
    right = right_half()
    pad = SEAM
    own = pl.multiple_of(pad + pad * right, pad)
    seam = pl.multiple_of(pad + width * (1 - right), pad)
    span = width + SEAM
    flow = state_rows(low_ref, high_ref)
    gates = gates_ref[...].reshape(taps * 2 * ch, 2 * ch)
    count = range(len(rows))
    for r in count:
        piece, at = flow[rows[r]]
        for edge in (0, span + pad):
            joined[r, pl.ds(edge, pad), :] = jnp.zeros((pad, 2 * ch), bf16)
            reset[r, pl.ds(edge, pad), :] = jnp.zeros((pad, ch), bf16)
        joined[r, pl.ds(own, width), 0:ch] = hidden_ref[rows[r]]
        joined[r, pl.ds(own, width), ch : 2 * ch] = piece[at]
        joined[r, pl.ds(seam, SEAM), :] = seam_ref[rows[r]]
    sums = [
        dotf(
            jnp.concatenate(
                [joined[r, pl.ds(pad - half + t, span), :] for t in range(taps)], axis=1
            ),
            gates,
        )
        for r in count
    ]
    update = []
    for r in count:
        update.append(sigmoid(sums[r][:, :ch]))
        current = joined[r, pl.ds(pad, span), 0:ch].astype(f32)
        reset[r, pl.ds(pad, span), :] = (sigmoid(sums[r][:, ch:]) * current).astype(bf16)
    for r in count:
        both = jnp.concatenate([reset[r], joined[r, :, ch : 2 * ch]], axis=1)
        for t in range(0, taps, 2):
            pair = jnp.concatenate([cand_ref[k] for k in range(t, min(t + 2, taps))], axis=1)
            partial[r, :, pl.ds(t * ch, pair.shape[1])] = dotf(both, pair)
    totals = []
    for r in count:
        total = None
        for t in range(taps):
            part = partial[r, pl.ds(pad - half + t, span), pl.ds(t * ch, ch)]
            total = part if total is None else total + part
        totals.append(total)
    for r in count:
        current = joined[r, pl.ds(pad, span), 0:ch].astype(f32)
        cand = jnp.tanh(totals[r])
        blended = (1.0 - update[r]) * current + update[r] * cand
        reset[r, pl.ds(pad, span), :] = blended.astype(bf16)
    for r in count:
        out_ref[r] = reset[r, pl.ds(own, width), :]
    near = half * near_below()
    for sent_ref, first in zip(sent, (near, half - near)):
        sent_ref[...] = out_ref[pl.ds(first, half)]


def horizontal_pass(rows, send, hidden, low, high, seam, gates, cand):
    _, width, ch = hidden.shape
    taps = gates.shape[0]
    length = width + SEAM + 2 * SEAM
    shape = lambda count: jax.ShapeDtypeStruct((count, width, ch), bf16)
    shapes = [shape(len(rows))] + [shape(taps // 2)] * (2 if send else 0)
    return pl.pallas_call(
        functools.partial(horizontal_kernel, rows),
        in_specs=[IN_VMEM] * 6,
        out_specs=[IN_VMEM] * len(shapes),
        out_shape=shapes,
        scratch_shapes=[
            pltpu.VMEM((len(rows), length, 2 * ch), bf16),
            pltpu.VMEM((len(rows), length, ch), bf16),
            pltpu.VMEM((len(rows), length, taps * ch), f32),
        ],
        compiler_params=params(11),
        name="horizontal",
    )(hidden, low, high, seam, gates, cand)


def pairs_kernel(gates_ref, cand_ref, reset_out, cand_out):
    taps, depth, ch = cand_ref.shape
    none = jnp.zeros((depth, ch), bf16)
    reset = lambda j: gates_ref[j, :, pl.ds(ch, ch)]
    cand = lambda j: cand_ref[j]
    for out_ref, tap in ((reset_out, reset), (cand_out, cand)):
        for j in range(taps + 1):
            out_ref[j, :, 0:ch] = tap(j) if j < taps else none
            out_ref[j, :, ch : 2 * ch] = tap(j - 1) if j > 0 else none


def pairs_of(gates, cand):
    taps, depth, ch = cand.shape
    shape = jax.ShapeDtypeStruct((taps + 1, depth, 2 * ch), bf16)
    return pl.pallas_call(
        pairs_kernel,
        in_specs=[IN_VMEM] * 2,
        out_specs=[IN_VMEM] * 2,
        out_shape=[shape, shape],
        compiler_params=params(4),
        name="pairs",
    )(gates, cand)


def banded(outer_ref, inner_ref, half):
    outer = state_rows(outer_ref)
    return outer[:half] + state_rows(inner_ref) + outer[half:]


def stack(sources, rows):
    return jnp.concatenate(
        [piece[at] for y in rows for piece, at in (source[y] for source in sources)], axis=1
    )


def own_sums_kernel(
    outer_ref, inner_ref, low_ref, high_ref, gates_ref, partial_ref, near_ref, far_ref
):
    taps, _, wide = gates_ref.shape
    ch = wide // 2
    half = taps // 2
    sources = (banded(outer_ref, inner_ref, half), state_rows(low_ref, high_ref))
    rows = len(sources[0])
    weights = lambda first, last: gates_ref[pl.ds(first, last - first)].reshape(-1, wide)
    for i, y in enumerate([*range(half), *range(rows - half, rows)]):
        first, last = max(y - half, 0), min(y + half + 1, rows)
        partial_ref[i] = dotf(
            stack(sources, range(first, last)), weights(first - y + half, last - y + half)
        )
    near = half * near_below()
    near_ref[...] = partial_ref[pl.ds(near, half), :, pl.ds(ch, ch)].astype(bf16)
    far_ref[...] = partial_ref[pl.ds(half - near, half), :, pl.ds(ch, ch)].astype(bf16)


def own_sums(outer, inner, low, high, gates):
    count, width, ch = outer.shape
    half = gates.shape[0] // 2
    sent = jax.ShapeDtypeStruct((half, width, ch), bf16)
    return pl.pallas_call(
        own_sums_kernel,
        in_specs=[IN_VMEM] * 5,
        out_specs=[IN_VMEM] * 3,
        out_shape=[jax.ShapeDtypeStruct((count, width, 2 * ch), f32), sent, sent],
        compiler_params=params(4),
        name="own_sums",
    )(outer, inner, low, high, gates)


def gates_kernel(outer_ref, inner_ref, low_ref, high_ref, gates_ref, update_ref, reset_ref):
    taps, _, wide = gates_ref.shape
    ch = wide // 2
    half = taps // 2
    state = banded(outer_ref, inner_ref, half)
    sources = (state, state_rows(low_ref, high_ref))
    inner = range(half, len(state) - half)
    weights = gates_ref[...].reshape(-1, wide)
    sums = [dotf(stack(sources, range(y - half, y + half + 1)), weights) for y in inner]
    for i, y in enumerate(inner):
        piece, at = state[y]
        update_ref[i] = sigmoid(sums[i][:, :ch])
        reset_ref[i] = (sigmoid(sums[i][:, ch:]) * piece[at].astype(f32)).astype(bf16)


def inner_gates(outer, inner, low, high, gates, *earlier):
    count, width, ch = inner.shape
    return pl.pallas_call(
        ordered(gates_kernel, 5, earlier),
        in_specs=[IN_VMEM] * (5 + len(earlier)),
        out_specs=[IN_VMEM] * 2,
        out_shape=[
            jax.ShapeDtypeStruct((count, width, ch), f32),
            jax.ShapeDtypeStruct((count, width, ch), bf16),
        ],
        compiler_params=params(4),
        name="inner_gates",
    )(outer, inner, low, high, gates, *earlier)


def outer_kernel(
    outer_ref, partial_ref, low_ref, high_ref, hidden_near, hidden_far, motion_near, motion_far,
    gates_ref, pairs_ref, update_ref, reset_ref, rim_ref, motion_rim, hidden_rim,
):
    taps, _, wide = gates_ref.shape
    ch = wide // 2
    half = taps // 2
    fill_rim(motion_rim, motion_near, motion_far)
    fill_rim(hidden_rim, hidden_near, hidden_far)
    above, below = state_rows(hidden_rim)[:half], state_rows(hidden_rim)[half:]
    own, flow = state_rows(outer_ref), state_rows(low_ref, high_ref)
    rim = state_rows(motion_rim)
    top = (above + own[:half], rim[:half] + flow[:half])
    bottom = (own[half:] + below, flow[-half:] + rim[half:])
    weights = lambda first, last: gates_ref[pl.ds(first, last - first)].reshape(-1, wide)
    pairs = lambda first, last: pairs_ref[pl.ds(first, last - first)].reshape(-1, wide)
    sums = []
    for i in range(half):
        sums.append(dotf(stack(top, range(i, half)), weights(0, half - i)))
    for i in range(half):
        rows = range(half, half + i + 1)
        sums.append(dotf(stack(bottom, rows), weights(taps - 1 - i, taps)))
    beyond = [
        dotf(stack(top, range(half, 2 * half)), pairs(2 * half, 3 * half)),
        dotf(stack(bottom, range(half)), pairs(0, half)),
    ]
    for i in range(2 * half):
        total = sums[i] + partial_ref[i]
        update_ref[i] = sigmoid(total[:, :ch])
        reset_ref[i] = (sigmoid(total[:, ch:]) * outer_ref[i].astype(f32)).astype(bf16)
    for i in range(2):
        rim_ref[2 * i], rim_ref[2 * i + 1] = beyond[i][:, :ch], beyond[i][:, ch:]


def outer_gates(outer, partial, low, high, hidden_rims, motion_rims, gates, pairs):
    count, width, ch = outer.shape
    half = gates.shape[0] // 2
    shape = lambda kind: jax.ShapeDtypeStruct((count, width, ch), kind)
    return pl.pallas_call(
        outer_kernel,
        in_specs=[IN_VMEM] * 10,
        out_specs=[IN_VMEM] * 4,
        out_shape=[
            shape(f32),
            shape(bf16),
            shape(f32),
            shape(bf16),
        ],
        scratch_shapes=[pltpu.VMEM((2 * half, width, ch), bf16)],
        compiler_params=params(4),
        name="outer_gates",
    )(outer, partial, low, high, *hidden_rims, *motion_rims, gates, pairs)


def blend(state, update, total):
    return ((1.0 - update) * state.astype(f32) + update * jnp.tanh(total)).astype(bf16)


def cand_kernel(
    reset_outer, reset_inner, low_ref, high_ref, motion_rim, inner_ref, update_ref, pairs_ref,
    out_ref, partial_ref,
):
    blocks, depth, wide = pairs_ref.shape
    ch = wide // 2
    half = (blocks - 1) // 2
    reset = banded(reset_outer, reset_inner, half)
    sources = (reset, state_rows(low_ref, high_ref))
    rows = len(reset)
    weights = lambda first, last: pairs_ref[pl.ds(first, last - first)].reshape(-1, wide)
    sums = {}
    for y in range(half, rows - half, 2):
        rows_read = range(y - half, y + half + 2)
        sums[y] = dotf(stack(sources, rows_read), weights(0, blocks))
    rim = state_rows(motion_rim)
    flow_weights = lambda first, last: pairs_ref[pl.ds(first, last - first), ch:, :].reshape(
        -1, wide
    )
    for i, y in enumerate((0, rows - half)):
        first, last = max(y - half, 0), min(y + half + 2, rows)
        total = dotf(stack(sources, range(first, last)), weights(first - y + half, last - y + half))
        at = (0, half) if i == 0 else (blocks - half, blocks)
        total += dotf(stack((rim,), range(half * i, half * (i + 1))), flow_weights(*at))
        partial_ref[2 * i], partial_ref[2 * i + 1] = total[:, :ch], total[:, ch:]
    for y in range(half, rows - half, 2):
        for k in range(2):
            i = y - half + k
            total = sums[y][:, k * ch : (k + 1) * ch]
            out_ref[i] = blend(inner_ref[i], update_ref[i], total)


def inner_states(resets, low, high, motion_rim, inner, update, pairs):
    count, width, ch = inner.shape
    half = (pairs.shape[0] - 1) // 2
    return pl.pallas_call(
        cand_kernel,
        in_specs=[IN_VMEM] * 8,
        out_specs=[IN_VMEM] * 2,
        out_shape=[
            jax.ShapeDtypeStruct((count, width, ch), bf16),
            jax.ShapeDtypeStruct((2 * half, width, ch), f32),
        ],
        compiler_params=params(4),
        name="inner_states",
    )(*resets, low, high, motion_rim, inner, update, pairs)


def final_kernel(
    inner_ref, edge_near, edge_far, last_near, last_far, outer_ref, update_ref, partial_ref,
    beyond_ref, cand_pairs, out_ref, edge_rim, last_rim, reset_rim, done, sems,
):
    blocks, _, wide = cand_pairs.shape
    ch = wide // 2
    half = (blocks - 1) // 2
    rows = out_ref.shape[1]
    count = inner_ref.shape[0]
    stores = [pltpu.make_async_copy(inner_ref, out_ref.at[0, pl.ds(half, count)], sems.at[0])]
    stores[0].start()
    fill_rim(edge_rim, edge_near, edge_far)
    fill_rim(last_rim, last_near, last_far)
    rim = state_rows(reset_rim)
    side = lambda i: range(half * i, half * i + half)
    weights = lambda ref, i: ref[pl.ds((blocks - half) * i, half), :ch, :].reshape(-1, wide)
    for at in range(2 * half):
        total = beyond_ref[at] + last_rim[at].astype(f32)
        reset_rim[at] = (sigmoid(total) * edge_rim[at].astype(f32)).astype(bf16)
    sums = [dotf(stack((rim,), side(i)), weights(cand_pairs, i)) for i in range(2)]
    for i in range(2):
        for k in range(2):
            at = 2 * i + k
            total = partial_ref[at] + sums[i][:, k * ch : (k + 1) * ch]
            done[at] = blend(outer_ref[at], update_ref[at], total)
        target = out_ref.at[0, pl.ds(0 if i == 0 else rows - half, half)]
        stores.append(pltpu.make_async_copy(done.at[pl.ds(half * i, half)], target, sems.at[i + 1]))
        stores[-1].start()
    for store in stores:
        store.wait()


def final_states(inner, edge_rims, last_rims, outer, update, partial, beyond, cand_pairs):
    count, width, ch = outer.shape
    rows = count + inner.shape[0]
    return pl.pallas_call(
        final_kernel,
        in_specs=[IN_VMEM] * 10,
        out_specs=IN_HBM,
        out_shape=jax.ShapeDtypeStruct((1, rows, width, ch), bf16),
        scratch_shapes=[pltpu.VMEM((count, width, ch), bf16)] * 4 + [pltpu.SemaphoreType.DMA((3,))],
        compiler_params=params(4),
        name="final_states",
    )(inner, *edge_rims, *last_rims, outer, update, partial, beyond, cand_pairs)


def shards(
    left_feats, right_feats, prev_hidden, warp_list, enc_weight, hgate_w, hcand_w, vgate_w, vcand_w
):
    rows = prev_hidden.shape[1]
    half = vgate_w.shape[0] // 2
    outer_rows = (*range(half), *range(rows - half, rows))
    inner_rows = tuple(range(half, rows - half))
    swap_cols = lambda value: lax.ppermute(value, "cols", [(0, 1), (1, 0)])
    swap_rows = lambda near, far: (swap_near(near, "rows"), swap_far(far, "rows"))
    pinned = lax.optimization_barrier

    warp_list = jnp.transpose(warp_list, (0, 2, 3, 1))
    lists = swap_rows(warp_list, warp_list)
    edge = swap_cols(right_feats)
    low = motion_of(0, rows // 2, left_feats, right_feats, edge, enc_weight)
    blocks = gather_blocks(*lists, prev_hidden, low)
    near, far = swap_rows(*blocks)
    high = motion_of(rows // 2, rows // 2, left_feats, right_feats, edge, enc_weight, *blocks)
    reset_pairs, cand_pairs = pairs_of(vgate_w, vcand_w)
    edges = edges_of(low, high, half)
    motion_rims = swap_rows(*edges)
    seam = seam_of(warp_list, prev_hidden, near, far, low, high)
    warped = warp_of(warp_list, prev_hidden, near, far, seam)
    seam = swap_cols(seam)
    outer, *edges = horizontal_pass(outer_rows, True, warped, low, high, seam, hgate_w, hcand_w)
    warped, edges, motion_rims = pinned((warped, edges, motion_rims))
    edge_rims = swap_rows(*edges)
    (inner,) = horizontal_pass(
        inner_rows, False, warped, low, high, seam, hgate_w, hcand_w
    )
    partial, *edges = own_sums(outer, inner, low, high, vgate_w)
    last_rims = swap_rows(*edges)
    update_inner, reset_inner = inner_gates(outer, inner, low, high, vgate_w, *edges)
    update_outer, reset_outer, beyond, motion_rim = outer_gates(
        outer, partial, low, high, edge_rims, motion_rims, vgate_w, reset_pairs
    )
    resets = (reset_outer, reset_inner)
    inner, partial = inner_states(
        resets, low, high, motion_rim, inner, update_inner, cand_pairs
    )
    return final_states(
        inner, edge_rims, last_rims, outer, update_outer, partial, beyond, cand_pairs
    )


def solution(mesh):
    spread = P(("groups", "cams"), "rows", "cols", None)
    return jax.shard_map(
        shards,
        mesh=mesh,
        in_specs=(spread,) * 4 + (P(),) * 5,
        out_specs=spread,
        check_vma=False,
    )
```

```python
import functools

import jax
import jax.numpy as jnp
from jax import lax
from jax.experimental import pallas as pl
from jax.experimental.pallas import tpu as pltpu
from jax.sharding import PartitionSpec as P

bf16 = jnp.bfloat16
f32 = jnp.float32
SEAM = 16


def dotf(a, b):
    return jnp.dot(a, b, preferred_element_type=f32)


def sigmoid(v):
    return 0.5 * jnp.tanh(0.5 * v) + 0.5


def state_rows(*pieces):
    return [(piece, r) for piece in pieces for r in range(piece.shape[0])]


def fill_rim(rim_ref, near_ref, far_ref):
    count = near_ref.shape[0]
    near = count * near_below()
    rim_ref[pl.ds(near, count)] = near_ref[...]
    rim_ref[pl.ds(count - near, count)] = far_ref[...]


def swap_near(value, axis):
    count = lax.axis_size(axis)
    pairs = [(i, i ^ 1) for i in range(count) if i ^ 1 < count]
    return lax.ppermute(value, axis, pairs)


def swap_far(value, axis):
    count = lax.axis_size(axis)
    pairs = []
    for i in range(1, count - 1, 2):
        pairs += [(i, i + 1), (i + 1, i)]
    return lax.ppermute(value, axis, pairs)


IN_VMEM = pl.BlockSpec(memory_space=pltpu.VMEM)
IN_SMEM = pl.BlockSpec(memory_space=pltpu.SMEM)
IN_HBM = pl.BlockSpec(memory_space=pltpu.HBM)


def ordered(kernel, inputs, earlier):
    return lambda *refs: kernel(*refs[:inputs], *refs[inputs + len(earlier) :])


def right_half():
    return lax.axis_index("cols")


def near_below():
    return 1 - lax.axis_index("rows") % 2


def in_hbm(value):
    return pltpu.with_memory_space_constraint(value, pltpu.HBM)


def params(megabytes):
    return pltpu.CompilerParams(vmem_limit_bytes=megabytes << 20)


def motion_kernel(
    first, left_feats, right_feats, edge_ref, weight, out_ref, left_ref, window,
    weight_ref, sems,
):
    disparities = weight_ref.shape[0]
    rows, width, feats = left_ref.shape
    tile = 128
    own = pl.ds(first, rows)
    loads = [
        pltpu.make_async_copy(left_feats.at[0, own], left_ref, sems.at[0]),
        pltpu.make_async_copy(
            right_feats.at[0, own], window.at[:, pl.ds(disparities, width), :], sems.at[1]
        ),
        pltpu.make_async_copy(weight, weight_ref, sems.at[2]),
    ]
    for load in loads:
        load.start()
    far_edge = edge_ref.shape[2] - disparities
    for r in range(rows):
        other = edge_ref[0, first + r, pl.ds(far_edge, disparities), :]
        window[r, pl.ds(0, disparities), :] = jnp.where(
            right_half() == 1, other, jnp.zeros_like(other)
        )
    scale = feats**-0.5
    lane = lax.broadcasted_iota(jnp.int32, (tile, tile), 1)
    row = lax.broadcasted_iota(jnp.int32, (tile, tile), 0)
    keep = lane < row
    flip = (lane + row == tile - 1).astype(f32).astype(bf16)
    for load in loads:
        load.wait()
    turned = jnp.concatenate(
        [
            dotf(flip, weight_ref[pl.ds(disparities - tile, tile), :]).astype(bf16),
            dotf(flip, weight_ref[pl.ds(0, tile), :]).astype(bf16)[2 * tile - disparities :, :],
        ],
        axis=0,
    )
    span = disparities + tile
    blocks = -(-span // tile)
    tiles = [(r, t * tile) for r in range(rows) for t in range(width // tile)]
    flipped = [dotf(flip, left_ref[r, pl.ds(x, tile), :]).astype(bf16) for r, x in tiles]
    scores = [
        lax.dot_general(
            part,
            window[r, pl.ds(x, blocks * tile), :],
            (((1,), (1,)), ((), ())),
            preferred_element_type=f32,
        )
        * scale
        for part, (r, x) in zip(flipped, tiles)
    ]
    skewed = []
    for score in scores:
        rolled = [
            pltpu.roll(score[:, tile * j : tile * (j + 1)], 0, 1, stride=1, stride_axis=0)
            for j in range(blocks)
        ]
        lanes = [jnp.where(keep, rolled[j], rolled[j + 1]).astype(bf16) for j in range(blocks - 1)]
        skewed.append(jnp.concatenate(lanes, axis=1)[:, :disparities])
    motions = [dotf(part, turned).astype(bf16) for part in skewed]
    for part, (r, x) in zip(motions, tiles):
        out_ref[r, pl.ds(x, tile), :] = dotf(flip, part).astype(bf16)


def motion_of(first, rows, left, right, edge, weight, *earlier):
    width, feats = left.shape[2:]
    return pl.pallas_call(
        ordered(functools.partial(motion_kernel, first), 4, earlier),
        in_specs=[IN_HBM, IN_HBM, IN_VMEM, IN_HBM] + [IN_VMEM] * len(earlier),
        out_specs=IN_VMEM,
        out_shape=jax.ShapeDtypeStruct((rows, width, weight.shape[1]), bf16),
        scratch_shapes=[
            pltpu.VMEM((rows, width, feats), bf16),
            pltpu.VMEM((rows, width + 256, feats), bf16),
            pltpu.VMEM(weight.shape, bf16),
            pltpu.SemaphoreType.DMA((3,)),
        ],
        compiler_params=params(4),
        name="motion",
    )(in_hbm(left), in_hbm(right), edge, in_hbm(weight), *earlier)


def edges_kernel(low_ref, high_ref, near_ref, far_ref):
    count = near_ref.shape[0]
    low, high = low_ref[pl.ds(0, count)], high_ref[pl.ds(high_ref.shape[0] - count, count)]
    below = near_below() == 1
    near_ref[...] = jnp.where(below, high, low)
    far_ref[...] = jnp.where(below, low, high)


def edges_of(low, high, count, *earlier):
    shape = jax.ShapeDtypeStruct((count,) + low.shape[1:], bf16)
    return pl.pallas_call(
        ordered(edges_kernel, 2, earlier),
        in_specs=[IN_VMEM] * (2 + len(earlier)),
        out_specs=[IN_VMEM, IN_VMEM],
        out_shape=[shape, shape],
        compiler_params=params(4),
        name="edges",
    )(low, high, *earlier)


def gather_kernel(near_list, far_list, prev_ref, near_out, far_out, sems):
    _, band_blocks, _, band_rows = near_list.shape
    slots, width, _ = near_out.shape
    sign = 2 * near_below() - 1
    lane = lax.broadcasted_iota(jnp.int32, (1, band_rows), 1)
    copies = []
    sides = ((near_list, near_out, sign), (far_list, far_out, -sign))
    for side, (list_ref, out, wanted) in enumerate(sides):
        before = jnp.zeros((1, 1), jnp.int32)
        ranks, asked = [], []
        for block in range(band_blocks):
            field = lambda k: list_ref[0, block, pl.ds(k, 1), :]
            hit = (field(0) == wanted).astype(jnp.int32)
            rank = jnp.broadcast_to(before, (1, band_rows))
            for r in range(band_rows - 1):
                rank = rank + jnp.where(lane > r, hit[:, r : r + 1], 0)
            ranks.append(jnp.where(hit > 0, rank, -1))
            asked.append(field(1) * band_blocks + field(2))
            before = before + jnp.sum(hit, axis=1, keepdims=True)
        for slot in range(slots):
            found = sum(
                jnp.where(rank == slot, source, 0) for rank, source in zip(ranks, asked)
            )
            source = jnp.sum(found)
            row = source // band_blocks
            column = pl.multiple_of(source % band_blocks * width, width)
            block = prev_ref.at[0, row, pl.ds(column, width), :]
            copies.append(pltpu.make_async_copy(block, out.at[slot], sems.at[side, slot]))
            copies[-1].start()
    for copy in copies:
        copy.wait()


def gather_blocks(near_list, far_list, prev, *earlier):
    _, band_blocks, _, band_rows = near_list.shape
    _, _, width, hidden = prev.shape
    slots = band_rows * band_blocks // 4
    shape = jax.ShapeDtypeStruct((slots, width // band_blocks, hidden), bf16)
    return pl.pallas_call(
        ordered(gather_kernel, 3, earlier),
        in_specs=[IN_VMEM, IN_VMEM, IN_HBM] + [IN_VMEM] * len(earlier),
        out_specs=[IN_VMEM, IN_VMEM],
        out_shape=[shape, shape],
        scratch_shapes=[pltpu.SemaphoreType.DMA((2, slots))],
        compiler_params=params(4),
        name="gather",
    )(near_list, far_list, in_hbm(prev), *earlier)


def pick_blocks(list_ref, rows, blocks, visit):
    last = rows * blocks // 4 - 1
    sign = 2 * near_below() - 1
    nears, fars = jnp.int32(0), jnp.int32(0)
    for block in range(blocks):
        for row in range(rows):
            field = lambda k: list_ref[0, block, k, row]
            offset = field(0)
            is_near, is_far = offset == -sign, offset == sign
            visit(
                row, block, field, is_near, is_far, jnp.minimum(nears, last),
                jnp.minimum(fars, last),
            )
            nears += is_near.astype(jnp.int32)
            fars += is_far.astype(jnp.int32)


def seam_kernel(list_ref, prev_ref, near_ref, far_ref, low_ref, high_ref, seam_ref):
    width, ch = near_ref.shape[1:]
    rows, total = prev_ref.shape[1:3]
    band_blocks = total // width
    is_left = right_half() == 0
    start = pl.multiple_of((width - SEAM) * (1 - right_half()), SEAM)
    inside = pl.ds(start, SEAM)

    def visit(row, block, field, is_near, is_far, near_slot, far_slot):
        if block in (0, band_blocks - 1):
            source = pl.multiple_of(field(2) * width + start, SEAM)
            local = prev_ref[0, field(1), pl.ds(source, SEAM), :]
            near, far = near_ref[near_slot, inside, :], far_ref[far_slot, inside, :]
            picked = jnp.where(is_near, near, jnp.where(is_far, far, local))
            picked = jnp.where(field(3) > 0, picked, jnp.zeros_like(picked))
            if block > 0:
                picked = jnp.where(is_left, picked, seam_ref[row, :, 0:ch])
            seam_ref[row, :, 0:ch] = picked

    pick_blocks(list_ref, rows, band_blocks, visit)
    edge = pl.multiple_of((band_blocks * width - SEAM) * (1 - right_half()), SEAM)
    half = low_ref.shape[0]
    seam_ref[pl.ds(0, half), :, ch : 2 * ch] = low_ref[:, pl.ds(edge, SEAM), :]
    seam_ref[pl.ds(half, half), :, ch : 2 * ch] = high_ref[:, pl.ds(edge, SEAM), :]


def seam_of(warp_list, prev, near, far, low, high):
    _, rows, _, ch = prev.shape
    return pl.pallas_call(
        seam_kernel,
        in_specs=[IN_SMEM] + [IN_VMEM] * 5,
        out_specs=IN_VMEM,
        out_shape=jax.ShapeDtypeStruct((rows, SEAM, 2 * ch), bf16),
        compiler_params=params(4),
        name="seam",
    )(warp_list, prev, near, far, low, high)


def warp_kernel(list_ref, prev_ref, near_ref, far_ref, out_ref):
    width = near_ref.shape[1]

    def visit(row, block, field, is_near, is_far, near_slot, far_slot):
        column = pl.multiple_of(field(2) * width, width)
        local = prev_ref[0, field(1), pl.ds(column, width), :]
        picked = jnp.where(
            is_near, near_ref[near_slot], jnp.where(is_far, far_ref[far_slot], local)
        )
        picked = jnp.where(field(3) > 0, picked, jnp.zeros_like(picked))
        out_ref[row, pl.ds(block * width, width), :] = picked

    rows, total = prev_ref.shape[1:3]
    pick_blocks(list_ref, rows, total // width, visit)


def warp_of(warp_list, prev, near, far, *earlier):
    return pl.pallas_call(
        ordered(warp_kernel, 4, earlier),
        in_specs=[IN_SMEM] + [IN_VMEM] * (3 + len(earlier)),
        out_specs=IN_VMEM,
        out_shape=jax.ShapeDtypeStruct(prev.shape[1:], bf16),
        compiler_params=params(4),
        name="warp",
    )(warp_list, prev, near, far, *earlier)


def horizontal_kernel(
    rows, hidden_ref, low_ref, high_ref, seam_ref, gates_ref, cand_ref, out_ref, *rest
):
    *sent, joined, reset, partial = rest
    _, width, ch = hidden_ref.shape
    taps = gates_ref.shape[0]
    half = taps // 2
    right = right_half()
    pad = SEAM
    own = pl.multiple_of(pad + pad * right, pad)
    seam = pl.multiple_of(pad + width * (1 - right), pad)
    span = width + SEAM
    flow = state_rows(low_ref, high_ref)
    gates = gates_ref[...].reshape(taps * 2 * ch, 2 * ch)
    count = range(len(rows))
    for r in count:
        piece, at = flow[rows[r]]
        for edge in (0, span + pad):
            joined[r, pl.ds(edge, pad), :] = jnp.zeros((pad, 2 * ch), bf16)
            reset[r, pl.ds(edge, pad), :] = jnp.zeros((pad, ch), bf16)
        joined[r, pl.ds(own, width), 0:ch] = hidden_ref[rows[r]]
        joined[r, pl.ds(own, width), ch : 2 * ch] = piece[at]
        joined[r, pl.ds(seam, SEAM), :] = seam_ref[rows[r]]
    sums = [
        dotf(
            jnp.concatenate(
                [joined[r, pl.ds(pad - half + t, span), :] for t in range(taps)], axis=1
            ),
            gates,
        )
        for r in count
    ]
    update = []
    for r in count:
        update.append(sigmoid(sums[r][:, :ch]))
        current = joined[r, pl.ds(pad, span), 0:ch].astype(f32)
        reset[r, pl.ds(pad, span), :] = (sigmoid(sums[r][:, ch:]) * current).astype(bf16)
    for r in count:
        both = jnp.concatenate([reset[r], joined[r, :, ch : 2 * ch]], axis=1)
        for t in range(0, taps, 2):
            pair = jnp.concatenate([cand_ref[k] for k in range(t, min(t + 2, taps))], axis=1)
            partial[r, :, pl.ds(t * ch, pair.shape[1])] = dotf(both, pair)
    totals = []
    for r in count:
        total = None
        for t in range(taps):
            part = partial[r, pl.ds(pad - half + t, span), pl.ds(t * ch, ch)]
            total = part if total is None else total + part
        totals.append(total)
    for r in count:
        current = joined[r, pl.ds(pad, span), 0:ch].astype(f32)
        cand = jnp.tanh(totals[r])
        blended = (1.0 - update[r]) * current + update[r] * cand
        reset[r, pl.ds(pad, span), :] = blended.astype(bf16)
    for r in count:
        out_ref[r] = reset[r, pl.ds(own, width), :]
    near = half * near_below()
    for sent_ref, first in zip(sent, (near, half - near)):
        sent_ref[...] = out_ref[pl.ds(first, half)]


def horizontal_pass(rows, send, hidden, low, high, seam, gates, cand):
    _, width, ch = hidden.shape
    taps = gates.shape[0]
    length = width + SEAM + 2 * SEAM
    shape = lambda count: jax.ShapeDtypeStruct((count, width, ch), bf16)
    shapes = [shape(len(rows))] + [shape(taps // 2)] * (2 if send else 0)
    return pl.pallas_call(
        functools.partial(horizontal_kernel, rows),
        in_specs=[IN_VMEM] * 6,
        out_specs=[IN_VMEM] * len(shapes),
        out_shape=shapes,
        scratch_shapes=[
            pltpu.VMEM((len(rows), length, 2 * ch), bf16),
            pltpu.VMEM((len(rows), length, ch), bf16),
            pltpu.VMEM((len(rows), length, taps * ch), f32),
        ],
        compiler_params=params(11),
        name="horizontal",
    )(hidden, low, high, seam, gates, cand)


def pairs_kernel(gates_ref, cand_ref, update_out, reset_out, cand_out):
    taps, depth, ch = cand_ref.shape
    none = jnp.zeros((depth, ch), bf16)
    update = lambda j: gates_ref[j, :, pl.ds(0, ch)]
    reset = lambda j: gates_ref[j, :, pl.ds(ch, ch)]
    cand = lambda j: cand_ref[j]
    for out_ref, tap in ((update_out, update), (reset_out, reset), (cand_out, cand)):
        for j in range(taps + 1):
            out_ref[j, :, 0:ch] = tap(j) if j < taps else none
            out_ref[j, :, ch : 2 * ch] = tap(j - 1) if j > 0 else none


def pairs_of(gates, cand):
    taps, depth, ch = cand.shape
    shape = jax.ShapeDtypeStruct((taps + 1, depth, 2 * ch), bf16)
    return pl.pallas_call(
        pairs_kernel,
        in_specs=[IN_VMEM] * 2,
        out_specs=[IN_VMEM] * 3,
        out_shape=[shape, shape, shape],
        compiler_params=params(4),
        name="pairs",
    )(gates, cand)


def banded(outer_ref, inner_ref, half):
    outer = state_rows(outer_ref)
    return outer[:half] + state_rows(inner_ref) + outer[half:]


def stack(sources, rows):
    return jnp.concatenate(
        [piece[at] for y in rows for piece, at in (source[y] for source in sources)], axis=1
    )


def edge_sums(sources, pairs_ref, sums_ref):
    blocks, _, wide = pairs_ref.shape
    ch = wide // 2
    half = (blocks - 1) // 2
    rows = len(sources[0])
    sides = ((range(2 * half), half), (range(rows - 2 * half, rows), 0))
    for i, (own, first) in enumerate(sides):
        weights = pairs_ref[pl.ds(first, 2 * half)].reshape(-1, wide)
        both = dotf(stack(sources, own), weights)
        sums_ref[2 * i], sums_ref[2 * i + 1] = both[:, :ch], both[:, ch:]


def own_sums_kernel(
    outer_ref, inner_ref, low_ref, high_ref, pairs_ref, sums_ref, near_ref, far_ref
):
    half = near_ref.shape[0]
    sources = (banded(outer_ref, inner_ref, half), state_rows(low_ref, high_ref))
    edge_sums(sources, pairs_ref, sums_ref)
    near = half * near_below()
    near_ref[...] = sums_ref[pl.ds(near, half)].astype(bf16)
    far_ref[...] = sums_ref[pl.ds(half - near, half)].astype(bf16)


def own_sums(outer, inner, low, high, pairs):
    count, width, ch = outer.shape
    sent = jax.ShapeDtypeStruct((count // 2, width, ch), bf16)
    return pl.pallas_call(
        own_sums_kernel,
        in_specs=[IN_VMEM] * 5,
        out_specs=[IN_VMEM] * 3,
        out_shape=[jax.ShapeDtypeStruct((count, width, ch), f32), sent, sent],
        compiler_params=params(4),
        name="own_sums",
    )(outer, inner, low, high, pairs)


def gates_kernel(
    outer_ref, inner_ref, low_ref, high_ref, gates_ref, pairs_ref, update_ref, reset_ref, sums_ref
):
    taps, _, wide = gates_ref.shape
    ch = wide // 2
    half = taps // 2
    state = banded(outer_ref, inner_ref, half)
    sources = (state, state_rows(low_ref, high_ref))
    inner = range(half, len(state) - half)
    weights = gates_ref[...].reshape(-1, wide)
    sums = [dotf(stack(sources, range(y - half, y + half + 1)), weights) for y in inner]
    edge_sums(sources, pairs_ref, sums_ref)
    for i, y in enumerate(inner):
        piece, at = state[y]
        update_ref[i] = sigmoid(sums[i][:, :ch])
        reset_ref[i] = (sigmoid(sums[i][:, ch:]) * piece[at].astype(f32)).astype(bf16)


def inner_gates(outer, inner, low, high, gates, pairs, *earlier):
    count, width, ch = inner.shape
    shape = lambda n, kind: jax.ShapeDtypeStruct((n, width, ch), kind)
    return pl.pallas_call(
        ordered(gates_kernel, 6, earlier),
        in_specs=[IN_VMEM] * (6 + len(earlier)),
        out_specs=[IN_VMEM] * 3,
        out_shape=[shape(count, f32), shape(count, bf16), shape(outer.shape[0], f32)],
        compiler_params=params(4),
        name="inner_gates",
    )(outer, inner, low, high, gates, pairs, *earlier)


def outer_kernel(
    outer_ref, update_sums, reset_sums, low_ref, high_ref, hidden_near, hidden_far, motion_near, motion_far,
    gates_ref, pairs_ref, update_ref, reset_ref, rim_ref, motion_rim, hidden_rim,
):
    taps, _, wide = gates_ref.shape
    ch = wide // 2
    half = taps // 2
    fill_rim(motion_rim, motion_near, motion_far)
    fill_rim(hidden_rim, hidden_near, hidden_far)
    above, below = state_rows(hidden_rim)[:half], state_rows(hidden_rim)[half:]
    own, flow = state_rows(outer_ref), state_rows(low_ref, high_ref)
    rim = state_rows(motion_rim)
    top = (above + own[:half], rim[:half] + flow[:half])
    bottom = (own[half:] + below, flow[-half:] + rim[half:])
    weights = lambda first, last: gates_ref[pl.ds(first, last - first)].reshape(-1, wide)
    pairs = lambda first, last: pairs_ref[pl.ds(first, last - first)].reshape(-1, wide)
    sums = []
    for i in range(half):
        sums.append(dotf(stack(top, range(i, half)), weights(0, half - i)))
    for i in range(half):
        rows = range(half, half + i + 1)
        sums.append(dotf(stack(bottom, rows), weights(taps - 1 - i, taps)))
    beyond = [
        dotf(stack(top, range(half, 2 * half)), pairs(2 * half, 3 * half)),
        dotf(stack(bottom, range(half)), pairs(0, half)),
    ]
    for i in range(2 * half):
        update_ref[i] = sigmoid(sums[i][:, :ch] + update_sums[i])
        reset = sigmoid(sums[i][:, ch:] + reset_sums[i])
        reset_ref[i] = (reset * outer_ref[i].astype(f32)).astype(bf16)
    for i in range(2):
        rim_ref[2 * i], rim_ref[2 * i + 1] = beyond[i][:, :ch], beyond[i][:, ch:]


def outer_gates(outer, sums, low, high, hidden_rims, motion_rims, gates, pairs):
    count, width, ch = outer.shape
    half = gates.shape[0] // 2
    shape = lambda kind: jax.ShapeDtypeStruct((count, width, ch), kind)
    return pl.pallas_call(
        outer_kernel,
        in_specs=[IN_VMEM] * 11,
        out_specs=[IN_VMEM] * 4,
        out_shape=[
            shape(f32),
            shape(bf16),
            shape(f32),
            shape(bf16),
        ],
        scratch_shapes=[pltpu.VMEM((2 * half, width, ch), bf16)],
        compiler_params=params(4),
        name="outer_gates",
    )(outer, *sums, low, high, *hidden_rims, *motion_rims, gates, pairs)


def blend(state, update, total):
    return ((1.0 - update) * state.astype(f32) + update * jnp.tanh(total)).astype(bf16)


def cand_kernel(
    reset_outer, reset_inner, low_ref, high_ref, motion_rim, inner_ref, update_ref, pairs_ref,
    out_ref, partial_ref,
):
    blocks, depth, wide = pairs_ref.shape
    ch = wide // 2
    half = (blocks - 1) // 2
    reset = banded(reset_outer, reset_inner, half)
    sources = (reset, state_rows(low_ref, high_ref))
    rows = len(reset)
    weights = lambda first, last: pairs_ref[pl.ds(first, last - first)].reshape(-1, wide)
    sums = {}
    for y in range(half, rows - half, 2):
        rows_read = range(y - half, y + half + 2)
        sums[y] = dotf(stack(sources, rows_read), weights(0, blocks))
    rim = state_rows(motion_rim)
    flow_weights = lambda first, last: pairs_ref[pl.ds(first, last - first), ch:, :].reshape(
        -1, wide
    )
    for i, y in enumerate((0, rows - half)):
        first, last = max(y - half, 0), min(y + half + 2, rows)
        total = dotf(stack(sources, range(first, last)), weights(first - y + half, last - y + half))
        at = (0, half) if i == 0 else (blocks - half, blocks)
        total += dotf(stack((rim,), range(half * i, half * (i + 1))), flow_weights(*at))
        partial_ref[2 * i], partial_ref[2 * i + 1] = total[:, :ch], total[:, ch:]
    for y in range(half, rows - half, 2):
        for k in range(2):
            i = y - half + k
            total = sums[y][:, k * ch : (k + 1) * ch]
            out_ref[i] = blend(inner_ref[i], update_ref[i], total)


def inner_states(resets, low, high, motion_rim, inner, update, pairs):
    count, width, ch = inner.shape
    half = (pairs.shape[0] - 1) // 2
    return pl.pallas_call(
        cand_kernel,
        in_specs=[IN_VMEM] * 8,
        out_specs=[IN_VMEM] * 2,
        out_shape=[
            jax.ShapeDtypeStruct((count, width, ch), bf16),
            jax.ShapeDtypeStruct((2 * half, width, ch), f32),
        ],
        compiler_params=params(4),
        name="inner_states",
    )(*resets, low, high, motion_rim, inner, update, pairs)


def final_kernel(
    near, first_ref, edge_ref, last_ref, outer_ref, update_ref, partial_ref, beyond_ref, cand_pairs,
    out_ref, done, sems,
):
    blocks, _, wide = cand_pairs.shape
    ch = wide // 2
    half = (blocks - 1) // 2
    rows = out_ref.shape[1]
    stores = []
    if near:
        count = first_ref.shape[0]
        target = out_ref.at[0, pl.ds(half, count)]
        stores.append(pltpu.make_async_copy(first_ref, target, sems.at[0]))
        stores[0].start()
    side = near_below() if near else 1 - near_below()
    at = half * side
    reset = []
    for k in range(half):
        total = beyond_ref[at + k] + last_ref[k].astype(f32)
        reset.append((sigmoid(total) * edge_ref[k].astype(f32)).astype(bf16))
    weights = cand_pairs[pl.ds((blocks - half) * side, half), :ch, :].reshape(-1, wide)
    sums = dotf(jnp.concatenate(reset, axis=1), weights)
    for k in range(half):
        total = partial_ref[at + k] + sums[:, k * ch : (k + 1) * ch]
        done[k] = blend(outer_ref[at + k], update_ref[at + k], total)
    target = out_ref.at[0, pl.ds((rows - half) * side, half)]
    stores.append(pltpu.make_async_copy(done, target, sems.at[1]))
    stores[-1].start()
    for store in stores:
        store.wait()


def final_states(inner, edge_rims, last_rims, outer, update, partial, beyond, cand_pairs):
    count, width, ch = outer.shape
    rows = count + inner.shape[0]
    half = edge_rims[0].shape[0]

    def side(near, first, edge, last):
        return pl.pallas_call(
            functools.partial(final_kernel, near),
            in_specs=[IN_VMEM if near else IN_HBM] + [IN_VMEM] * 7,
            out_specs=IN_HBM,
            out_shape=jax.ShapeDtypeStruct((1, rows, width, ch), bf16),
            scratch_shapes=[pltpu.VMEM((half, width, ch), bf16), pltpu.SemaphoreType.DMA((2,))],
            input_output_aliases={} if near else {0: 0},
            compiler_params=params(4),
            name="final_near" if near else "final_far",
        )(first, edge, last, outer, update, partial, beyond, cand_pairs)

    out = side(True, inner, edge_rims[0], last_rims[0])
    return side(False, out, edge_rims[1], last_rims[1])


def shards(
    left_feats, right_feats, prev_hidden, warp_list, enc_weight, hgate_w, hcand_w, vgate_w, vcand_w
):
    rows = prev_hidden.shape[1]
    half = vgate_w.shape[0] // 2
    outer_rows = (*range(half), *range(rows - half, rows))
    inner_rows = tuple(range(half, rows - half))
    swap_cols = lambda value: lax.ppermute(value, "cols", [(0, 1), (1, 0)])
    swap_rows = lambda near, far: (swap_near(near, "rows"), swap_far(far, "rows"))
    pinned = lax.optimization_barrier

    warp_list = jnp.transpose(warp_list, (0, 2, 3, 1))
    lists = swap_rows(warp_list, warp_list)
    edge = swap_cols(right_feats)
    low = motion_of(0, rows // 2, left_feats, right_feats, edge, enc_weight)
    blocks = gather_blocks(*lists, prev_hidden, low)
    near, far = swap_rows(*blocks)
    high = motion_of(rows // 2, rows // 2, left_feats, right_feats, edge, enc_weight, *blocks)
    update_pairs, reset_pairs, cand_pairs = pairs_of(vgate_w, vcand_w)
    edges = edges_of(low, high, half, reset_pairs)
    motion_rims = swap_rows(*edges)
    seam = seam_of(warp_list, prev_hidden, near, far, low, high)
    warped = warp_of(warp_list, prev_hidden, near, far, seam)
    seam = swap_cols(seam)
    outer, *edges = horizontal_pass(outer_rows, True, warped, low, high, seam, hgate_w, hcand_w)
    warped, edges, motion_rims = pinned((warped, edges, motion_rims))
    edge_rims = swap_rows(*edges)
    (inner,) = horizontal_pass(
        inner_rows, False, warped, low, high, seam, hgate_w, hcand_w
    )
    reset_sums, *edges = own_sums(outer, inner, low, high, reset_pairs)
    last_rims = swap_rows(*edges)
    update_inner, reset_inner, update_sums = inner_gates(
        outer, inner, low, high, vgate_w, update_pairs, *edges
    )
    update_outer, reset_outer, beyond, motion_rim = outer_gates(
        outer, (update_sums, reset_sums), low, high, edge_rims, motion_rims, vgate_w, reset_pairs
    )
    resets = (reset_outer, reset_inner)
    inner, partial = inner_states(
        resets, low, high, motion_rim, inner, update_inner, cand_pairs
    )
    return final_states(
        inner, edge_rims, last_rims, outer, update_outer, partial, beyond, cand_pairs
    )


def solution(mesh):
    spread = P(("groups", "cams"), "rows", "cols", None)
    return jax.shard_map(
        shards,
        mesh=mesh,
        in_specs=(spread,) * 4 + (P(),) * 5,
        out_specs=spread,
        check_vma=False,
    )
```

```python
import functools

import jax
import jax.numpy as jnp
from jax import lax
from jax.experimental import pallas as pl
from jax.experimental.pallas import tpu as pltpu
from jax.sharding import PartitionSpec as P

bf16 = jnp.bfloat16
f32 = jnp.float32
SEAM = 16


def dotf(a, b):
    return jnp.dot(a, b, preferred_element_type=f32)


def sigmoid(v):
    return 0.5 * jnp.tanh(0.5 * v) + 0.5


def state_rows(*pieces):
    return [(piece, r) for piece in pieces for r in range(piece.shape[0])]


def fill_rim(rim_ref, near_ref, far_ref):
    count = near_ref.shape[0]
    near = count * near_below()
    rim_ref[pl.ds(near, count)] = near_ref[...]
    rim_ref[pl.ds(count - near, count)] = far_ref[...]


def swap_near(value, axis):
    count = lax.axis_size(axis)
    pairs = [(i, i ^ 1) for i in range(count) if i ^ 1 < count]
    return lax.ppermute(value, axis, pairs)


def swap_far(value, axis):
    count = lax.axis_size(axis)
    pairs = []
    for i in range(1, count - 1, 2):
        pairs += [(i, i + 1), (i + 1, i)]
    return lax.ppermute(value, axis, pairs)


IN_VMEM = pl.BlockSpec(memory_space=pltpu.VMEM)
IN_SMEM = pl.BlockSpec(memory_space=pltpu.SMEM)
IN_HBM = pl.BlockSpec(memory_space=pltpu.HBM)


def ordered(kernel, inputs, earlier):
    return lambda *refs: kernel(*refs[:inputs], *refs[inputs + len(earlier) :])


def right_half():
    return lax.axis_index("cols")


def near_below():
    return 1 - lax.axis_index("rows") % 2


def in_hbm(value):
    return pltpu.with_memory_space_constraint(value, pltpu.HBM)


def params(megabytes):
    return pltpu.CompilerParams(vmem_limit_bytes=megabytes << 20)


def motion_kernel(
    first, left_feats, right_feats, edge_ref, weight, out_ref, left_ref, window,
    weight_ref, sems,
):
    disparities = weight_ref.shape[0]
    rows, width, feats = left_ref.shape
    tile = 128
    own = pl.ds(first, rows)
    loads = [
        pltpu.make_async_copy(left_feats.at[0, own], left_ref, sems.at[0]),
        pltpu.make_async_copy(
            right_feats.at[0, own], window.at[:, pl.ds(disparities, width), :], sems.at[1]
        ),
        pltpu.make_async_copy(weight, weight_ref, sems.at[2]),
    ]
    for load in loads:
        load.start()
    far_edge = edge_ref.shape[2] - disparities
    for r in range(rows):
        other = edge_ref[0, first + r, pl.ds(far_edge, disparities), :]
        window[r, pl.ds(0, disparities), :] = jnp.where(
            right_half() == 1, other, jnp.zeros_like(other)
        )
    scale = feats**-0.5
    lane = lax.broadcasted_iota(jnp.int32, (tile, tile), 1)
    row = lax.broadcasted_iota(jnp.int32, (tile, tile), 0)
    keep = lane < row
    flip = (lane + row == tile - 1).astype(f32).astype(bf16)
    for load in loads:
        load.wait()
    turned = jnp.concatenate(
        [
            dotf(flip, weight_ref[pl.ds(disparities - tile, tile), :]).astype(bf16),
            dotf(flip, weight_ref[pl.ds(0, tile), :]).astype(bf16)[2 * tile - disparities :, :],
        ],
        axis=0,
    )
    span = disparities + tile
    blocks = -(-span // tile)
    tiles = [(r, t * tile) for r in range(rows) for t in range(width // tile)]
    flipped = [dotf(flip, left_ref[r, pl.ds(x, tile), :]).astype(bf16) for r, x in tiles]
    scores = [
        lax.dot_general(
            part,
            window[r, pl.ds(x, blocks * tile), :],
            (((1,), (1,)), ((), ())),
            preferred_element_type=f32,
        )
        * scale
        for part, (r, x) in zip(flipped, tiles)
    ]
    skewed = []
    for score in scores:
        rolled = [
            pltpu.roll(score[:, tile * j : tile * (j + 1)], 0, 1, stride=1, stride_axis=0)
            for j in range(blocks)
        ]
        lanes = [jnp.where(keep, rolled[j], rolled[j + 1]).astype(bf16) for j in range(blocks - 1)]
        skewed.append(jnp.concatenate(lanes, axis=1)[:, :disparities])
    motions = [dotf(part, turned).astype(bf16) for part in skewed]
    for part, (r, x) in zip(motions, tiles):
        out_ref[r, pl.ds(x, tile), :] = dotf(flip, part).astype(bf16)


def motion_of(first, rows, left, right, edge, weight, *earlier):
    width, feats = left.shape[2:]
    return pl.pallas_call(
        ordered(functools.partial(motion_kernel, first), 4, earlier),
        in_specs=[IN_HBM, IN_HBM, IN_VMEM, IN_HBM] + [IN_VMEM] * len(earlier),
        out_specs=IN_VMEM,
        out_shape=jax.ShapeDtypeStruct((rows, width, weight.shape[1]), bf16),
        scratch_shapes=[
            pltpu.VMEM((rows, width, feats), bf16),
            pltpu.VMEM((rows, width + 256, feats), bf16),
            pltpu.VMEM(weight.shape, bf16),
            pltpu.SemaphoreType.DMA((3,)),
        ],
        compiler_params=params(4),
        name="motion",
    )(in_hbm(left), in_hbm(right), edge, in_hbm(weight), *earlier)


def edges_kernel(low_ref, high_ref, near_ref, far_ref):
    count = near_ref.shape[0]
    low, high = low_ref[pl.ds(0, count)], high_ref[pl.ds(high_ref.shape[0] - count, count)]
    below = near_below() == 1
    near_ref[...] = jnp.where(below, high, low)
    far_ref[...] = jnp.where(below, low, high)


def edges_of(low, high, count, *earlier):
    shape = jax.ShapeDtypeStruct((count,) + low.shape[1:], bf16)
    return pl.pallas_call(
        ordered(edges_kernel, 2, earlier),
        in_specs=[IN_VMEM] * (2 + len(earlier)),
        out_specs=[IN_VMEM, IN_VMEM],
        out_shape=[shape, shape],
        compiler_params=params(4),
        name="edges",
    )(low, high, *earlier)


def gather_kernel(near_list, far_list, prev_ref, near_out, far_out):
    _, band_blocks, _, band_rows = near_list.shape
    slots, width, _ = near_out.shape
    sign = 2 * near_below() - 1
    lane = lax.broadcasted_iota(jnp.int32, (1, band_rows), 1)
    sides = ((near_list, near_out, sign), (far_list, far_out, -sign))
    for list_ref, out, wanted in sides:
        before = jnp.zeros((1, 1), jnp.int32)
        ranks, asked = [], []
        for block in range(band_blocks):
            field = lambda k: list_ref[0, block, pl.ds(k, 1), :]
            hit = (field(0) == wanted).astype(jnp.int32)
            rank = jnp.broadcast_to(before, (1, band_rows))
            for r in range(band_rows - 1):
                rank = rank + jnp.where(lane > r, hit[:, r : r + 1], 0)
            ranks.append(jnp.where(hit > 0, rank, -1))
            asked.append(field(1) * band_blocks + field(2))
            before = before + jnp.sum(hit, axis=1, keepdims=True)
        for slot in range(slots):
            found = sum(
                jnp.where(rank == slot, source, 0) for rank, source in zip(ranks, asked)
            )
            source = jnp.sum(found)
            row = source // band_blocks
            column = pl.multiple_of(source % band_blocks * width, width)
            out[slot] = prev_ref[0, row, pl.ds(column, width), :]


def gather_blocks(near_list, far_list, prev, *earlier):
    _, band_blocks, _, band_rows = near_list.shape
    _, _, width, hidden = prev.shape
    slots = band_rows * band_blocks // 4
    shape = jax.ShapeDtypeStruct((slots, width // band_blocks, hidden), bf16)
    return pl.pallas_call(
        ordered(gather_kernel, 3, earlier),
        in_specs=[IN_VMEM] * (3 + len(earlier)),
        out_specs=[IN_VMEM, IN_VMEM],
        out_shape=[shape, shape],
        compiler_params=params(4),
        name="gather",
    )(near_list, far_list, prev, *earlier)


def pick_blocks(list_ref, rows, blocks, visit):
    last = rows * blocks // 4 - 1
    sign = 2 * near_below() - 1
    nears, fars = jnp.int32(0), jnp.int32(0)
    for block in range(blocks):
        for row in range(rows):
            field = lambda k: list_ref[0, block, k, row]
            offset = field(0)
            is_near, is_far = offset == -sign, offset == sign
            visit(
                row, block, field, is_near, is_far, jnp.minimum(nears, last),
                jnp.minimum(fars, last),
            )
            nears += is_near.astype(jnp.int32)
            fars += is_far.astype(jnp.int32)


def seam_kernel(list_ref, prev_ref, near_ref, far_ref, low_ref, high_ref, seam_ref):
    width, ch = near_ref.shape[1:]
    rows, total = prev_ref.shape[1:3]
    band_blocks = total // width
    is_left = right_half() == 0
    start = pl.multiple_of((width - SEAM) * (1 - right_half()), SEAM)
    inside = pl.ds(start, SEAM)

    def visit(row, block, field, is_near, is_far, near_slot, far_slot):
        if block in (0, band_blocks - 1):
            source = pl.multiple_of(field(2) * width + start, SEAM)
            local = prev_ref[0, field(1), pl.ds(source, SEAM), :]
            near, far = near_ref[near_slot, inside, :], far_ref[far_slot, inside, :]
            picked = jnp.where(is_near, near, jnp.where(is_far, far, local))
            picked = jnp.where(field(3) > 0, picked, jnp.zeros_like(picked))
            if block > 0:
                picked = jnp.where(is_left, picked, seam_ref[row, :, 0:ch])
            seam_ref[row, :, 0:ch] = picked

    pick_blocks(list_ref, rows, band_blocks, visit)
    edge = pl.multiple_of((band_blocks * width - SEAM) * (1 - right_half()), SEAM)
    half = low_ref.shape[0]
    seam_ref[pl.ds(0, half), :, ch : 2 * ch] = low_ref[:, pl.ds(edge, SEAM), :]
    seam_ref[pl.ds(half, half), :, ch : 2 * ch] = high_ref[:, pl.ds(edge, SEAM), :]


def seam_of(warp_list, prev, near, far, low, high):
    _, rows, _, ch = prev.shape
    return pl.pallas_call(
        seam_kernel,
        in_specs=[IN_SMEM] + [IN_VMEM] * 5,
        out_specs=IN_VMEM,
        out_shape=jax.ShapeDtypeStruct((rows, SEAM, 2 * ch), bf16),
        compiler_params=params(4),
        name="seam",
    )(warp_list, prev, near, far, low, high)


def warp_kernel(list_ref, prev_ref, near_ref, far_ref, out_ref):
    width = near_ref.shape[1]

    def visit(row, block, field, is_near, is_far, near_slot, far_slot):
        column = pl.multiple_of(field(2) * width, width)
        local = prev_ref[0, field(1), pl.ds(column, width), :]
        picked = jnp.where(
            is_near, near_ref[near_slot], jnp.where(is_far, far_ref[far_slot], local)
        )
        picked = jnp.where(field(3) > 0, picked, jnp.zeros_like(picked))
        out_ref[row, pl.ds(block * width, width), :] = picked

    rows, total = prev_ref.shape[1:3]
    pick_blocks(list_ref, rows, total // width, visit)


def warp_of(warp_list, prev, near, far, *earlier):
    return pl.pallas_call(
        ordered(warp_kernel, 4, earlier),
        in_specs=[IN_SMEM] + [IN_VMEM] * (3 + len(earlier)),
        out_specs=IN_VMEM,
        out_shape=jax.ShapeDtypeStruct(prev.shape[1:], bf16),
        compiler_params=params(4),
        name="warp",
    )(warp_list, prev, near, far, *earlier)


def horizontal_kernel(
    rows, hidden_ref, low_ref, high_ref, seam_ref, gates_ref, cand_ref, out_ref, *rest
):
    *sent, joined, reset, partial = rest
    _, width, ch = hidden_ref.shape
    taps = gates_ref.shape[0]
    half = taps // 2
    right = right_half()
    pad = SEAM
    own = pl.multiple_of(pad + pad * right, pad)
    seam = pl.multiple_of(pad + width * (1 - right), pad)
    span = width + SEAM
    flow = state_rows(low_ref, high_ref)
    gates = gates_ref[...].reshape(taps * 2 * ch, 2 * ch)
    count = range(len(rows))
    for r in count:
        piece, at = flow[rows[r]]
        for edge in (0, span + pad):
            joined[r, pl.ds(edge, pad), :] = jnp.zeros((pad, 2 * ch), bf16)
            reset[r, pl.ds(edge, pad), :] = jnp.zeros((pad, ch), bf16)
        joined[r, pl.ds(own, width), 0:ch] = hidden_ref[rows[r]]
        joined[r, pl.ds(own, width), ch : 2 * ch] = piece[at]
        joined[r, pl.ds(seam, SEAM), :] = seam_ref[rows[r]]
    sums = [
        dotf(
            jnp.concatenate(
                [joined[r, pl.ds(pad - half + t, span), :] for t in range(taps)], axis=1
            ),
            gates,
        )
        for r in count
    ]
    update = []
    for r in count:
        update.append(sigmoid(sums[r][:, :ch]))
        current = joined[r, pl.ds(pad, span), 0:ch].astype(f32)
        reset[r, pl.ds(pad, span), :] = (sigmoid(sums[r][:, ch:]) * current).astype(bf16)
    for r in count:
        both = jnp.concatenate([reset[r], joined[r, :, ch : 2 * ch]], axis=1)
        for t in range(0, taps, 2):
            pair = jnp.concatenate([cand_ref[k] for k in range(t, min(t + 2, taps))], axis=1)
            partial[r, :, pl.ds(t * ch, pair.shape[1])] = dotf(both, pair)
    totals = []
    for r in count:
        total = None
        for t in range(taps):
            part = partial[r, pl.ds(pad - half + t, span), pl.ds(t * ch, ch)]
            total = part if total is None else total + part
        totals.append(total)
    for r in count:
        current = joined[r, pl.ds(pad, span), 0:ch].astype(f32)
        cand = jnp.tanh(totals[r])
        blended = (1.0 - update[r]) * current + update[r] * cand
        reset[r, pl.ds(pad, span), :] = blended.astype(bf16)
    for r in count:
        out_ref[r] = reset[r, pl.ds(own, width), :]
    near = half * near_below()
    for sent_ref, first in zip(sent, (near, half - near)):
        sent_ref[...] = out_ref[pl.ds(first, half)]


def horizontal_pass(rows, send, hidden, low, high, seam, gates, cand):
    _, width, ch = hidden.shape
    taps = gates.shape[0]
    length = width + SEAM + 2 * SEAM
    shape = lambda count: jax.ShapeDtypeStruct((count, width, ch), bf16)
    shapes = [shape(len(rows))] + [shape(taps // 2)] * (2 if send else 0)
    return pl.pallas_call(
        functools.partial(horizontal_kernel, rows),
        in_specs=[IN_VMEM] * 6,
        out_specs=[IN_VMEM] * len(shapes),
        out_shape=shapes,
        scratch_shapes=[
            pltpu.VMEM((len(rows), length, 2 * ch), bf16),
            pltpu.VMEM((len(rows), length, ch), bf16),
            pltpu.VMEM((len(rows), length, taps * ch), f32),
        ],
        compiler_params=params(11),
        name="horizontal",
    )(hidden, low, high, seam, gates, cand)


def pairs_kernel(gates_ref, cand_ref, update_out, reset_out, cand_out):
    taps, depth, ch = cand_ref.shape
    none = jnp.zeros((depth, ch), bf16)
    update = lambda j: gates_ref[j, :, pl.ds(0, ch)]
    reset = lambda j: gates_ref[j, :, pl.ds(ch, ch)]
    cand = lambda j: cand_ref[j]
    for out_ref, tap in ((update_out, update), (reset_out, reset), (cand_out, cand)):
        for j in range(taps + 1):
            out_ref[j, :, 0:ch] = tap(j) if j < taps else none
            out_ref[j, :, ch : 2 * ch] = tap(j - 1) if j > 0 else none


def pairs_of(gates, cand):
    taps, depth, ch = cand.shape
    shape = jax.ShapeDtypeStruct((taps + 1, depth, 2 * ch), bf16)
    return pl.pallas_call(
        pairs_kernel,
        in_specs=[IN_VMEM] * 2,
        out_specs=[IN_VMEM] * 3,
        out_shape=[shape, shape, shape],
        compiler_params=params(4),
        name="pairs",
    )(gates, cand)


def banded(outer_ref, inner_ref, half):
    outer = state_rows(outer_ref)
    return outer[:half] + state_rows(inner_ref) + outer[half:]


def stack(sources, rows):
    return jnp.concatenate(
        [piece[at] for y in rows for piece, at in (source[y] for source in sources)], axis=1
    )


def edge_sums(sources, pairs_ref, sums_ref):
    blocks, _, wide = pairs_ref.shape
    ch = wide // 2
    half = (blocks - 1) // 2
    rows = len(sources[0])
    sides = ((range(2 * half), half), (range(rows - 2 * half, rows), 0))
    for i, (own, first) in enumerate(sides):
        weights = pairs_ref[pl.ds(first, 2 * half)].reshape(-1, wide)
        both = dotf(stack(sources, own), weights)
        sums_ref[2 * i], sums_ref[2 * i + 1] = both[:, :ch], both[:, ch:]


def own_sums_kernel(
    outer_ref, inner_ref, low_ref, high_ref, pairs_ref, sums_ref, near_ref, far_ref
):
    half = near_ref.shape[0]
    sources = (banded(outer_ref, inner_ref, half), state_rows(low_ref, high_ref))
    edge_sums(sources, pairs_ref, sums_ref)
    near = half * near_below()
    near_ref[...] = sums_ref[pl.ds(near, half)].astype(bf16)
    far_ref[...] = sums_ref[pl.ds(half - near, half)].astype(bf16)


def own_sums(outer, inner, low, high, pairs):
    count, width, ch = outer.shape
    sent = jax.ShapeDtypeStruct((count // 2, width, ch), bf16)
    return pl.pallas_call(
        own_sums_kernel,
        in_specs=[IN_VMEM] * 5,
        out_specs=[IN_VMEM] * 3,
        out_shape=[jax.ShapeDtypeStruct((count, width, ch), f32), sent, sent],
        compiler_params=params(4),
        name="own_sums",
    )(outer, inner, low, high, pairs)


def gates_kernel(
    outer_ref, inner_ref, low_ref, high_ref, gates_ref, pairs_ref, update_ref, reset_ref, sums_ref
):
    taps, _, wide = gates_ref.shape
    ch = wide // 2
    half = taps // 2
    state = banded(outer_ref, inner_ref, half)
    sources = (state, state_rows(low_ref, high_ref))
    inner = range(half, len(state) - half)
    weights = gates_ref[...].reshape(-1, wide)
    sums = [dotf(stack(sources, range(y - half, y + half + 1)), weights) for y in inner]
    edge_sums(sources, pairs_ref, sums_ref)
    for i, y in enumerate(inner):
        piece, at = state[y]
        update_ref[i] = sigmoid(sums[i][:, :ch])
        reset_ref[i] = (sigmoid(sums[i][:, ch:]) * piece[at].astype(f32)).astype(bf16)


def inner_gates(outer, inner, low, high, gates, pairs, *earlier):
    count, width, ch = inner.shape
    shape = lambda n, kind: jax.ShapeDtypeStruct((n, width, ch), kind)
    return pl.pallas_call(
        ordered(gates_kernel, 6, earlier),
        in_specs=[IN_VMEM] * (6 + len(earlier)),
        out_specs=[IN_VMEM] * 3,
        out_shape=[shape(count, f32), shape(count, bf16), shape(outer.shape[0], f32)],
        compiler_params=params(4),
        name="inner_gates",
    )(outer, inner, low, high, gates, pairs, *earlier)


def outer_kernel(
    outer_ref, update_sums, reset_sums, low_ref, high_ref, hidden_near, hidden_far, motion_near, motion_far,
    gates_ref, pairs_ref, update_ref, reset_ref, rim_ref, motion_rim, hidden_rim,
):
    taps, _, wide = gates_ref.shape
    ch = wide // 2
    half = taps // 2
    fill_rim(motion_rim, motion_near, motion_far)
    fill_rim(hidden_rim, hidden_near, hidden_far)
    above, below = state_rows(hidden_rim)[:half], state_rows(hidden_rim)[half:]
    own, flow = state_rows(outer_ref), state_rows(low_ref, high_ref)
    rim = state_rows(motion_rim)
    top = (above + own[:half], rim[:half] + flow[:half])
    bottom = (own[half:] + below, flow[-half:] + rim[half:])
    weights = lambda first, last: gates_ref[pl.ds(first, last - first)].reshape(-1, wide)
    pairs = lambda first, last: pairs_ref[pl.ds(first, last - first)].reshape(-1, wide)
    sums = []
    for i in range(half):
        sums.append(dotf(stack(top, range(i, half)), weights(0, half - i)))
    for i in range(half):
        rows = range(half, half + i + 1)
        sums.append(dotf(stack(bottom, rows), weights(taps - 1 - i, taps)))
    beyond = [
        dotf(stack(top, range(half, 2 * half)), pairs(2 * half, 3 * half)),
        dotf(stack(bottom, range(half)), pairs(0, half)),
    ]
    for i in range(2 * half):
        update_ref[i] = sigmoid(sums[i][:, :ch] + update_sums[i])
        reset = sigmoid(sums[i][:, ch:] + reset_sums[i])
        reset_ref[i] = (reset * outer_ref[i].astype(f32)).astype(bf16)
    for i in range(2):
        rim_ref[2 * i], rim_ref[2 * i + 1] = beyond[i][:, :ch], beyond[i][:, ch:]


def outer_gates(outer, sums, low, high, hidden_rims, motion_rims, gates, pairs):
    count, width, ch = outer.shape
    half = gates.shape[0] // 2
    shape = lambda kind: jax.ShapeDtypeStruct((count, width, ch), kind)
    return pl.pallas_call(
        outer_kernel,
        in_specs=[IN_VMEM] * 11,
        out_specs=[IN_VMEM] * 4,
        out_shape=[
            shape(f32),
            shape(bf16),
            shape(f32),
            shape(bf16),
        ],
        scratch_shapes=[pltpu.VMEM((2 * half, width, ch), bf16)],
        compiler_params=params(4),
        name="outer_gates",
    )(outer, *sums, low, high, *hidden_rims, *motion_rims, gates, pairs)


def blend(state, update, total):
    return ((1.0 - update) * state.astype(f32) + update * jnp.tanh(total)).astype(bf16)


def cand_kernel(
    reset_outer, reset_inner, low_ref, high_ref, motion_rim, inner_ref, update_ref, pairs_ref,
    out_ref, partial_ref,
):
    blocks, depth, wide = pairs_ref.shape
    ch = wide // 2
    half = (blocks - 1) // 2
    reset = banded(reset_outer, reset_inner, half)
    sources = (reset, state_rows(low_ref, high_ref))
    rows = len(reset)
    weights = lambda first, last: pairs_ref[pl.ds(first, last - first)].reshape(-1, wide)
    sums = {}
    for y in range(half, rows - half, 2):
        rows_read = range(y - half, y + half + 2)
        sums[y] = dotf(stack(sources, rows_read), weights(0, blocks))
    rim = state_rows(motion_rim)
    flow_weights = lambda first, last: pairs_ref[pl.ds(first, last - first), ch:, :].reshape(
        -1, wide
    )
    for i, y in enumerate((0, rows - half)):
        first, last = max(y - half, 0), min(y + half + 2, rows)
        total = dotf(stack(sources, range(first, last)), weights(first - y + half, last - y + half))
        at = (0, half) if i == 0 else (blocks - half, blocks)
        total += dotf(stack((rim,), range(half * i, half * (i + 1))), flow_weights(*at))
        partial_ref[2 * i], partial_ref[2 * i + 1] = total[:, :ch], total[:, ch:]
    for y in range(half, rows - half, 2):
        for k in range(2):
            i = y - half + k
            total = sums[y][:, k * ch : (k + 1) * ch]
            out_ref[i] = blend(inner_ref[i], update_ref[i], total)


def inner_states(resets, low, high, motion_rim, inner, update, pairs):
    count, width, ch = inner.shape
    half = (pairs.shape[0] - 1) // 2
    return pl.pallas_call(
        cand_kernel,
        in_specs=[IN_VMEM] * 8,
        out_specs=[IN_VMEM] * 2,
        out_shape=[
            jax.ShapeDtypeStruct((count, width, ch), bf16),
            jax.ShapeDtypeStruct((2 * half, width, ch), f32),
        ],
        compiler_params=params(4),
        name="inner_states",
    )(*resets, low, high, motion_rim, inner, update, pairs)


def final_kernel(
    near, first_ref, edge_ref, last_ref, outer_ref, update_ref, partial_ref, beyond_ref, cand_pairs,
    out_ref, done, sems,
):
    blocks, _, wide = cand_pairs.shape
    ch = wide // 2
    half = (blocks - 1) // 2
    rows = out_ref.shape[1]
    stores = []
    if near:
        count = first_ref.shape[0]
        target = out_ref.at[0, pl.ds(half, count)]
        stores.append(pltpu.make_async_copy(first_ref, target, sems.at[0]))
        stores[0].start()
    side = near_below() if near else 1 - near_below()
    at = half * side
    reset = []
    for k in range(half):
        total = beyond_ref[at + k] + last_ref[k].astype(f32)
        reset.append((sigmoid(total) * edge_ref[k].astype(f32)).astype(bf16))
    weights = cand_pairs[pl.ds((blocks - half) * side, half), :ch, :].reshape(-1, wide)
    sums = dotf(jnp.concatenate(reset, axis=1), weights)
    for k in range(half):
        total = partial_ref[at + k] + sums[:, k * ch : (k + 1) * ch]
        done[k] = blend(outer_ref[at + k], update_ref[at + k], total)
    target = out_ref.at[0, pl.ds((rows - half) * side, half)]
    stores.append(pltpu.make_async_copy(done, target, sems.at[1]))
    stores[-1].start()
    for store in stores:
        store.wait()


def final_states(inner, edge_rims, last_rims, outer, update, partial, beyond, cand_pairs):
    count, width, ch = outer.shape
    rows = count + inner.shape[0]
    half = edge_rims[0].shape[0]

    def side(near, first, edge, last):
        return pl.pallas_call(
            functools.partial(final_kernel, near),
            in_specs=[IN_VMEM if near else IN_HBM] + [IN_VMEM] * 7,
            out_specs=IN_HBM,
            out_shape=jax.ShapeDtypeStruct((1, rows, width, ch), bf16),
            scratch_shapes=[pltpu.VMEM((half, width, ch), bf16), pltpu.SemaphoreType.DMA((2,))],
            input_output_aliases={} if near else {0: 0},
            compiler_params=params(4),
            name="final_near" if near else "final_far",
        )(first, edge, last, outer, update, partial, beyond, cand_pairs)

    out = side(True, inner, edge_rims[0], last_rims[0])
    return side(False, out, edge_rims[1], last_rims[1])


def shards(
    left_feats, right_feats, prev_hidden, warp_list, enc_weight, hgate_w, hcand_w, vgate_w, vcand_w
):
    rows = prev_hidden.shape[1]
    half = vgate_w.shape[0] // 2
    outer_rows = (*range(half), *range(rows - half, rows))
    inner_rows = tuple(range(half, rows - half))
    swap_cols = lambda value: lax.ppermute(value, "cols", [(0, 1), (1, 0)])
    swap_rows = lambda near, far: (swap_near(near, "rows"), swap_far(far, "rows"))
    pinned = lax.optimization_barrier

    warp_list = jnp.transpose(warp_list, (0, 2, 3, 1))
    lists = swap_rows(warp_list, warp_list)
    edge = swap_cols(right_feats)
    low = motion_of(0, rows // 2, left_feats, right_feats, edge, enc_weight)
    blocks = gather_blocks(*lists, prev_hidden, low)
    near, far = swap_rows(*blocks)
    high = motion_of(rows // 2, rows // 2, left_feats, right_feats, edge, enc_weight, *blocks)
    update_pairs, reset_pairs, cand_pairs = pairs_of(vgate_w, vcand_w)
    edges = edges_of(low, high, half, reset_pairs)
    motion_rims = swap_rows(*edges)
    seam = seam_of(warp_list, prev_hidden, near, far, low, high)
    warped = warp_of(warp_list, prev_hidden, near, far, seam)
    seam = swap_cols(seam)
    outer, *edges = horizontal_pass(outer_rows, True, warped, low, high, seam, hgate_w, hcand_w)
    warped, edges, motion_rims = pinned((warped, edges, motion_rims))
    edge_rims = swap_rows(*edges)
    (inner,) = horizontal_pass(
        inner_rows, False, warped, low, high, seam, hgate_w, hcand_w
    )
    reset_sums, *edges = own_sums(outer, inner, low, high, reset_pairs)
    last_rims = swap_rows(*edges)
    update_inner, reset_inner, update_sums = inner_gates(
        outer, inner, low, high, vgate_w, update_pairs, *edges
    )
    update_outer, reset_outer, beyond, motion_rim = outer_gates(
        outer, (update_sums, reset_sums), low, high, edge_rims, motion_rims, vgate_w, reset_pairs
    )
    resets = (reset_outer, reset_inner)
    inner, partial = inner_states(
        resets, low, high, motion_rim, inner, update_inner, cand_pairs
    )
    return final_states(
        inner, edge_rims, last_rims, outer, update_outer, partial, beyond, cand_pairs
    )


def solution(mesh):
    spread = P(("groups", "cams"), "rows", "cols", None)
    return jax.shard_map(
        shards,
        mesh=mesh,
        in_specs=(spread,) * 4 + (P(),) * 5,
        out_specs=spread,
        check_vma=False,
    )
```
